32 devices in a mesh: ens: 2 (over y), row: 4 (over z), col: 2 (over x), chan: 2 (over core).
Axes of the slice: x: 2, y: 2, z: 4, core: 2. Of those that a mesh axis runs over, the one named last changes fastest.
Arguments:
- latent: float32 [4, 12, 32, 256], P('ens', None, 'row', 'col'), parts along dimension 0, may hold values from -6 to 6
- fresh_noise: float32 [4, 12, 32, 256], P('ens', None, 'row', 'col'), parts along dimension 0, may hold values from -6 to 6
- step_index: int32 [4], P('ens'), parts along dimension 0, may hold values from 0 to 11
- coarse: float32 [24, 4, 32], P('ens', None, 'col'), parts along dimension 0, may hold values from -6 to 6
- weight_in: bfloat16 [9, 256, 24], replicated, may hold values from -0.4375 to 0.4375
- bias_in: float32 [256], replicated, may hold values from -4 to 4
- weight_noise: float32 [256], replicated, may hold values from -4 to 4
- weight_mid: bfloat16 [9, 256, 256], P(None, 'chan'), may hold values from -0.125 to 0.125
- bias_mid: float32 [256], P('chan'), may hold values from -4 to 4
- weight_out: bfloat16 [12, 256], P(None, 'chan'), may hold values from -0.375 to 0.375
Outputs:
- fine_field: float32 [4, 12, 32, 256], P('ens', None, 'row', 'col'), parts along dimension 0
- next_latent: float32 [4, 12, 32, 256], P('ens', None, 'row', 'col'), parts along dimension 0
The draws below stay inside these ranges and needn't reach their ends.
There are 2 independent parts, one for each index of `ens`. The reference program is written for one: setup_inputs(seed, part) draws one part's arguments, and reference() takes and returns one part's arrays. A program takes and returns all parts, laid end to end along the dimension named above; an argument that names none is the same for every part. Nothing has to cross between parts.
Inputs may be any that keep to these rules, and one draw needn't show every extreme that they name: `step_index`: each sample's position in the noise plan of 18 steps.
All inputs are finite; a program needn't handle non-finite values.
Results may differ from the reference program's by a relative error of at most 0.0024.
Values may be sent and summed in bfloat16 or wider, within the bound.
No kernel may reach another device: no remote copies, remote signals or barrier semaphores. Data moves between devices by JAX's collectives and lax.ppermute only.
A program may use at most 64 MiB of HBM per device.

```python
import jax
import jax.numpy as jnp
from jax import lax

CC = 12
HID = 256
S = 2
STEPS = 18
FACTOR = 8
TH = 8
H = 32
W = 256
HC = 4
WC = 32


def level_of(key, shape, pieces, least, high):
    loudness = 1.0
    for dim, parts in pieces:
        draws = jax.random.uniform(jax.random.fold_in(jax.random.fold_in(key, 6), dim), (parts,), jnp.float32, least / len(pieces), high / len(pieces))
        loudness = loudness * jnp.repeat(jnp.exp(draws), shape[dim] // parts).reshape((-1,) + (1,) * (len(shape) - 1 - dim))
    return loudness


def normal_values(stream_key, shape, scale, reach, pieces=(), held_as=jnp.bfloat16):
    entries = jax.random.normal(stream_key, shape, jnp.float32) * scale
    if len(pieces) > 0:
        entries = level_of(stream_key, shape, pieces, -0.22, 0.18) * entries
    return jnp.clip(entries, min=-reach, max=reach).astype(held_as)


def setup_inputs(seed: int = 0, part: int = 0) -> dict:
    keys = jax.random.split(jax.random.key(seed), 11)
    part_splits = jax.random.split(jax.random.fold_in(keys[10], part), 11)
    latent = normal_values(part_splits[0], (S, CC, H, W), 1.0, 6.0, ((2, 4), (3, 2)), jnp.float32)
    fresh_noise = normal_values(part_splits[1], (S, CC, H, W), 1.0, 6.0, ((2, 4), (3, 2)), jnp.float32)
    step_index = jax.random.randint(part_splits[2], (S,), 0, 12).astype(jnp.int32)
    coarse = normal_values(part_splits[3], (CC, HC, WC), 1.0, 6.0, ((2, 2),), jnp.float32)
    weight_in = normal_values(keys[4], (9, HID, 2 * CC), (18 * CC) ** -0.5, 0.4375)
    bias_in = normal_values(keys[5], (HID,), 1.0, 4.0, (), jnp.float32)
    weight_noise = normal_values(keys[6], (HID,), 1.0, 4.0, (), jnp.float32)
    weight_mid = normal_values(keys[7], (9, HID, HID), (9 * HID) ** -0.5, 0.125, ((1, 2),))
    bias_mid = normal_values(keys[8], (HID,), 1.0, 4.0, ((0, 2),), jnp.float32)
    weight_out = normal_values(keys[9], (CC, HID), HID ** -0.5, 0.375, ((1, 2),))
    return dict(latent=latent, fresh_noise=fresh_noise, step_index=step_index, coarse=coarse, weight_in=weight_in, bias_in=bias_in, weight_noise=weight_noise, weight_mid=weight_mid, bias_mid=bias_mid, weight_out=weight_out)


sigma_data = 0.5
sigma_high = 80.0
sigma_low = 0.002
rho_power = 7.0

def blend_matrix(fine_index, coarse_index, coarse_count, factor):
    twice_pos = 2 * fine_index + 1 - factor
    lower_cell = twice_pos // (2 * factor)
    fraction = (twice_pos - lower_cell * 2 * factor).astype(jnp.float32) / (2.0 * factor)
    before = lower_cell < 0
    fraction = jnp.where(before, 0.0, fraction)
    lower_clip = jnp.clip(lower_cell, 0, coarse_count - 1)
    upper_clip = jnp.clip(lower_cell + 1, 0, coarse_count - 1)
    lower_hit = (lower_clip[:, None] == coarse_index[None, :]).astype(jnp.float32)
    upper_hit = (upper_clip[:, None] == coarse_index[None, :]).astype(jnp.float32)
    return (1.0 - fraction)[:, None] * lower_hit + fraction[:, None] * upper_hit

def noise_level(position):
    top_root = sigma_high ** (1.0 / rho_power)
    bottom_root = sigma_low ** (1.0 / rho_power)
    along = position.astype(jnp.float32) / (STEPS - 1)
    return (top_root + along * (bottom_root - top_root)) ** rho_power

def conv_valid(source, weight, out_rows, out_cols):
    total = None
    for offset_row in range(3):
        for offset_col in range(3):
            window = source[:, :, offset_row:offset_row + out_rows, offset_col:offset_col + out_cols]
            term = jnp.einsum('oi,siyx->soyx', weight[3 * offset_row + offset_col].astype(jnp.float32), window.astype(jnp.float32), precision=lax.Precision.HIGHEST)
            total = term if total is None else total + term
    return total

def reference(latent, fresh_noise, step_index, coarse, weight_in, bias_in, weight_noise, weight_mid, bias_mid, weight_out):
    samples, channels, height, width = latent.shape
    coarse_rows = coarse.shape[1]
    coarse_cols = coarse.shape[2]
    rows_matrix = blend_matrix(jnp.arange(height, dtype=jnp.int32), jnp.arange(coarse_rows, dtype=jnp.int32), coarse_rows, FACTOR)
    cols_matrix = blend_matrix(jnp.arange(width, dtype=jnp.int32), jnp.arange(coarse_cols, dtype=jnp.int32), coarse_cols, FACTOR)
    mean_up = jnp.einsum('yh,khw,xw->kyx', rows_matrix, coarse, cols_matrix, precision=lax.Precision.HIGHEST)
    noise_now = noise_level(step_index)
    noise_next = noise_level(step_index + 1)
    inputs = jnp.concatenate([latent, jnp.broadcast_to(mean_up[None], (samples,) + mean_up.shape)], axis=1).astype(jnp.bfloat16)
    padded = jnp.pad(inputs, ((0, 0), (0, 0), (2, 2), (2, 2)))
    conditioning = bias_in[None, :, None, None] + (jnp.log(noise_now) / 4.0)[:, None, None, None] * weight_noise[None, :, None, None]
    band_rows = TH
    band_count = height // band_rows

    def one_band(band_index):
        start_row = band_index * band_rows
        source = lax.dynamic_slice_in_dim(padded, start_row, band_rows + 4, 2)
        hidden = jax.nn.silu(conv_valid(source, weight_in, band_rows + 2, width + 2) + conditioning)
        global_rows = start_row - 1 + jnp.arange(band_rows + 2, dtype=jnp.int32)
        global_cols = -1 + jnp.arange(width + 2, dtype=jnp.int32)
        inside = ((global_rows >= 0) & (global_rows < height))[:, None] & ((global_cols >= 0) & (global_cols < width))[None, :]
        hidden = jnp.where(inside, hidden, 0.0).astype(jnp.bfloat16)
        middle = jax.nn.silu(conv_valid(hidden, weight_mid, band_rows, width) + bias_mid[None, :, None, None]).astype(jnp.bfloat16)
        return jnp.einsum('ko,soyx->skyx', weight_out.astype(jnp.float32), middle.astype(jnp.float32), precision=lax.Precision.HIGHEST)
    bands = lax.map(one_band, jnp.arange(band_count, dtype=jnp.int32))
    network = jnp.transpose(bands, (1, 2, 0, 3, 4)).reshape(samples, channels, height, width)
    scale_now = jnp.sqrt(noise_now * noise_now + sigma_data * sigma_data)
    skip_coef = sigma_data * sigma_data / (noise_now * noise_now + sigma_data * sigma_data)
    out_coef = sigma_data * noise_now / scale_now
    denoised = (skip_coef * scale_now)[:, None, None, None] * latent + out_coef[:, None, None, None] * network
    fine_field = mean_up[None] + denoised
    scale_next = jnp.sqrt(noise_next * noise_next + sigma_data * sigma_data)
    next_latent = (denoised + noise_next[:, None, None, None] * fresh_noise) / scale_next[:, None, None, None]
    return (fine_field, next_latent)
```

```python
import functools

import jax
import jax.numpy as jnp
from jax import lax
from jax.experimental import pallas as pl
from jax.experimental.pallas import tpu as pltpu
from jax.sharding import PartitionSpec as P

STEPS = 18
FACTOR = 8

sigma_data = 0.5
sigma_high = 80.0
sigma_low = 0.002
rho_power = 7.0

F32 = jnp.float32
BF16 = jnp.bfloat16
LANES = 128
CPAD = 16


def lane_index(rows):
    return lax.broadcasted_iota(jnp.int32, (rows, LANES), 1)


def noise_level(position):
    top_root = sigma_high ** (1.0 / rho_power)
    bottom_root = sigma_low ** (1.0 / rho_power)
    root = top_root + position * (1.0 / (STEPS - 1)) * (bottom_root - top_root)
    square = root * root
    return square * square * square * root


def silu(value):
    half = 0.5 * value
    return half + half * jnp.tanh(half)


def three_terms(value):
    high = value.astype(BF16).astype(F32)
    rest = value - high
    mid = rest.astype(BF16).astype(F32)
    return high, mid, (rest - mid).astype(BF16).astype(F32)


def pack_kernel(dims, latent, coarse, weight_out, bias_mid, rows_out, shared_out, *side_outs):
    samples, channels, rows, cols = latent.shape
    coarse_rows, local_cols = coarse.shape[1:]
    count = dims["col"]
    col_place = lax.axis_index("col")
    lower = lax.axis_index("chan") == 1
    for near in range(2):
        for s in range(samples):
            first = latent[s, :, near, :]
            last = latent[s, :, rows - 2 + near, :]
            rows_out[near * samples + s, 0:channels, :] = jnp.where(lower, first, last).astype(BF16)
            rows_out[near * samples + s, channels:CPAD, :] = jnp.zeros(
                (CPAD - channels, LANES), BF16
            )
    shared_out[0:channels, :] = weight_out[...].astype(F32)
    shared_out[channels : channels + 1, :] = bias_mid[...]
    shared_out[channels + 1 : CPAD, :] = jnp.zeros((CPAD - channels - 1, LANES), F32)
    lane = lane_index(channels)
    sums = [jnp.zeros((channels, LANES), F32) for _ in side_outs]
    for s in range(samples):
        for y in range(rows):
            row = latent[s, :, y, :]
            place = 2 * (s * rows + y)
            right = pltpu.roll(row, (place + 2) % LANES, 1)
            left = row if place == 0 else pltpu.roll(row, place, 1)
            if count > 2:
                values = (right, left)
            else:
                values = (jnp.where(col_place == 0, right, left),)
            hit = (lane == place) | (lane == place + 1)
            sums = [jnp.where(hit, v, t) for v, t in zip(values, sums)]
    base = 2 * samples * rows
    for h in range(coarse_rows):
        line = coarse[:, h, :]
        right = jnp.broadcast_to(line[:, local_cols - 1 : local_cols], (channels, LANES))
        left = jnp.broadcast_to(line[:, 0:1], (channels, LANES))
        if count > 2:
            values = (right, left)
        else:
            values = (jnp.where(col_place == 0, right, left),)
        sums = [jnp.where(lane == base + h, v, t) for v, t in zip(values, sums)]
    for out, total in zip(side_outs, sums):
        out[0:channels, :] = total
        out[channels:CPAD, :] = jnp.zeros((CPAD - channels, LANES), F32)


def blend(target, index, size):
    twice = 2.0 * target + (1.0 - FACTOR)
    lower = jnp.floor(twice * (1.0 / (2 * FACTOR)))
    fraction = (twice - lower * (2.0 * FACTOR)) * (1.0 / (2 * FACTOR))
    fraction = jnp.where(lower < 0.0, 0.0, fraction)
    low = jnp.clip(lower, 0.0, size - 1.0)
    high = jnp.clip(lower + 1.0, 0.0, size - 1.0)
    return jnp.where(low == index, 1.0 - fraction, 0.0) + jnp.where(high == index, fraction, 0.0)


def row_weight(row, h, size):
    twice = 2 * row + 1 - FACTOR
    lower = (twice + 2 * FACTOR) // (2 * FACTOR) - 1
    fraction = (twice - lower * 2 * FACTOR).astype(F32) * (1.0 / (2 * FACTOR))
    fraction = jnp.where(lower < 0, 0.0, fraction)
    low = jnp.clip(lower, 0, size - 1)
    high = jnp.clip(lower + 1, 0, size - 1)
    return jnp.where(low == h, 1.0 - fraction, 0.0) + jnp.where(high == h, fraction, 0.0)


def main_kernel(
    dims,
    steps,
    latent,
    coarse,
    weight_in,
    bias_in,
    weight_noise,
    own_mid,
    other_mid,
    own_shared,
    other_shared,
    rows_in,
    *rest,
):
    sides = rest[: dims["messages"]]
    corners = rest[dims["messages"] : 2 * dims["messages"]]
    net_out, mean_out, xs, zx, w1, ce, hs, tr = rest[2 * dims["messages"] :]
    samples, channels, rows, cols = latent.shape
    coarse_rows, local_cols = coarse.shape[1:]
    taps, hidden, deep = weight_in.shape
    half = rows // 2
    reach = half + 4
    height, width = dims["row"] * rows, dims["col"] * cols
    coarse_cols = dims["col"] * local_cols
    block = 3 * deep + 8
    row_place = lax.axis_index("row")
    col_place = lax.axis_index("col")
    place = lax.axis_index("chan")
    upper = place == 0
    start = row_place * rows + half * place - 2
    lane = lane_index(CPAD)
    even = lane % 2 == 0

    w1[...] = jnp.zeros(w1.shape, F32)
    for i in range(3):
        for j in range(3):
            at = i * block + j * deep
            w1[:, at : at + deep] = weight_in[3 * i + j].astype(F32)
    vectors = jnp.concatenate(
        [bias_in[...], weight_noise[...], jnp.zeros((LANES - 2, hidden), F32)], axis=0
    )
    columns = vectors.T
    bias_terms = three_terms(columns[:, 0:1])
    noise_terms = three_terms(columns[:, 1:2])
    for i in range(3):
        at = i * block + 3 * deep
        w1[:, at : at + 1] = bias_terms[i]
        for j in range(3 - i):
            w1[:, at + 1 + j : at + 2 + j] = noise_terms[i]

    for y in range(rows):
        for s in range(samples):
            xs[2 + y, s, 0:channels, :] = latent[s, :, y, :]
            xs[2 + y, s, channels:CPAD, :] = jnp.zeros((CPAD - channels, LANES), F32)
    for near in range(2):
        for s in range(samples):
            got = rows_in[near * samples + s].astype(F32)
            xs[near, s] = got
            xs[2 + rows + near, s] = got
    tile = {}
    for v in range(reach):
        row = start + v
        inside = (row >= 0) & (row < height)
        for s in range(samples):
            tile[s, v] = jnp.where(inside, xs[half * place + v, s], 0.0)

    lane_v = (lane // 2) % reach
    lane_row = start + lane_v
    row_ok = (lane_row >= 0) & (lane_row < height) & (lane < 2 * samples * reach)
    near_first = jnp.where(upper, 0, reach - 2)
    near_line = (lane_v >= near_first) & (lane_v < near_first + 2)

    def halo(side, corner, ok):
        shift = 2 * (reach - rows)
        from_side = jnp.where(
            upper,
            pltpu.roll(side, 4, 1),
            pltpu.roll(side, (4 - 2 * half) % LANES, 1),
        )
        from_corner = jnp.where(
            upper,
            pltpu.roll(corner, (4 - 2 * rows) % LANES, 1),
            pltpu.roll(corner, 2 * reach - 4, 1),
        )
        return jnp.where(row_ok & ok, jnp.where(near_line, from_corner, from_side), 0.0)

    from_left = halo(sides[0][...], corners[0][...], col_place > 0)
    from_right = halo(sides[-1][...], corners[-1][...], col_place < dims["col"] - 1)
    own = jnp.zeros((CPAD, LANES), F32)
    for s in range(samples):
        for v in range(reach):
            at = 2 * (s * reach + v)
            first = tile[s, v] if at == 0 else pltpu.roll(tile[s, v], at, 1)
            own = jnp.where(lane == at, first, own)
            own = jnp.where(lane == at + 1, pltpu.roll(tile[s, v], (at + 2) % LANES, 1), own)
    edge = (
        jnp.where(even, from_left, own),
        jnp.where(even, pltpu.roll(from_left, LANES - 1, 1), pltpu.roll(from_right, 1, 1)),
        jnp.where(even, own, from_right),
    )

    ce[...] = jnp.zeros(ce.shape, F32)
    base = 2 * samples * rows
    for h in range(coarse_rows):
        at = h * CPAD
        ce[at : at + channels, 0:local_cols] = coarse[:, h, :]
        left = jnp.broadcast_to(sides[0][:, base + h : base + h + 1], (CPAD, 1))
        right = jnp.broadcast_to(sides[-1][:, base + h : base + h + 1], (CPAD, 1))
        ce[at : at + CPAD, local_cols : local_cols + 1] = left
        ce[at : at + CPAD, local_cols + 1 : local_cols + 2] = right
    group = local_cols + 2
    high, mid, low = three_terms(ce[...])
    cells = (high + pltpu.roll(mid, group, 1) + pltpu.roll(low, 2 * group, 1)).astype(BF16)
    depth = lax.broadcasted_iota(jnp.int32, (LANES, LANES), 0)
    spot = depth % group
    index = col_place * local_cols + jnp.where(
        spot < local_cols, spot, jnp.where(spot == local_cols, -1, local_cols)
    )
    index = jnp.where(depth < 3 * group, index, -2).astype(F32)
    wide = lax.broadcasted_iota(jnp.int32, (LANES, LANES), 1)
    targets = [col_place * cols + wide - 1 + j for j in range(3)]
    targets += [
        col_place * cols + jnp.where(wide % 2 == 0, j - 2, cols - 1 + j) for j in range(3)
    ]
    cols_matrix = [
        jnp.where((t >= 0) & (t < width), blend(t.astype(F32), index, coarse_cols), 0.0)
        for t in targets
    ]
    cols_matrix = jnp.concatenate([m.astype(BF16) for m in cols_matrix], axis=1)
    spread = jnp.dot(cells, cols_matrix, preferred_element_type=F32)

    def mean_of(weights, j):
        total = None
        for h in range(coarse_rows):
            term = weights[h] * spread[h * CPAD : (h + 1) * CPAD, j * LANES : (j + 1) * LANES]
            total = term if total is None else total + term
        return total

    ones = jnp.ones((1, LANES), F32)
    level_terms = [
        three_terms(jnp.log(noise_level(ones * steps[s].astype(F32))) * 0.25)
        for s in range(samples)
    ]
    tails = [
        jnp.concatenate([ones, *level_terms[s], jnp.zeros((4, LANES), F32)], axis=0)
        for s in range(samples)
    ]
    means = {}
    for v in range(reach):
        row = start + v
        inside = (row >= 0) & (row < height)
        weights = [
            jnp.where(inside, row_weight(row, h, coarse_rows), 0.0) for h in range(coarse_rows)
        ]
        for j in range(3):
            means[v, j] = mean_of(weights, j)
    for y in range(rows):
        row = row_place * rows + y
        mean_out[y] = mean_of([row_weight(row, h, coarse_rows) for h in range(coarse_rows)], 1)
    lane_weights = [
        jnp.where(
            row_ok, blend(lane_row.astype(F32), float(h), coarse_rows), 0.0
        )
        for h in range(coarse_rows)
    ]
    edge_means = [mean_of(lane_weights, 3 + j) for j in range(3)]

    for s in range(samples):
        for v in range(reach):
            at = 2 * (s * reach + v)
            turned = pltpu.roll(edge[1], LANES - 1 - at, 1)
            here = tile[s, v]
            moved = (
                pltpu.roll(jnp.where(lane == LANES - 1, turned, here), 1, 1),
                here,
                pltpu.roll(jnp.where(lane == 0, turned, here), LANES - 1, 1),
            )
            for j in range(3):
                zx[s, v, j * deep : j * deep + channels, :] = moved[j][0:channels]
                zx[s, v, j * deep + channels : (j + 1) * deep, :] = means[v, j][0:channels]
            zx[s, v, 3 * deep : block, :] = tails[s]
    sample_of = lane_index(8) // (2 * reach)
    edge_tail = tails[0]
    for s in range(1, samples):
        edge_tail = jnp.where(sample_of == s, tails[s], edge_tail)
    edge_block = jnp.concatenate(
        sum([[edge[j][0:channels], edge_means[j][0:channels]] for j in range(3)], []) + [edge_tail],
        axis=0,
    )

    first_weight = w1[...].astype(BF16)
    stacked = jnp.concatenate(
        [edge_block, pltpu.roll(edge_block, LANES - 2, 1), pltpu.roll(edge_block, LANES - 4, 1)],
        axis=0,
    ).astype(BF16)
    edge_hidden = silu(jnp.dot(first_weight, stacked, preferred_element_type=F32))
    lane_h = lane_index(hidden)
    v_h = (lane_h // 2) % reach
    row_h = start + 1 + v_h
    side_h = col_place + lane_h % 2
    side_h = (side_h > 0) & (side_h < dims["col"])
    edge_hidden = jnp.where((row_h >= 0) & (row_h < height) & side_h, edge_hidden, 0.0)
    for s in range(samples):
        for v in range(0, half + 2, 2):
            pair = jnp.concatenate(
                [
                    jnp.concatenate([zx[s, v + e + i] for i in range(3)], axis=0).astype(BF16)
                    for e in range(2)
                ],
                axis=1,
            )
            value = silu(jnp.dot(first_weight, pair, preferred_element_type=F32))
            for e in range(2):
                row = start + 1 + v + e
                inside = (row >= 0) & (row < height)
                here = jnp.where(inside, value[:, e * LANES : (e + 1) * LANES], 0.0)
                at = 2 * (s * reach + v + e)
                turned = pltpu.roll(edge_hidden, LANES - 1 - at, 1)
                left = pltpu.roll(jnp.where(lane_h == LANES - 1, turned, here), 1, 1)
                right = pltpu.roll(jnp.where(lane_h == 0, turned, here), LANES - 1, 1)
                hs[0, s, v + e] = left.astype(BF16)
                hs[1, s, v + e] = here.astype(BF16)
                hs[2, s, v + e] = right.astype(BF16)

    tr[...] = jnp.zeros(tr.shape, F32)
    tr[0:CPAD] = own_shared[...]
    own_bias = tr[...].T[:, channels : channels + 1]
    tr[0:CPAD] = other_shared[...]
    other_bias = tr[...].T[:, channels : channels + 1]
    bias = jnp.concatenate([own_bias, other_bias], axis=0)
    out_weight = jnp.concatenate([own_shared[...], other_shared[...]], axis=1).astype(BF16)
    second_weight = jnp.concatenate(
        [
            jnp.concatenate([own_mid[t] for t in range(taps)], axis=1),
            jnp.concatenate([other_mid[t] for t in range(taps)], axis=1),
        ],
        axis=0,
    )
    for s in range(samples):
        for v in range(0, half, 2):
            stacked = jnp.concatenate(
                [
                    jnp.concatenate([hs[j, s, v + i], hs[j, s, v + 1 + i]], axis=1)
                    for i in range(3)
                    for j in range(3)
                ],
                axis=0,
            )
            value = jnp.dot(second_weight, stacked, preferred_element_type=F32)
            middle = silu(value + bias).astype(BF16)
            net = jnp.dot(out_weight, middle, preferred_element_type=F32)
            for e in range(2):
                net_out[s * half + v + e] = net[:, e * LANES : (e + 1) * LANES]
    del cols, place


def finish_kernel(steps, latent, fresh, own_net, other_net, own_mean, fine, following):
    samples, channels, rows, cols = latent.shape
    half = rows // 2
    upper = lax.axis_index("chan") == 0

    def joined(own, other, at):
        a = jnp.swapaxes(own[at : at + half], 0, 1)
        b = jnp.swapaxes(other[at : at + half], 0, 1)
        return jnp.concatenate([jnp.where(upper, a, b), jnp.where(upper, b, a)], axis=1)

    mean = jnp.swapaxes(own_mean[...], 0, 1)[0:channels]
    for s in range(samples):
        net = joined(own_net[...], other_net[...], s * half)[0:channels]
        step = jnp.full((1, 1, cols), 1.0, F32) * steps[s].astype(F32)
        now = noise_level(step)
        ahead = noise_level(step + 1.0)
        variance = now * now + sigma_data * sigma_data
        scale = jnp.sqrt(variance)
        skip = sigma_data * sigma_data / variance * scale
        gain = sigma_data * now / scale
        denoised = skip * latent[s] + gain * net
        fine[s] = mean + denoised
        inverse = 1.0 / jnp.sqrt(ahead * ahead + sigma_data * sigma_data)
        following[s] = (denoised + ahead * fresh[s]) * inverse


def on_device(
    dims,
    latent,
    fresh_noise,
    step_index,
    coarse,
    weight_in,
    bias_in,
    weight_noise,
    weight_mid,
    bias_mid,
    weight_out,
):
    samples, channels, rows, cols = latent.shape
    taps, hidden, deep = weight_in.shape
    half = rows // 2
    row_count, col_count = dims["row"], dims["col"]
    messages = dims["messages"]
    vmem = pl.BlockSpec(memory_space=pltpu.VMEM)
    smem = pl.BlockSpec(memory_space=pltpu.SMEM)
    struct = jax.ShapeDtypeStruct

    swap = [(0, 1), (1, 0)]
    other_mid = lax.ppermute(weight_mid, "chan", swap)
    packed = pl.pallas_call(
        functools.partial(pack_kernel, dims),
        out_shape=[
            struct((2 * samples, CPAD, cols), BF16),
            struct((CPAD, hidden // 2), F32),
        ]
        + [struct((CPAD, LANES), F32)] * messages,
        in_specs=[vmem] * 4,
        out_specs=[vmem] * (2 + messages),
        name="pack",
    )(latent, coarse, weight_out, bias_mid.reshape(1, -1))
    rows_message, shared, side_messages = packed[0], packed[1], packed[2:]

    down = [(r, 0, r + 1, 0) for r in range(row_count - 1)]
    down += [(r + 1, 1, r, 1) for r in range(row_count - 1)]
    ends = [(row_count - 1, 0, row_count - 1, 1), (0, 1, 0, 0)]
    vertical = [(2 * a + b, 2 * c + d) for a, b, c, d in down + ends]
    rows_in = lax.ppermute(rows_message, ("row", "chan"), vertical)
    sides, corners = [], []
    for n, message in enumerate(side_messages):
        if col_count > 2:
            step = 1 if n == 0 else -1
            columns = [(i, (i + step) % col_count) for i in range(col_count)]
        else:
            columns = [(i, col_count - 1 - i) for i in range(col_count)]
        sides.append(lax.ppermute(message, "col", columns))
        diagonal = [
            (2 * (a * col_count + i) + b, 2 * (c * col_count + k) + d)
            for a, b, c, d in down
            for i, k in columns
        ]
        diagonal += [
            (2 * (a * col_count + i) + b, 2 * (c * col_count + i) + d)
            for a, b, c, d in ends
            for i in range(col_count)
        ]
        corners.append(lax.ppermute(message, ("row", "col", "chan"), diagonal))
    other_shared = lax.ppermute(shared, "chan", swap)

    block = 3 * deep + 8
    net, mean = pl.pallas_call(
        functools.partial(main_kernel, dims),
        out_shape=[
            struct((samples * half, CPAD, cols), F32),
            struct((rows, CPAD, cols), F32),
        ],
        in_specs=[smem] + [vmem] * (10 + 2 * messages),
        out_specs=[vmem] * 2,
        scratch_shapes=[
            pltpu.VMEM((rows + 4, samples, CPAD, cols), F32),
            pltpu.VMEM((samples, half + 4, block, cols), F32),
            pltpu.VMEM((hidden, 3 * block), F32),
            pltpu.VMEM((coarse.shape[1] * CPAD, LANES), F32),
            pltpu.VMEM((3, samples, half + 2, hidden, cols), BF16),
            pltpu.VMEM((LANES, LANES), F32),
        ],
        name="sections",
    )(
        step_index,
        latent,
        coarse,
        weight_in,
        bias_in.reshape(1, -1),
        weight_noise.reshape(1, -1),
        weight_mid,
        other_mid,
        shared,
        other_shared,
        rows_in,
        *sides,
        *corners,
    )
    other_net = lax.ppermute(net, "chan", swap)
    return pl.pallas_call(
        finish_kernel,
        out_shape=[struct(latent.shape, F32)] * 2,
        in_specs=[smem] + [vmem] * 5,
        out_specs=[vmem] * 2,
        name="finish",
    )(step_index, latent, fresh_noise, net, other_net, mean)


def solution(mesh):
    dims = {axis: mesh.shape[axis] for axis in ("row", "col", "chan")}
    dims["messages"] = 2 if dims["col"] > 2 else 1
    tile = P("ens", None, "row", "col")
    in_specs = (
        tile,
        tile,
        P("ens"),
        P("ens", None, "col"),
        P(),
        P(),
        P(),
        P(None, "chan", None),
        P("chan"),
        P(None, "chan"),
    )

    def body(*args):
        return tuple(on_device(dims, *args))

    return jax.shard_map(
        body, mesh=mesh, in_specs=in_specs, out_specs=(tile, tile), check_vma=False
    )
```

```python
import functools

import jax
import jax.numpy as jnp
from jax import lax
from jax.experimental import pallas as pl
from jax.experimental.pallas import tpu as pltpu
from jax.sharding import PartitionSpec as P

STEPS = 18
FACTOR = 8

sigma_data = 0.5
sigma_high = 80.0
sigma_low = 0.002
rho_power = 7.0

F32 = jnp.float32
BF16 = jnp.bfloat16
LANES = 128
CPAD = 16


def lane_index(rows):
    return lax.broadcasted_iota(jnp.int32, (rows, LANES), 1)


def noise_level(position):
    top_root = sigma_high ** (1.0 / rho_power)
    bottom_root = sigma_low ** (1.0 / rho_power)
    root = top_root + position * (1.0 / (STEPS - 1)) * (bottom_root - top_root)
    square = root * root
    return square * square * square * root


def silu(value):
    half = 0.5 * value
    return half + half * jnp.tanh(half)


def three_terms(value):
    high = value.astype(BF16).astype(F32)
    rest = value - high
    mid = rest.astype(BF16).astype(F32)
    return high, mid, (rest - mid).astype(BF16).astype(F32)


def pack_kernel(dims, latent, coarse, weight_out, bias_mid, own_out, rows_out, shared_out, *side_outs):
    samples, channels, rows, cols = latent.shape
    coarse_rows, local_cols = coarse.shape[1:]
    count = dims["col"]
    col_place = lax.axis_index("col")
    lower = lax.axis_index("chan") == 1
    for near in range(2):
        for s in range(samples):
            first = latent[s, :, near, :]
            last = latent[s, :, rows - 2 + near, :]
            rows_out[near * samples + s, 0:channels, :] = jnp.where(lower, first, last).astype(BF16)
            rows_out[near * samples + s, channels:CPAD, :] = jnp.zeros(
                (CPAD - channels, LANES), BF16
            )
    for out in (own_out, shared_out):
        out[0:channels, :] = weight_out[...].astype(F32)
        out[channels : channels + 1, :] = bias_mid[...]
        out[channels + 1 : CPAD, :] = jnp.zeros((CPAD - channels - 1, LANES), F32)
    lane = lane_index(channels)
    sums = [jnp.zeros((channels, LANES), F32) for _ in side_outs]
    for s in range(samples):
        for y in range(rows):
            row = latent[s, :, y, :]
            place = 2 * (s * rows + y)
            right = pltpu.roll(row, (place + 2) % LANES, 1)
            left = row if place == 0 else pltpu.roll(row, place, 1)
            if count > 2:
                values = (right, left)
            else:
                values = (jnp.where(col_place == 0, right, left),)
            hit = (lane == place) | (lane == place + 1)
            sums = [jnp.where(hit, v, t) for v, t in zip(values, sums)]
    base = 2 * samples * rows
    for h in range(coarse_rows):
        line = coarse[:, h, :]
        right = jnp.broadcast_to(line[:, local_cols - 1 : local_cols], (channels, LANES))
        left = jnp.broadcast_to(line[:, 0:1], (channels, LANES))
        if count > 2:
            values = (right, left)
        else:
            values = (jnp.where(col_place == 0, right, left),)
        sums = [jnp.where(lane == base + h, v, t) for v, t in zip(values, sums)]
    for out, total in zip(side_outs, sums):
        out[0:channels, :] = total
        out[channels:CPAD, :] = jnp.zeros((CPAD - channels, LANES), F32)


def blend(target, index, size):
    twice = 2.0 * target + (1.0 - FACTOR)
    lower = jnp.floor(twice * (1.0 / (2 * FACTOR)))
    fraction = (twice - lower * (2.0 * FACTOR)) * (1.0 / (2 * FACTOR))
    fraction = jnp.where(lower < 0.0, 0.0, fraction)
    low = jnp.clip(lower, 0.0, size - 1.0)
    high = jnp.clip(lower + 1.0, 0.0, size - 1.0)
    return jnp.where(low == index, 1.0 - fraction, 0.0) + jnp.where(high == index, fraction, 0.0)


def row_weight(row, h, size):
    twice = 2 * row + 1 - FACTOR
    lower = (twice + 2 * FACTOR) // (2 * FACTOR) - 1
    fraction = (twice - lower * 2 * FACTOR).astype(F32) * (1.0 / (2 * FACTOR))
    fraction = jnp.where(lower < 0, 0.0, fraction)
    low = jnp.clip(lower, 0, size - 1)
    high = jnp.clip(lower + 1, 0, size - 1)
    return jnp.where(low == h, 1.0 - fraction, 0.0) + jnp.where(high == h, fraction, 0.0)


def main_kernel(
    dims,
    steps,
    latent,
    coarse,
    weight_in,
    bias_in,
    weight_noise,
    own_mid,
    other_mid,
    own_shared,
    other_shared,
    rows_in,
    *rest,
):
    sides = rest[: dims["messages"]]
    corners = rest[dims["messages"] : 2 * dims["messages"]]
    net_out, own_out, mean_out, xs, zx, w1, ce, hs, tr = rest[2 * dims["messages"] :]
    samples, channels, rows, cols = latent.shape
    coarse_rows, local_cols = coarse.shape[1:]
    taps, hidden, deep = weight_in.shape
    half = rows // 2
    reach = half + 4
    height, width = dims["row"] * rows, dims["col"] * cols
    coarse_cols = dims["col"] * local_cols
    block = 3 * deep + 8
    row_place = lax.axis_index("row")
    col_place = lax.axis_index("col")
    place = lax.axis_index("chan")
    upper = place == 0
    start = row_place * rows + half * place - 2
    lane = lane_index(CPAD)
    even = lane % 2 == 0

    w1[...] = jnp.zeros(w1.shape, F32)
    for i in range(3):
        for j in range(3):
            at = i * block + j * deep
            w1[:, at : at + deep] = weight_in[3 * i + j].astype(F32)
    vectors = jnp.concatenate(
        [bias_in[...], weight_noise[...], jnp.zeros((LANES - 2, hidden), F32)], axis=0
    )
    columns = vectors.T
    bias_terms = three_terms(columns[:, 0:1])
    noise_terms = three_terms(columns[:, 1:2])
    for i in range(3):
        at = i * block + 3 * deep
        w1[:, at : at + 1] = bias_terms[i]
        for j in range(3 - i):
            w1[:, at + 1 + j : at + 2 + j] = noise_terms[i]

    for y in range(rows):
        for s in range(samples):
            xs[2 + y, s, 0:channels, :] = latent[s, :, y, :]
            xs[2 + y, s, channels:CPAD, :] = jnp.zeros((CPAD - channels, LANES), F32)
    for near in range(2):
        for s in range(samples):
            got = rows_in[near * samples + s].astype(F32)
            xs[near, s] = got
            xs[2 + rows + near, s] = got
    tile = {}
    for v in range(reach):
        row = start + v
        inside = (row >= 0) & (row < height)
        for s in range(samples):
            tile[s, v] = jnp.where(inside, xs[half * place + v, s], 0.0)

    lane_v = (lane // 2) % reach
    lane_row = start + lane_v
    row_ok = (lane_row >= 0) & (lane_row < height) & (lane < 2 * samples * reach)
    near_first = jnp.where(upper, 0, reach - 2)
    near_line = (lane_v >= near_first) & (lane_v < near_first + 2)

    def halo(side, corner, ok):
        shift = 2 * (reach - rows)
        from_side = jnp.where(
            upper,
            pltpu.roll(side, 4, 1),
            pltpu.roll(side, (4 - 2 * half) % LANES, 1),
        )
        from_corner = jnp.where(
            upper,
            pltpu.roll(corner, (4 - 2 * rows) % LANES, 1),
            pltpu.roll(corner, 2 * reach - 4, 1),
        )
        return jnp.where(row_ok & ok, jnp.where(near_line, from_corner, from_side), 0.0)

    from_left = halo(sides[0][...], corners[0][...], col_place > 0)
    from_right = halo(sides[-1][...], corners[-1][...], col_place < dims["col"] - 1)
    own = jnp.zeros((CPAD, LANES), F32)
    for s in range(samples):
        for v in range(reach):
            at = 2 * (s * reach + v)
            first = tile[s, v] if at == 0 else pltpu.roll(tile[s, v], at, 1)
            own = jnp.where(lane == at, first, own)
            own = jnp.where(lane == at + 1, pltpu.roll(tile[s, v], (at + 2) % LANES, 1), own)
    edge = (
        jnp.where(even, from_left, own),
        jnp.where(even, pltpu.roll(from_left, LANES - 1, 1), pltpu.roll(from_right, 1, 1)),
        jnp.where(even, own, from_right),
    )

    ce[...] = jnp.zeros(ce.shape, F32)
    base = 2 * samples * rows
    for h in range(coarse_rows):
        at = h * CPAD
        ce[at : at + channels, 0:local_cols] = coarse[:, h, :]
        left = jnp.broadcast_to(sides[0][:, base + h : base + h + 1], (CPAD, 1))
        right = jnp.broadcast_to(sides[-1][:, base + h : base + h + 1], (CPAD, 1))
        ce[at : at + CPAD, local_cols : local_cols + 1] = left
        ce[at : at + CPAD, local_cols + 1 : local_cols + 2] = right
    group = local_cols + 2
    high, mid, low = three_terms(ce[...])
    cells = (high + pltpu.roll(mid, group, 1) + pltpu.roll(low, 2 * group, 1)).astype(BF16)
    depth = lax.broadcasted_iota(jnp.int32, (LANES, LANES), 0)
    spot = depth % group
    index = col_place * local_cols + jnp.where(
        spot < local_cols, spot, jnp.where(spot == local_cols, -1, local_cols)
    )
    index = jnp.where(depth < 3 * group, index, -2).astype(F32)
    wide = lax.broadcasted_iota(jnp.int32, (LANES, LANES), 1)
    targets = [col_place * cols + wide - 1 + j for j in range(3)]
    targets += [
        col_place * cols + jnp.where(wide % 2 == 0, j - 2, cols - 1 + j) for j in range(3)
    ]
    cols_matrix = [
        jnp.where((t >= 0) & (t < width), blend(t.astype(F32), index, coarse_cols), 0.0)
        for t in targets
    ]
    cols_matrix = jnp.concatenate([m.astype(BF16) for m in cols_matrix], axis=1)
    spread = jnp.dot(cells, cols_matrix, preferred_element_type=F32)

    def mean_of(weights, j):
        total = None
        for h in range(coarse_rows):
            term = weights[h] * spread[h * CPAD : (h + 1) * CPAD, j * LANES : (j + 1) * LANES]
            total = term if total is None else total + term
        return total

    ones = jnp.ones((1, LANES), F32)
    level_terms = [
        three_terms(jnp.log(noise_level(ones * steps[s].astype(F32))) * 0.25)
        for s in range(samples)
    ]
    tails = [
        jnp.concatenate([ones, *level_terms[s], jnp.zeros((4, LANES), F32)], axis=0)
        for s in range(samples)
    ]
    means = {}
    for v in range(reach):
        row = start + v
        inside = (row >= 0) & (row < height)
        weights = [
            jnp.where(inside, row_weight(row, h, coarse_rows), 0.0) for h in range(coarse_rows)
        ]
        for j in range(3):
            means[v, j] = mean_of(weights, j)
    for y in range(rows):
        row = row_place * rows + y
        mean_out[y] = mean_of([row_weight(row, h, coarse_rows) for h in range(coarse_rows)], 1)
    lane_weights = [
        jnp.where(
            row_ok, blend(lane_row.astype(F32), float(h), coarse_rows), 0.0
        )
        for h in range(coarse_rows)
    ]
    edge_means = [mean_of(lane_weights, 3 + j) for j in range(3)]

    for s in range(samples):
        for v in range(reach):
            at = 2 * (s * reach + v)
            turned = pltpu.roll(edge[1], LANES - 1 - at, 1)
            here = tile[s, v]
            moved = (
                pltpu.roll(jnp.where(lane == LANES - 1, turned, here), 1, 1),
                here,
                pltpu.roll(jnp.where(lane == 0, turned, here), LANES - 1, 1),
            )
            for j in range(3):
                zx[s, v, j * deep : j * deep + channels, :] = moved[j][0:channels]
                zx[s, v, j * deep + channels : (j + 1) * deep, :] = means[v, j][0:channels]
            zx[s, v, 3 * deep : block, :] = tails[s]
    sample_of = lane_index(8) // (2 * reach)
    edge_tail = tails[0]
    for s in range(1, samples):
        edge_tail = jnp.where(sample_of == s, tails[s], edge_tail)
    edge_block = jnp.concatenate(
        sum([[edge[j][0:channels], edge_means[j][0:channels]] for j in range(3)], []) + [edge_tail],
        axis=0,
    )

    first_weight = w1[...].astype(BF16)
    stacked = jnp.concatenate(
        [edge_block, pltpu.roll(edge_block, LANES - 2, 1), pltpu.roll(edge_block, LANES - 4, 1)],
        axis=0,
    ).astype(BF16)
    edge_hidden = silu(jnp.dot(first_weight, stacked, preferred_element_type=F32))
    lane_h = lane_index(hidden)
    v_h = (lane_h // 2) % reach
    row_h = start + 1 + v_h
    side_h = col_place + lane_h % 2
    side_h = (side_h > 0) & (side_h < dims["col"])
    edge_hidden = jnp.where((row_h >= 0) & (row_h < height) & side_h, edge_hidden, 0.0)
    for s in range(samples):
        for v in range(0, half + 2, 2):
            pair = jnp.concatenate(
                [
                    jnp.concatenate([zx[s, v + e + i] for i in range(3)], axis=0).astype(BF16)
                    for e in range(2)
                ],
                axis=1,
            )
            value = silu(jnp.dot(first_weight, pair, preferred_element_type=F32))
            for e in range(2):
                row = start + 1 + v + e
                inside = (row >= 0) & (row < height)
                here = jnp.where(inside, value[:, e * LANES : (e + 1) * LANES], 0.0)
                at = 2 * (s * reach + v + e)
                turned = pltpu.roll(edge_hidden, LANES - 1 - at, 1)
                left = pltpu.roll(jnp.where(lane_h == LANES - 1, turned, here), 1, 1)
                right = pltpu.roll(jnp.where(lane_h == 0, turned, here), LANES - 1, 1)
                hs[0, s, v + e] = left.astype(BF16)
                hs[1, s, v + e] = here.astype(BF16)
                hs[2, s, v + e] = right.astype(BF16)

    tr[...] = jnp.zeros(tr.shape, F32)
    tr[0:CPAD] = own_shared[...]
    own_bias = tr[...].T[:, channels : channels + 1]
    tr[0:CPAD] = other_shared[...]
    other_bias = tr[...].T[:, channels : channels + 1]
    bias = jnp.concatenate([own_bias, other_bias], axis=0)
    out_weight = jnp.concatenate([own_shared[...], other_shared[...]], axis=1).astype(BF16)
    second_weight = jnp.concatenate(
        [
            jnp.concatenate([own_mid[t] for t in range(taps)], axis=1),
            jnp.concatenate([other_mid[t] for t in range(taps)], axis=1),
        ],
        axis=0,
    )
    for s in range(samples):
        for v in range(0, half, 2):
            stacked = jnp.concatenate(
                [
                    jnp.concatenate([hs[j, s, v + i], hs[j, s, v + 1 + i]], axis=1)
                    for i in range(3)
                    for j in range(3)
                ],
                axis=0,
            )
            value = jnp.dot(second_weight, stacked, preferred_element_type=F32)
            middle = silu(value + bias).astype(BF16)
            net = jnp.dot(out_weight, middle, preferred_element_type=F32)
            for e in range(2):
                net_out[s * half + v + e] = net[:, e * LANES : (e + 1) * LANES]
                own_out[s * half + v + e] = net[:, e * LANES : (e + 1) * LANES]
    del cols, place


def finish_kernel(steps, latent, fresh, own_net, other_net, own_mean, fine, following):
    samples, channels, rows, cols = latent.shape
    half = rows // 2
    upper = lax.axis_index("chan") == 0

    def joined(own, other, at):
        a = jnp.swapaxes(own[at : at + half], 0, 1)
        b = jnp.swapaxes(other[at : at + half], 0, 1)
        return jnp.concatenate([jnp.where(upper, a, b), jnp.where(upper, b, a)], axis=1)

    mean = jnp.swapaxes(own_mean[...], 0, 1)[0:channels]
    for s in range(samples):
        net = joined(own_net[...], other_net[...], s * half)[0:channels]
        step = jnp.full((1, 1, cols), 1.0, F32) * steps[s].astype(F32)
        now = noise_level(step)
        ahead = noise_level(step + 1.0)
        variance = now * now + sigma_data * sigma_data
        scale = jnp.sqrt(variance)
        skip = sigma_data * sigma_data / variance * scale
        gain = sigma_data * now / scale
        denoised = skip * latent[s] + gain * net
        fine[s] = mean + denoised
        inverse = 1.0 / jnp.sqrt(ahead * ahead + sigma_data * sigma_data)
        following[s] = (denoised + ahead * fresh[s]) * inverse


def on_device(
    dims,
    latent,
    fresh_noise,
    step_index,
    coarse,
    weight_in,
    bias_in,
    weight_noise,
    weight_mid,
    bias_mid,
    weight_out,
):
    samples, channels, rows, cols = latent.shape
    taps, hidden, deep = weight_in.shape
    half = rows // 2
    row_count, col_count = dims["row"], dims["col"]
    messages = dims["messages"]
    vmem = pl.BlockSpec(memory_space=pltpu.VMEM)
    smem = pl.BlockSpec(memory_space=pltpu.SMEM)
    struct = jax.ShapeDtypeStruct
    near = functools.partial(pltpu.with_memory_space_constraint, memory_space=pltpu.VMEM)

    swap = [(0, 1), (1, 0)]
    other_mid = lax.ppermute(weight_mid, "chan", swap)
    packed = pl.pallas_call(
        functools.partial(pack_kernel, dims),
        out_shape=[
            pltpu.VMEM((CPAD, hidden // 2), F32),
            struct((2 * samples, CPAD, cols), BF16),
            struct((CPAD, hidden // 2), F32),
        ]
        + [struct((CPAD, LANES), F32)] * messages,
        in_specs=[vmem] * 4,
        out_specs=[vmem] * (3 + messages),
        name="pack",
    )(latent, coarse, weight_out, bias_mid.reshape(1, -1))
    own_shared, rows_message, shared, side_messages = *packed[:3], packed[3:]

    down = [(r, 0, r + 1, 0) for r in range(row_count - 1)]
    down += [(r + 1, 1, r, 1) for r in range(row_count - 1)]
    ends = [(row_count - 1, 0, row_count - 1, 1), (0, 1, 0, 0)]
    vertical = [(2 * a + b, 2 * c + d) for a, b, c, d in down + ends]
    rows_in = lax.ppermute(rows_message, ("row", "chan"), vertical)
    sides, corners = [], []
    for n, message in enumerate(side_messages):
        if col_count > 2:
            step = 1 if n == 0 else -1
            columns = [(i, (i + step) % col_count) for i in range(col_count)]
        else:
            columns = [(i, col_count - 1 - i) for i in range(col_count)]
        sides.append(lax.ppermute(message, "col", columns))
        diagonal = [
            (2 * (a * col_count + i) + b, 2 * (c * col_count + k) + d)
            for a, b, c, d in down
            for i, k in columns
        ]
        diagonal += [
            (2 * (a * col_count + i) + b, 2 * (c * col_count + i) + d)
            for a, b, c, d in ends
            for i in range(col_count)
        ]
        corners.append(lax.ppermute(message, ("row", "col", "chan"), diagonal))
    other_shared = lax.ppermute(shared, "chan", swap)

    block = 3 * deep + 8
    net, own_net, mean = pl.pallas_call(
        functools.partial(main_kernel, dims),
        out_shape=[
            struct((samples * half, CPAD, cols), F32),
            pltpu.VMEM((samples * half, CPAD, cols), F32),
            pltpu.VMEM((rows, CPAD, cols), F32),
        ],
        in_specs=[smem] + [vmem] * (10 + 2 * messages),
        out_specs=[vmem] * 3,
        scratch_shapes=[
            pltpu.VMEM((rows + 4, samples, CPAD, cols), F32),
            pltpu.VMEM((samples, half + 4, block, cols), F32),
            pltpu.VMEM((hidden, 3 * block), F32),
            pltpu.VMEM((coarse.shape[1] * CPAD, LANES), F32),
            pltpu.VMEM((3, samples, half + 2, hidden, cols), BF16),
            pltpu.VMEM((LANES, LANES), F32),
        ],
        name="sections",
    )(
        step_index,
        near(latent),
        near(coarse),
        near(weight_in),
        near(bias_in.reshape(1, -1)),
        near(weight_noise.reshape(1, -1)),
        near(weight_mid),
        near(other_mid),
        near(own_shared),
        near(other_shared),
        near(rows_in),
        *[near(side) for side in sides],
        *[near(corner) for corner in corners],
    )
    other_net = lax.ppermute(net, "chan", swap)
    return pl.pallas_call(
        finish_kernel,
        out_shape=[struct(latent.shape, F32)] * 2,
        in_specs=[smem] + [vmem] * 5,
        out_specs=[vmem] * 2,
        name="finish",
    )(step_index, near(latent), near(fresh_noise), near(own_net), near(other_net), near(mean))


def solution(mesh):
    dims = {axis: mesh.shape[axis] for axis in ("row", "col", "chan")}
    dims["messages"] = 2 if dims["col"] > 2 else 1
    tile = P("ens", None, "row", "col")
    in_specs = (
        tile,
        tile,
        P("ens"),
        P("ens", None, "col"),
        P(),
        P(),
        P(),
        P(None, "chan", None),
        P("chan"),
        P(None, "chan"),
    )

    def body(*args):
        return tuple(on_device(dims, *args))

    return jax.shard_map(
        body, mesh=mesh, in_specs=in_specs, out_specs=(tile, tile), check_vma=False
    )
```

```python
import functools

import jax
import jax.numpy as jnp
from jax import lax
from jax.experimental import pallas as pl
from jax.experimental.pallas import tpu as pltpu
from jax.sharding import PartitionSpec as P

STEPS = 18
FACTOR = 8

sigma_data = 0.5
sigma_high = 80.0
sigma_low = 0.002
rho_power = 7.0

F32 = jnp.float32
BF16 = jnp.bfloat16
LANES = 128
CPAD = 16
LIMIT = pltpu.CompilerParams(vmem_limit_bytes=12 * 1024 * 1024)


def lane_index(rows):
    return lax.broadcasted_iota(jnp.int32, (rows, LANES), 1)


def tile_row(w, rows):
    return jnp.where(lax.axis_index("chan") == 0, w - 2, rows + 1 - w)


def tap_row(i):
    return jnp.where(lax.axis_index("chan") == 0, i, 2 - i)


def noise_level(position):
    top_root = sigma_high ** (1.0 / rho_power)
    bottom_root = sigma_low ** (1.0 / rho_power)
    root = top_root + position * (1.0 / (STEPS - 1)) * (bottom_root - top_root)
    square = root * root
    return square * square * square * root


def silu_of_half(half):
    return half + half * jnp.tanh(half)


def three_terms(value):
    high = value.astype(BF16).astype(F32)
    rest = value - high
    mid = rest.astype(BF16).astype(F32)
    return high, mid, (rest - mid).astype(BF16).astype(F32)


def channel_rows(ref, s, y, channels, rows):
    return ref[s, pl.ds(y, channels, stride=rows), :]


def pack_kernel(
    dims,
    latent_far,
    coarse_far,
    weight_out_far,
    bias_mid_far,
    weight_in_far,
    bias_in_far,
    weight_noise_far,
    steps_far,
    latent,
    coarse,
    weight_in,
    bias_in,
    weight_noise,
    steps_out,
    cols_matrix,
    rows_out,
    shared_out,
    *rest,
):
    sides = rest[: dims["messages"]]
    weight_out, bias_mid, steps, sem = rest[dims["messages"] :]
    pairs = (
        (latent_far, latent),
        (coarse_far, coarse),
        (weight_out_far, weight_out),
        (bias_mid_far, bias_mid),
        (steps_far, steps),
        (weight_in_far, weight_in),
        (bias_in_far, bias_in),
        (weight_noise_far, weight_noise),
    )
    copies = [pltpu.make_async_copy(a, b, sem.at[n]) for n, (a, b) in enumerate(pairs)]
    for copy in copies:
        copy.start()
    samples = latent.shape[0]
    channels, coarse_rows, local_cols = coarse.shape
    rows = latent.shape[1] // channels
    count = dims["col"]
    col_place = lax.axis_index("col")
    upper = lax.axis_index("chan") == 0

    cols = latent.shape[2]
    width = count * cols
    coarse_cols = count * local_cols
    group = local_cols + 2
    depth = lax.broadcasted_iota(jnp.int32, (cols_matrix.shape[0], LANES), 0)
    spot = depth % group
    index = col_place * local_cols + jnp.where(
        spot < local_cols, spot, jnp.where(spot == local_cols, -1, local_cols)
    )
    index = jnp.where(depth < 3 * group, index, -2).astype(F32)
    wide = lax.broadcasted_iota(jnp.int32, (1, LANES), 1)
    targets = [col_place * cols + wide - 1 + j for j in range(3)]
    targets += [
        col_place * cols + jnp.where(wide % 2 == 0, j - 2, cols - 1 + j) for j in range(3)
    ]
    for n, target in enumerate(targets):
        low, high, fraction = blend(target.astype(F32), coarse_cols)
        outside = (target < 0) | (target >= width)
        low = jnp.where(outside, -3.0, low)
        high = jnp.where(outside, -3.0, high)
        weights = jnp.where(low == index, 1.0 - fraction, 0.0)
        weights += jnp.where(high == index, fraction, 0.0)
        cols_matrix[:, n * LANES : (n + 1) * LANES] = weights.astype(BF16)

    copies[0].wait()
    for near in range(2):
        y = jnp.where(upper, rows - 2 + near, 1 - near)
        for s in range(samples):
            got = channel_rows(latent, s, y, channels, rows).astype(BF16)
            rows_out[near * samples + s, 0:channels, :] = got
            rows_out[near * samples + s, channels:CPAD, :] = jnp.zeros(
                (CPAD - channels, LANES), BF16
            )
    lane = lane_index(channels)
    sums = [jnp.zeros((channels, LANES), F32) for _ in sides]
    if count > 2:
        shifts = (2, 0)
    else:
        shifts = (jnp.where(col_place == 0, 2, 0),)
    for s in range(samples):
        for q in range(rows):
            y = jnp.where(upper, q, rows - 1 - q)
            row = channel_rows(latent, s, y, channels, rows)
            place = 2 * (s * rows + q)
            hit = (lane == place) | (lane == place + 1)
            sums = [
                jnp.where(hit, pltpu.roll(row, place + shift, 1), total)
                for shift, total in zip(shifts, sums)
            ]
    for copy in copies[1:5]:
        copy.wait()
    base = 2 * samples * rows
    for h in range(coarse_rows):
        line = coarse[:, h, :]
        right = jnp.broadcast_to(line[:, local_cols - 1 : local_cols], (channels, LANES))
        left = jnp.broadcast_to(line[:, 0:1], (channels, LANES))
        if count > 2:
            values = (right, left)
        else:
            values = (jnp.where(col_place == 0, right, left),)
        sums = [jnp.where(lane == base + h, v, t) for v, t in zip(values, sums)]
    for out, total in zip(sides, sums):
        out[0:channels, :] = total
        out[channels:CPAD, :] = jnp.zeros((CPAD - channels, LANES), F32)
    shared_out[0:channels, :] = weight_out[...].astype(F32)
    shared_out[channels : channels + 1, :] = bias_mid[...]
    shared_out[channels + 1 : CPAD, :] = jnp.zeros((CPAD - channels - 1, LANES), F32)
    for s in range(samples):
        steps_out[s : s + 1, :] = jnp.ones((1, LANES), F32) * steps[s].astype(F32)
    for copy in copies[5:]:
        copy.wait()


def blend(target, size):
    twice = 2.0 * target + (1.0 - FACTOR)
    lower = jnp.floor(twice * (1.0 / (2 * FACTOR)))
    fraction = (twice - lower * (2.0 * FACTOR)) * (1.0 / (2 * FACTOR))
    fraction = jnp.where(lower < 0.0, 0.0, fraction)
    return jnp.clip(lower, 0.0, size - 1.0), jnp.clip(lower + 1.0, 0.0, size - 1.0), fraction


def edge_parts(from_left, from_right, own, even):
    return (
        jnp.where(even, from_left, own),
        jnp.where(even, pltpu.roll(from_left, LANES - 1, 1), pltpu.roll(from_right, 1, 1)),
        jnp.where(even, own, from_right),
    )


def own_columns(lines, lane, samples, rows):
    own = jnp.zeros(lane.shape, F32)
    for (s, w), line in lines.items():
        at = 2 * (s * rows + w)
        first = line if at == 0 else pltpu.roll(line, at, 1)
        own = jnp.where(lane == at, first, own)
        own = jnp.where(lane == at + 1, pltpu.roll(line, (at + 2) % LANES, 1), own)
    return own


def shifted_lines(line, turned, lane):
    return (
        pltpu.roll(jnp.where(lane == LANES - 1, turned, line), 1, 1),
        line,
        pltpu.roll(jnp.where(lane == 0, turned, line), LANES - 1, 1),
    )


def stack_taps(lat, mean):
    parts = sum([[lat[i], mean[i]] for i in range(3)], [])
    return jnp.concatenate(parts, axis=0).astype(BF16)


def edge_first(weight, lat, mean, dims):
    col_place = lax.axis_index("col")
    stacked = stack_taps(
        [pltpu.roll(lat, LANES - 2 * i, 1) if i else lat for i in range(3)],
        [pltpu.roll(mean, LANES - 2 * i, 1) if i else mean for i in range(3)],
    )
    hidden = silu_of_half(jnp.dot(weight, stacked, preferred_element_type=F32))
    lane = lane_index(hidden.shape[0])
    side = col_place + lane % 2
    return jnp.where((side > 0) & (side < dims["col"]), hidden, 0.0).astype(BF16)


def store_hidden(hs, at, here, edge, turn, lane):
    turned = pltpu.roll(edge, (LANES - 1 - turn) % LANES, 1)
    left, middle, right = shifted_lines(here, turned, lane)
    hs[0, at] = left
    hs[1, at] = middle
    hs[2, at] = right


def second(own_mid, other_mid, bias, out_weight, lines):
    taps = [(tap_row(i), j) for i in range(3) for j in range(3)]
    weight = jnp.concatenate(
        [
            jnp.concatenate([ref[3 * i + j] for i, j in taps], axis=1)
            for ref in (own_mid, other_mid)
        ],
        axis=0,
    )
    stacked = jnp.concatenate(
        [
            jnp.concatenate([line(i, j) for line in lines], axis=1)
            for i in range(3)
            for j in range(3)
        ],
        axis=0,
    )
    value = jnp.dot(weight, stacked, preferred_element_type=F32)
    middle = silu_of_half(0.5 * value + bias).astype(BF16)
    return jnp.dot(out_weight, middle, preferred_element_type=F32)


def inner_kernel(
    dims,
    weight_mid,
    latent,
    coarse,
    weight_in,
    bias_in,
    weight_noise,
    steps,
    cols_matrix,
    other_mid,
    own_shared,
    other_shared,
    *rest,
):
    sides = rest[: dims["messages"]]
    (
        w1_out,
        lat_out,
        mean_lines,
        edge_lat_out,
        edge_mean_out,
        hs_out,
        bias_out,
        weight_out,
        net_out,
        mean_out,
        coef_out,
        own_mid,
        zl,
        zm,
        w1t,
        ce,
        hs,
        tr,
        ez,
        weight_sem,
    ) = rest[dims["messages"] :]
    fetch_weight = pltpu.make_async_copy(weight_mid, own_mid, weight_sem)
    fetch_weight.start()
    samples = latent.shape[0]
    channels, coarse_rows, local_cols = coarse.shape
    rows = latent.shape[1] // channels
    taps, deep, hidden = weight_in.shape
    half = rows // 2
    lat_rows = 3 * channels
    block = 2 * (lat_rows + 4)
    height = dims["row"] * rows
    row_place = lax.axis_index("row")
    col_place = lax.axis_index("col")
    lane = lane_index(CPAD)
    even = lane % 2 == 0

    w1t[...] = jnp.zeros(w1t.shape, F32)
    bias_terms = three_terms(0.5 * bias_in[...])
    noise_terms = three_terms(0.5 * weight_noise[...])
    for i in range(3):
        for j in range(3):
            tap = 0.5 * weight_in[3 * tap_row(i) + j].astype(F32)
            at = i * block + j * channels
            w1t[at : at + channels, :] = tap[0:channels]
            at += lat_rows + 4
            w1t[at : at + channels, :] = tap[channels:deep]
        at = i * block + lat_rows
        w1t[at : at + 1, :] = bias_terms[i]
        for j in range(3 - i):
            w1t[at + 1 + j : at + 2 + j, :] = noise_terms[i]
    first_weight = w1t[...].T.astype(BF16)
    w1_out[...] = first_weight

    lane_w = (lane // 2) % rows
    used = lane < 2 * samples * rows
    inside = used & (lane_w >= 2)

    def halo(side, ok):
        return jnp.where(inside & ok, pltpu.roll(side, 4, 1), 0.0)

    from_left = halo(sides[0][...], col_place > 0)
    from_right = halo(sides[-1][...], col_place < dims["col"] - 1)
    pad = jnp.zeros((CPAD - channels, LANES), F32)
    lines = {}
    for s in range(samples):
        for w in range(2, rows):
            line = channel_rows(latent, s, tile_row(w, rows), channels, rows)
            lines[s, w] = jnp.concatenate([line, pad], axis=0)
    own = own_columns(lines, lane, samples, rows)
    edge = edge_parts(from_left, from_right, own, even)

    ce[...] = jnp.zeros(ce.shape, F32)
    base = 2 * samples * rows
    for h in range(coarse_rows):
        at = h * CPAD
        ce[at : at + channels, 0:local_cols] = coarse[:, h, :]
        ce[at : at + CPAD, local_cols : local_cols + 1] = sides[0][:, base + h : base + h + 1]
        ce[at : at + CPAD, local_cols + 1 : local_cols + 2] = sides[-1][:, base + h : base + h + 1]
    blended = []
    for w in range(rows + 2):
        row = row_place * rows + tile_row(w, rows)
        first, following, fraction = blend(jnp.full((1, LANES), row.astype(F32)), coarse_rows)
        total = None
        for h in range(coarse_rows):
            weight = jnp.where(first == h, 1.0 - fraction, 0.0)
            weight += jnp.where(following == h, fraction, 0.0)
            if w < 2:
                weight = jnp.where((row >= 0) & (row < height), weight, 0.0)
            term = weight * ce[h * CPAD : (h + 1) * CPAD, :]
            total = term if total is None else total + term
        blended.append(total)
    group = local_cols + 2
    high, mid, low = three_terms(jnp.concatenate(blended, axis=0))
    cells = (high + pltpu.roll(mid, group, 1) + pltpu.roll(low, 2 * group, 1)).astype(BF16)
    cells = cells[:, 0 : cols_matrix.shape[0]]
    spread = jnp.dot(cells, cols_matrix[...], preferred_element_type=F32)

    def mean_line(w, j):
        return spread[w * CPAD : (w + 1) * CPAD, j * LANES : (j + 1) * LANES]

    zero_rows = jnp.zeros((4, LANES), F32)
    for w in range(rows + 2):
        if w >= 2:
            mean_out[w - 2] = mean_line(w, 1)
        if w < rows:
            for j in range(3):
                zm[w, j * channels : (j + 1) * channels, :] = mean_line(w, j)[0:channels]
            zm[w, lat_rows : lat_rows + 4, :] = zero_rows
    for j in range(3):
        at = j * channels
        total = jnp.zeros((CPAD, LANES), F32)
        for w in range(rows):
            total = jnp.where(used & (lane_w == w), mean_line(w, 3 + j), total)
        ez[1, at : at + channels, :] = total[0:channels]
        ez[0, at : at + channels, :] = edge[j][0:channels]
    ez[1, lat_rows : lat_rows + 4, :] = zero_rows

    ones = jnp.ones((1, LANES), F32)
    tails = []
    for s in range(samples):
        step = steps[s : s + 1, :]
        now = noise_level(step)
        ahead = noise_level(step + 1.0)
        tails.append(jnp.concatenate([ones, *three_terms(jnp.log(now) * 0.25)], axis=0))
        variance = now * now + sigma_data * sigma_data
        scale = jnp.sqrt(variance)
        inverse = 1.0 / jnp.sqrt(ahead * ahead + sigma_data * sigma_data)
        coef_out[s] = jnp.concatenate(
            [
                sigma_data * sigma_data / variance * scale,
                sigma_data * now / scale,
                ahead * inverse,
                inverse,
                jnp.zeros((4, LANES), F32),
            ],
            axis=0,
        )
    sample_of = lane_index(4) // (2 * rows)
    edge_tail = tails[0]
    for s in range(1, samples):
        edge_tail = jnp.where(sample_of == s, tails[s], edge_tail)
    ez[0, lat_rows : lat_rows + 4, :] = edge_tail

    for s in range(samples):
        for w in range(2, rows):
            turned = pltpu.roll(edge[1], (LANES - 1 - 2 * (s * rows + w)) % LANES, 1)
            moved = shifted_lines(lines[s, w], turned, lane)
            for j in range(3):
                zl[s, w - 2, j * channels : (j + 1) * channels, :] = moved[j][0:channels]
            zl[s, w - 2, lat_rows : lat_rows + 4, :] = tails[s]
    for s in range(samples):
        for w in range(2):
            lat_out[s, w] = zl[s, w]
    for w in range(4):
        mean_lines[w] = zm[w]
    edge_lat, edge_mean = ez[0], ez[1]
    edge_lat_out[...] = edge_lat
    edge_mean_out[...] = edge_mean

    edge_hidden = edge_first(first_weight, edge_lat, edge_mean, dims)
    lane_h = lane_index(hidden)
    for s in range(samples):
        stacked = jnp.concatenate(
            [
                stack_taps([zl[s, w - 2 + i] for i in range(3)], [zm[w + i] for i in range(3)])
                for w in range(2, half + 2)
            ],
            axis=1,
        )
        value = silu_of_half(jnp.dot(first_weight, stacked, preferred_element_type=F32))
        value = value.astype(BF16)
        for n in range(half):
            here = value[:, n * LANES : (n + 1) * LANES]
            turn = 2 * (s * rows + n + 2)
            store_hidden(hs, s * half + n, here, edge_hidden, turn, lane_h)
    for s in range(samples):
        for n in range(2):
            for j in range(3):
                hs_out[j, 2 * s + n] = hs[j, s * half + n]

    tr[...] = jnp.zeros(tr.shape, F32)
    tr[0:CPAD, 0:LANES] = own_shared[...]
    tr[0:CPAD, LANES:] = other_shared[...]
    bias = 0.5 * tr[...].T[:, channels : channels + 1]
    bias_out[...] = bias
    out_weight = tr[0:CPAD, :].astype(BF16)
    weight_out[...] = out_weight
    fetch_weight.wait()
    net = second(
        own_mid,
        other_mid,
        bias,
        out_weight,
        [
            functools.partial(lambda s, n, i, j: hs[j, s * half + n + i], s, n)
            for s in range(samples)
            for n in range(half - 2)
        ],
    )
    for n in range(samples * (half - 2)):
        net_out[n] = net[:, n * LANES : (n + 1) * LANES]


def outer_kernel(
    dims,
    rows_in,
    own_mid,
    other_mid,
    first_weight,
    lat_in,
    mean_lines,
    edge_lat_in,
    edge_mean_in,
    hs_in,
    bias,
    out_weight,
    net_in,
    *rest,
):
    corners = rest[: dims["messages"]]
    net_out, zl, hs, ez = rest[dims["messages"] :]
    samples = rows_in.shape[0] // 2
    rows = 8
    lat_rows = lat_in.shape[2] - 4
    channels = lat_rows // 3
    half = rows // 2
    height = dims["row"] * rows
    row_place = lax.axis_index("row")
    col_place = lax.axis_index("col")
    lane = lane_index(CPAD)
    even = lane % 2 == 0
    valid = []
    for w in range(2):
        row = row_place * rows + tile_row(w, rows)
        valid.append((row >= 0) & (row < height))
    lines = {}
    for s in range(samples):
        for w in range(2):
            lines[s, w] = jnp.where(valid[w], rows_in[w * samples + s].astype(F32), 0.0)
    lane_w = (lane // 2) % rows
    lane_row = row_place * rows + tile_row(lane_w, rows)
    inside = (lane < 2 * samples * rows) & (lane_w < 2) & (lane_row >= 0) & (lane_row < height)

    def halo(corner, ok):
        return jnp.where(inside & ok, pltpu.roll(corner, LANES - 2 * (rows - 2), 1), 0.0)

    from_left = halo(corners[0][...], col_place > 0)
    from_right = halo(corners[-1][...], col_place < dims["col"] - 1)
    own = own_columns(lines, lane, samples, rows)
    edge = edge_parts(from_left, from_right, own, even)
    for j in range(3):
        at = j * channels
        ez[at : at + channels, :] = edge[j][0:channels] + edge_lat_in[at : at + channels, :]
    ez[lat_rows : lat_rows + 4, :] = edge_lat_in[lat_rows : lat_rows + 4, :]
    for s in range(samples):
        for w in range(2):
            turned = pltpu.roll(edge[1], (LANES - 1 - 2 * (s * rows + w)) % LANES, 1)
            moved = shifted_lines(lines[s, w], turned, lane)
            for j in range(3):
                zl[s, w, j * channels : (j + 1) * channels, :] = moved[j][0:channels]
            zl[s, w, lat_rows : lat_rows + 4, :] = lat_in[s, 0, lat_rows : lat_rows + 4, :]

    weight = first_weight[...]
    edge_hidden = edge_first(weight, ez[...], edge_mean_in[...], dims)
    stacked = []
    for s in range(samples):
        lat = [zl[s, 0], zl[s, 1], lat_in[s, 0], lat_in[s, 1]]
        for w in range(2):
            stacked.append(stack_taps(lat[w : w + 3], [mean_lines[w + i] for i in range(3)]))
    value = jnp.dot(weight, jnp.concatenate(stacked, axis=1), preferred_element_type=F32)
    value = silu_of_half(value)
    lane_h = lane_index(value.shape[0])
    edge_row = ((lane_h // 2) % rows > 0) | valid[1]
    edge_hidden = jnp.where(edge_row, edge_hidden.astype(F32), 0.0).astype(BF16)
    for s in range(samples):
        for w in range(2):
            here = value[:, (2 * s + w) * LANES : (2 * s + w + 1) * LANES]
            if w == 0:
                here = jnp.where(valid[1], here, 0.0)
            store_hidden(
                hs, 2 * s + w, here.astype(BF16), edge_hidden, 2 * (s * rows + w), lane_h
            )

    def line(s, n, i, j):
        return hs[j, 2 * s + n + i] if n + i < 2 else hs_in[j, 2 * s + n + i - 2]

    net = second(
        own_mid,
        other_mid,
        bias[...],
        out_weight[...],
        [functools.partial(line, s, n) for s in range(samples) for n in range(2)],
    )
    rest_lines = half - 2
    for s in range(samples):
        for n in range(2):
            at = 2 * s + n
            net_out[s * half + n] = net[:, at * LANES : (at + 1) * LANES]
        for n in range(rest_lines):
            net_out[s * half + 2 + n] = net_in[s * rest_lines + n]


def finish_kernel(latent, fresh, own_net, other_net, mean, coef, fine, following):
    samples = latent.shape[0]
    rows = mean.shape[0]
    channels = latent.shape[1] // rows
    half = rows // 2
    upper = lax.axis_index("chan") == 0
    for s in range(samples):
        keep, gain, noise, inverse = (coef[s, n : n + 1, :] for n in range(4))
        for y in range(rows):
            place = s * half + (y if y < half else rows - 1 - y)
            own, other = own_net[place], other_net[place]
            net = jnp.where(upper, own, other) if y < half else jnp.where(upper, other, own)
            denoised = keep * channel_rows(latent, s, y, channels, rows) + gain * net[0:channels]
            at = pl.ds(y, channels, stride=rows)
            line = jnp.where(upper, y, rows - 1 - y)
            fine[s, at, :] = mean[line, 0:channels, :] + denoised
            following[s, at, :] = denoised * inverse + noise * channel_rows(
                fresh, s, y, channels, rows
            )


def on_device(
    dims,
    latent,
    fresh_noise,
    step_index,
    coarse,
    weight_in,
    bias_in,
    weight_noise,
    weight_mid,
    bias_mid,
    weight_out,
):
    samples, channels, rows, cols = latent.shape
    taps, hidden, deep = weight_in.shape
    half = rows // 2
    row_count, col_count = dims["row"], dims["col"]
    messages = dims["messages"]
    vmem = pl.BlockSpec(memory_space=pltpu.VMEM)
    struct = jax.ShapeDtypeStruct
    place = functools.partial(pltpu.with_memory_space_constraint, memory_space=pltpu.VMEM)

    far = functools.partial(pltpu.with_memory_space_constraint, memory_space=pltpu.HBM)
    anywhere = pl.BlockSpec(memory_space=pltpu.HBM)

    flat = latent.reshape(samples, channels * rows, cols)
    swap = [(0, 1), (1, 0)]
    other_mid = lax.ppermute(weight_mid, "chan", swap)
    group = coarse.shape[2] + 2
    depth = CPAD * ((3 * group + CPAD - 1) // CPAD)
    packed = pl.pallas_call(
        functools.partial(pack_kernel, dims),
        out_shape=[
            pltpu.VMEM(flat.shape, F32),
            pltpu.VMEM(coarse.shape, F32),
            pltpu.VMEM((taps, deep, hidden), BF16),
            pltpu.VMEM((1, hidden), F32),
            pltpu.VMEM((1, hidden), F32),
            pltpu.VMEM((8, LANES), F32),
            pltpu.VMEM((depth, 6 * LANES), BF16),
            pltpu.VMEM((2 * samples, CPAD, cols), BF16),
            pltpu.VMEM((CPAD, hidden // 2), F32),
        ]
        + [pltpu.VMEM((CPAD, LANES), F32)] * messages,
        in_specs=[anywhere] * 8,
        out_specs=[vmem] * (9 + messages),
        scratch_shapes=[
            pltpu.VMEM(weight_out.shape, BF16),
            pltpu.VMEM((1, hidden // 2), F32),
            pltpu.SMEM((samples,), jnp.int32),
            pltpu.SemaphoreType.DMA((8,)),
        ],
        compiler_params=LIMIT,
        name="pack",
    )(
        far(flat),
        far(coarse),
        far(weight_out),
        far(bias_mid.reshape(1, -1)),
        far(jnp.transpose(weight_in, (0, 2, 1))),
        far(bias_in.reshape(1, -1)),
        far(weight_noise.reshape(1, -1)),
        far(step_index),
    )
    prepared = [place(value) for value in packed[:7]]
    flat_near = prepared[0]
    rows_message, shared, side_messages = packed[7], packed[8], packed[9:]

    down = [(r, 0, r + 1, 0) for r in range(row_count - 1)]
    down += [(r + 1, 1, r, 1) for r in range(row_count - 1)]
    ends = [(row_count - 1, 0, row_count - 1, 1), (0, 1, 0, 0)]
    vertical = [(2 * a + b, 2 * c + d) for a, b, c, d in down + ends]
    sides, corners = [], []
    for n, message in enumerate(side_messages):
        if col_count > 2:
            step = 1 if n == 0 else -1
            columns = [(i, (i + step) % col_count) for i in range(col_count)]
        else:
            columns = [(i, col_count - 1 - i) for i in range(col_count)]
        sides.append(lax.ppermute(message, "col", columns))
        diagonal = [
            (2 * (a * col_count + i) + b, 2 * (c * col_count + k) + d)
            for a, b, c, d in down
            for i, k in columns
        ]
        diagonal += [
            (2 * (a * col_count + i) + b, 2 * (c * col_count + i) + d)
            for a, b, c, d in ends
            for i in range(col_count)
        ]
        corners.append(lax.ppermute(message, ("row", "col", "chan"), diagonal))
    rows_in = lax.ppermute(rows_message, ("row", "chan"), vertical)
    other_shared = lax.ppermute(shared, "chan", swap)

    other_mid = place(other_mid)
    lat_rows = 3 * channels + 4
    inner_lines = samples * (half - 2)
    inner = pl.pallas_call(
        functools.partial(inner_kernel, dims),
        out_shape=[
            pltpu.VMEM((hidden, 6 * lat_rows), BF16),
            pltpu.VMEM((samples, 2, lat_rows, cols), F32),
            pltpu.VMEM((4, lat_rows, cols), F32),
            pltpu.VMEM((lat_rows, cols), F32),
            pltpu.VMEM((lat_rows, cols), F32),
            pltpu.VMEM((3, 2 * samples, hidden, cols), BF16),
            pltpu.VMEM((hidden, 1), F32),
            pltpu.VMEM((CPAD, hidden), BF16),
            pltpu.VMEM((inner_lines, CPAD, cols), F32),
            pltpu.VMEM((rows, CPAD, cols), F32),
            pltpu.VMEM((samples, 8, cols), F32),
            pltpu.VMEM(weight_mid.shape, BF16),
        ],
        in_specs=[anywhere] + [vmem] * (10 + messages),
        out_specs=[vmem] * 12,
        scratch_shapes=[
            pltpu.VMEM((samples, rows - 2, lat_rows, cols), F32),
            pltpu.VMEM((rows, lat_rows, cols), F32),
            pltpu.VMEM((6 * lat_rows, hidden), F32),
            pltpu.VMEM((coarse.shape[1] * CPAD, LANES), F32),
            pltpu.VMEM((3, samples * half, hidden, cols), BF16),
            pltpu.VMEM((LANES, 2 * LANES), F32),
            pltpu.VMEM((2, lat_rows, cols), F32),
            pltpu.SemaphoreType.DMA,
        ],
        compiler_params=LIMIT,
        name="inner",
    )(
        far(weight_mid),
        *prepared,
        other_mid,
        place(shared),
        place(other_shared),
        *[place(side) for side in sides],
    )
    inner = [place(value) for value in inner]
    net = pl.pallas_call(
        functools.partial(outer_kernel, dims),
        out_shape=pltpu.VMEM((samples * half, CPAD, cols), F32),
        in_specs=[vmem] * (12 + messages),
        out_specs=vmem,
        scratch_shapes=[
            pltpu.VMEM((samples, 2, lat_rows, cols), F32),
            pltpu.VMEM((3, 2 * samples, hidden, cols), BF16),
            pltpu.VMEM((lat_rows, cols), F32),
        ],
        compiler_params=LIMIT,
        name="outer",
    )(
        place(rows_in),
        inner[11],
        other_mid,
        *inner[:9],
        *[place(corner) for corner in corners],
    )
    other_net = lax.ppermute(net, "chan", swap)
    results = pl.pallas_call(
        finish_kernel,
        out_shape=[struct(flat.shape, F32)] * 2,
        in_specs=[vmem] * 6,
        out_specs=[vmem] * 2,
        compiler_params=LIMIT,
        name="finish",
    )(
        flat_near,
        place(fresh_noise.reshape(flat.shape)),
        place(net),
        place(other_net),
        inner[9],
        inner[10],
    )
    return tuple(value.reshape(latent.shape) for value in results)


def solution(mesh):
    dims = {axis: mesh.shape[axis] for axis in ("row", "col", "chan")}
    dims["messages"] = 2 if dims["col"] > 2 else 1
    tile = P("ens", None, "row", "col")
    in_specs = (
        tile,
        tile,
        P("ens"),
        P("ens", None, "col"),
        P(),
        P(),
        P(),
        P(None, "chan", None),
        P("chan"),
        P(None, "chan"),
    )
    return jax.shard_map(
        functools.partial(on_device, dims),
        mesh=mesh,
        in_specs=in_specs,
        out_specs=(tile, tile),
        check_vma=False,
    )
```

```python
import functools

import jax
import jax.numpy as jnp
from jax import lax
from jax.experimental import pallas as pl
from jax.experimental.pallas import tpu as pltpu
from jax.sharding import PartitionSpec as P


STEPS = 18
FACTOR = 8

sigma_data = 0.5
sigma_high = 80.0
sigma_low = 0.002
rho_power = 7.0

F32 = jnp.float32
BF16 = jnp.bfloat16
LANES = 128
CPAD = 16
ORDER = (1, 0, 2)
LIMIT = pltpu.CompilerParams(vmem_limit_bytes=12 * 1024 * 1024)


def lane_index(rows):
    return lax.broadcasted_iota(jnp.int32, (rows, LANES), 1)


def tile_row(w, rows):
    return jnp.where(lax.axis_index("chan") == 0, w - 2, rows + 1 - w)


def tap_row(i):
    return jnp.where(lax.axis_index("chan") == 0, i, 2 - i)


def noise_level(position):
    top_root = sigma_high ** (1.0 / rho_power)
    bottom_root = sigma_low ** (1.0 / rho_power)
    root = top_root + position * (1.0 / (STEPS - 1)) * (bottom_root - top_root)
    square = root * root
    return square * square * square * root


def silu_of_half(half):
    return half + half * jnp.tanh(half)


def three_terms(value):
    high = value.astype(BF16).astype(F32)
    rest = value - high
    mid = rest.astype(BF16).astype(F32)
    return high, mid, (rest - mid).astype(BF16).astype(F32)


def channel_rows(ref, s, y, channels, rows):
    return ref[s, pl.ds(y, channels, stride=rows), :]


def pack_kernel(
    dims,
    latent_far,
    coarse_far,
    weight_out_far,
    bias_mid_far,
    weight_in_far,
    bias_in_far,
    weight_noise_far,
    steps_far,
    weight_mid_far,
    latent,
    coarse,
    weight_in,
    bias_in,
    weight_noise,
    steps_out,
    cols_matrix,
    own_mid,
    rows_out,
    shared_out,
    *rest,
):
    sides = rest[: dims["messages"]]
    weight_out, bias_mid, steps, sem = rest[dims["messages"] :]
    pairs = (
        (latent_far, latent),
        (coarse_far, coarse),
        (weight_out_far, weight_out),
        (bias_mid_far, bias_mid),
        (steps_far, steps),
        (weight_in_far, weight_in),
        (bias_in_far, bias_in),
        (weight_noise_far, weight_noise),
        (weight_mid_far, own_mid),
    )
    copies = [pltpu.make_async_copy(a, b, sem.at[n]) for n, (a, b) in enumerate(pairs)]
    for copy in copies:
        copy.start()
    samples = latent.shape[0]
    channels, coarse_rows, local_cols = coarse.shape
    rows = latent.shape[1] // channels
    count = dims["col"]
    col_place = lax.axis_index("col")
    upper = lax.axis_index("chan") == 0

    cols = latent.shape[2]
    width = count * cols
    coarse_cols = count * local_cols
    group = local_cols + 2
    depth = lax.broadcasted_iota(jnp.int32, (cols_matrix.shape[0], LANES), 0)
    spot = depth % group
    index = col_place * local_cols + jnp.where(
        spot < local_cols, spot, jnp.where(spot == local_cols, -1, local_cols)
    )
    index = jnp.where(depth < 3 * group, index, -2).astype(F32)
    wide = lax.broadcasted_iota(jnp.int32, (1, LANES), 1)
    targets = [col_place * cols + wide - 1 + j for j in range(3)]
    targets += [
        col_place * cols + jnp.where(wide % 2 == 0, j - 2, cols - 1 + j) for j in range(3)
    ]
    for n, target in enumerate(targets):
        low, high, fraction = blend(target.astype(F32), coarse_cols)
        outside = (target < 0) | (target >= width)
        low = jnp.where(outside, -3.0, low)
        high = jnp.where(outside, -3.0, high)
        weights = jnp.where(low == index, 1.0 - fraction, 0.0)
        weights += jnp.where(high == index, fraction, 0.0)
        cols_matrix[:, n * LANES : (n + 1) * LANES] = weights.astype(BF16)

    copies[0].wait()
    for near in range(2):
        y = jnp.where(upper, rows - 2 + near, 1 - near)
        for s in range(samples):
            got = channel_rows(latent, s, y, channels, rows).astype(BF16)
            rows_out[near * samples + s, 0:channels, :] = got
            rows_out[near * samples + s, channels:CPAD, :] = jnp.zeros(
                (CPAD - channels, LANES), BF16
            )
    lane = lane_index(channels)
    sums = [jnp.zeros((channels, LANES), F32) for _ in sides]
    if count > 2:
        shifts = (2, 0)
    else:
        shifts = (jnp.where(col_place == 0, 2, 0),)
    for s in range(samples):
        for q in range(rows):
            y = jnp.where(upper, q, rows - 1 - q)
            row = channel_rows(latent, s, y, channels, rows)
            place = 2 * (s * rows + q)
            hit = (lane == place) | (lane == place + 1)
            sums = [
                jnp.where(hit, pltpu.roll(row, place + shift, 1), total)
                for shift, total in zip(shifts, sums)
            ]
    for copy in copies[1:5]:
        copy.wait()
    base = 2 * samples * rows
    for h in range(coarse_rows):
        line = coarse[:, h, :]
        right = jnp.broadcast_to(line[:, local_cols - 1 : local_cols], (channels, LANES))
        left = jnp.broadcast_to(line[:, 0:1], (channels, LANES))
        if count > 2:
            values = (right, left)
        else:
            values = (jnp.where(col_place == 0, right, left),)
        sums = [jnp.where(lane == base + h, v, t) for v, t in zip(values, sums)]
    for out, total in zip(sides, sums):
        out[0:channels, :] = total
        out[channels:CPAD, :] = jnp.zeros((CPAD - channels, LANES), F32)
    shared_out[0:channels, :] = weight_out[...].astype(F32)
    shared_out[channels : channels + 1, :] = bias_mid[...]
    shared_out[channels + 1 : CPAD, :] = jnp.zeros((CPAD - channels - 1, LANES), F32)
    for s in range(samples):
        steps_out[s : s + 1, :] = jnp.ones((1, LANES), F32) * steps[s].astype(F32)
    for copy in copies[5:]:
        copy.wait()


def blend(target, size):
    twice = 2.0 * target + (1.0 - FACTOR)
    lower = jnp.floor(twice * (1.0 / (2 * FACTOR)))
    fraction = (twice - lower * (2.0 * FACTOR)) * (1.0 / (2 * FACTOR))
    fraction = jnp.where(lower < 0.0, 0.0, fraction)
    return jnp.clip(lower, 0.0, size - 1.0), jnp.clip(lower + 1.0, 0.0, size - 1.0), fraction


def edge_parts(from_left, from_right, own, even):
    return (
        jnp.where(even, from_left, own),
        jnp.where(even, pltpu.roll(from_left, LANES - 1, 1), pltpu.roll(from_right, 1, 1)),
        jnp.where(even, own, from_right),
    )


def own_columns(lines, lane, rows):
    own = jnp.zeros(lane.shape, F32)
    for (s, w), line in lines.items():
        at = 2 * (s * rows + w)
        first = line if at == 0 else pltpu.roll(line, at, 1)
        own = jnp.where(lane == at, first, own)
        own = jnp.where(lane == at + 1, pltpu.roll(line, (at + 2) % LANES, 1), own)
    return own


def shifted_lines(line, turned, lane):
    return (
        pltpu.roll(jnp.where(lane == LANES - 1, turned, line), 1, 1),
        line,
        pltpu.roll(jnp.where(lane == 0, turned, line), LANES - 1, 1),
    )


def stack_taps(lat, mean):
    parts = sum([[lat[i], mean[i]] for i in range(3)], [])
    return jnp.concatenate(parts, axis=0).astype(BF16)


def edge_first(weight, lat, mean, dims):
    col_place = lax.axis_index("col")
    stacked = stack_taps(
        [pltpu.roll(lat, LANES - 2 * i, 1) if i else lat for i in range(3)],
        [pltpu.roll(mean, LANES - 2 * i, 1) if i else mean for i in range(3)],
    )
    hidden = silu_of_half(jnp.dot(weight, stacked, preferred_element_type=F32))
    lane = lane_index(hidden.shape[0])
    side = col_place + lane % 2
    return jnp.where((side > 0) & (side < dims["col"]), hidden, 0.0).astype(BF16)


def store_hidden(hs, lines, edge, lane):
    for at, turn, here in lines:
        hs[1, at] = here
    for at, turn, here in lines:
        turned = pltpu.roll(edge, (LANES - 1 - turn) % LANES, 1)
        hs[0, at] = pltpu.roll(jnp.where(lane == LANES - 1, turned, here), 1, 1)
        hs[2, at] = pltpu.roll(jnp.where(lane == 0, turned, here), LANES - 1, 1)


def second(own_mid, other_mid, bias, out_weight, lines):
    taps = [(tap_row(i), j) for j in ORDER for i in range(3)]
    weight = jnp.concatenate(
        [
            jnp.concatenate([ref[3 * i + j] for i, j in taps], axis=1)
            for ref in (own_mid, other_mid)
        ],
        axis=0,
    )
    stacked = jnp.concatenate(
        [
            jnp.concatenate([line(i, j) for line in lines], axis=1)
            for j in ORDER
            for i in range(3)
        ],
        axis=0,
    )
    value = jnp.dot(weight, stacked, preferred_element_type=F32)
    middle = silu_of_half(0.5 * value + bias).astype(BF16)
    return jnp.dot(out_weight, middle, preferred_element_type=F32)


def inner_kernel(
    dims,
    latent,
    coarse,
    weight_in,
    bias_in,
    weight_noise,
    steps,
    cols_matrix,
    own_mid,
    other_mid,
    own_shared,
    other_shared,
    *rest,
):
    sides = rest[: dims["messages"]]
    (
        w1_out,
        lat_out,
        mean_lines,
        edge_lat_out,
        edge_mean_out,
        hs_out,
        bias_out,
        weight_out,
        net_out,
        mean_out,
        coef_out,
        zl,
        zm,
        w1t,
        ce,
        hs,
        tr,
        ez,
    ) = rest[dims["messages"] :]
    samples = latent.shape[0]
    channels, coarse_rows, local_cols = coarse.shape
    rows = latent.shape[1] // channels
    _, deep, hidden = weight_in.shape
    half = rows // 2
    lat_rows = 3 * channels
    block = 2 * (lat_rows + 4)
    height = dims["row"] * rows
    row_place = lax.axis_index("row")
    col_place = lax.axis_index("col")
    lane = lane_index(CPAD)
    even = lane % 2 == 0

    tr[...] = jnp.zeros(tr.shape, F32)
    tr[0:CPAD, 0:LANES] = own_shared[...]
    tr[0:CPAD, LANES:] = other_shared[...]
    bias = 0.5 * tr[...].T[:, channels : channels + 1]
    bias_out[...] = bias
    out_weight = tr[0:CPAD, :].astype(BF16)
    weight_out[...] = out_weight

    w1t[...] = jnp.zeros(w1t.shape, F32)
    bias_terms = three_terms(0.5 * bias_in[...])
    noise_terms = three_terms(0.5 * weight_noise[...])
    for i in range(3):
        for j in range(3):
            tap = 0.5 * weight_in[3 * tap_row(i) + j].astype(F32)
            at = i * block + j * channels
            w1t[at : at + channels, :] = tap[0:channels]
            at += lat_rows + 4
            w1t[at : at + channels, :] = tap[channels:deep]
        at = i * block + lat_rows
        w1t[at : at + 1, :] = bias_terms[i]
        for j in range(3 - i):
            w1t[at + 1 + j : at + 2 + j, :] = noise_terms[i]
    first_weight = w1t[...].T.astype(BF16)
    w1_out[...] = first_weight

    lane_w = (lane // 2) % rows
    used = lane < 2 * samples * rows
    inside = used & (lane_w >= 2)

    def halo(side, ok):
        return jnp.where(inside & ok, pltpu.roll(side, 4, 1), 0.0)

    from_left = halo(sides[0][...], col_place > 0)
    from_right = halo(sides[-1][...], col_place < dims["col"] - 1)
    pad = jnp.zeros((CPAD - channels, LANES), F32)
    lines = {}
    for s in range(samples):
        for w in range(2, rows):
            line = channel_rows(latent, s, tile_row(w, rows), channels, rows)
            lines[s, w] = jnp.concatenate([line, pad], axis=0)
    own = own_columns(lines, lane, rows)
    edge = edge_parts(from_left, from_right, own, even)

    ce[...] = jnp.zeros(ce.shape, F32)
    base = 2 * samples * rows
    for h in range(coarse_rows):
        at = h * CPAD
        ce[at : at + channels, 0:local_cols] = coarse[:, h, :]
        ce[at : at + CPAD, local_cols : local_cols + 1] = sides[0][:, base + h : base + h + 1]
        ce[at : at + CPAD, local_cols + 1 : local_cols + 2] = sides[-1][:, base + h : base + h + 1]
    blended = []
    for w in range(rows + 2):
        row = row_place * rows + tile_row(w, rows)
        first, following, fraction = blend(jnp.full((1, LANES), row.astype(F32)), coarse_rows)
        total = None
        for h in range(coarse_rows):
            weight = jnp.where(first == h, 1.0 - fraction, 0.0)
            weight += jnp.where(following == h, fraction, 0.0)
            if w < 2:
                weight = jnp.where((row >= 0) & (row < height), weight, 0.0)
            term = weight * ce[h * CPAD : (h + 1) * CPAD, :]
            total = term if total is None else total + term
        blended.append(total)
    group = local_cols + 2
    high, mid, low = three_terms(jnp.concatenate(blended, axis=0))
    cells = (high + pltpu.roll(mid, group, 1) + pltpu.roll(low, 2 * group, 1)).astype(BF16)
    cells = cells[:, 0 : cols_matrix.shape[0]]
    spread = jnp.dot(cells, cols_matrix[...], preferred_element_type=F32)

    def mean_line(w, j):
        return spread[w * CPAD : (w + 1) * CPAD, j * LANES : (j + 1) * LANES]

    zero_rows = jnp.zeros((4, LANES), F32)
    for w in range(rows + 2):
        if w >= 2:
            mean_out[w - 2] = mean_line(w, 1)
        if w < rows:
            for j in range(3):
                zm[w, j * channels : (j + 1) * channels, :] = mean_line(w, j)[0:channels]
            zm[w, lat_rows : lat_rows + 4, :] = zero_rows
    for j in range(3):
        at = j * channels
        total = jnp.zeros((CPAD, LANES), F32)
        for w in range(rows):
            total = jnp.where(used & (lane_w == w), mean_line(w, 3 + j), total)
        ez[1, at : at + channels, :] = total[0:channels]
        ez[0, at : at + channels, :] = edge[j][0:channels]
    ez[1, lat_rows : lat_rows + 4, :] = zero_rows

    ones = jnp.ones((1, LANES), F32)
    tails = []
    for s in range(samples):
        step = steps[s : s + 1, :]
        now = noise_level(step)
        ahead = noise_level(step + 1.0)
        tails.append(jnp.concatenate([ones, *three_terms(jnp.log(now) * 0.25)], axis=0))
        variance = now * now + sigma_data * sigma_data
        scale = jnp.sqrt(variance)
        inverse = 1.0 / jnp.sqrt(ahead * ahead + sigma_data * sigma_data)
        coef_out[s] = jnp.concatenate(
            [
                sigma_data * sigma_data / variance * scale,
                sigma_data * now / scale,
                ahead * inverse,
                inverse,
                jnp.zeros((4, LANES), F32),
            ],
            axis=0,
        )
    sample_of = lane_index(4) // (2 * rows)
    edge_tail = tails[0]
    for s in range(1, samples):
        edge_tail = jnp.where(sample_of == s, tails[s], edge_tail)
    ez[0, lat_rows : lat_rows + 4, :] = edge_tail

    for s in range(samples):
        for w in range(2, rows):
            turned = pltpu.roll(edge[1], (LANES - 1 - 2 * (s * rows + w)) % LANES, 1)
            moved = shifted_lines(lines[s, w], turned, lane)
            for j in range(3):
                zl[s, w - 2, j * channels : (j + 1) * channels, :] = moved[j][0:channels]
            zl[s, w - 2, lat_rows : lat_rows + 4, :] = tails[s]
    for s in range(samples):
        for w in range(2):
            lat_out[s, w] = zl[s, w]
    for w in range(4):
        mean_lines[w] = zm[w]
    edge_lat, edge_mean = ez[0], ez[1]
    edge_lat_out[...] = edge_lat
    edge_mean_out[...] = edge_mean

    edge_hidden = edge_first(first_weight, edge_lat, edge_mean, dims)
    lane_h = lane_index(hidden)
    hidden_lines = []
    for s in range(samples):
        stacked = jnp.concatenate(
            [
                stack_taps([zl[s, w - 2 + i] for i in range(3)], [zm[w + i] for i in range(3)])
                for w in range(2, half + 2)
            ],
            axis=1,
        )
        value = silu_of_half(jnp.dot(first_weight, stacked, preferred_element_type=F32))
        value = value.astype(BF16)
        for n in range(half):
            here = value[:, n * LANES : (n + 1) * LANES]
            hidden_lines.append((s * half + n, 2 * (s * rows + n + 2), here))
    store_hidden(hs, hidden_lines, edge_hidden, lane_h)
    for s in range(samples):
        for n in range(2):
            for j in range(3):
                hs_out[j, 2 * s + n] = hs[j, s * half + n]

    net = second(
        own_mid,
        other_mid,
        bias,
        out_weight,
        [
            functools.partial(lambda s, n, i, j: hs[j, s * half + n + i], s, n)
            for s in range(samples)
            for n in range(half - 2)
        ],
    )
    for n in range(samples * (half - 2)):
        net_out[n] = net[:, n * LANES : (n + 1) * LANES]


def outer_kernel(
    dims,
    rows_in,
    own_mid,
    other_mid,
    first_weight,
    lat_in,
    mean_lines,
    edge_lat_in,
    edge_mean_in,
    hs_in,
    bias,
    out_weight,
    net_in,
    *rest,
):
    corners = rest[: dims["messages"]]
    net_out, zl, hs, ez = rest[dims["messages"] :]
    samples = rows_in.shape[0] // 2
    rows = 8
    lat_rows = lat_in.shape[2] - 4
    channels = lat_rows // 3
    half = rows // 2
    height = dims["row"] * rows
    row_place = lax.axis_index("row")
    col_place = lax.axis_index("col")
    lane = lane_index(CPAD)
    even = lane % 2 == 0
    valid = []
    for w in range(2):
        row = row_place * rows + tile_row(w, rows)
        valid.append((row >= 0) & (row < height))
    lines = {}
    for s in range(samples):
        for w in range(2):
            lines[s, w] = jnp.where(valid[w], rows_in[w * samples + s].astype(F32), 0.0)
    lane_w = (lane // 2) % rows
    lane_row = row_place * rows + tile_row(lane_w, rows)
    inside = (lane < 2 * samples * rows) & (lane_w < 2) & (lane_row >= 0) & (lane_row < height)

    def halo(corner, ok):
        return jnp.where(inside & ok, pltpu.roll(corner, LANES - 2 * (rows - 2), 1), 0.0)

    from_left = halo(corners[0][...], col_place > 0)
    from_right = halo(corners[-1][...], col_place < dims["col"] - 1)
    own = own_columns(lines, lane, rows)
    edge = edge_parts(from_left, from_right, own, even)
    for j in range(3):
        at = j * channels
        ez[at : at + channels, :] = edge[j][0:channels] + edge_lat_in[at : at + channels, :]
    ez[lat_rows : lat_rows + 4, :] = edge_lat_in[lat_rows : lat_rows + 4, :]
    for s in range(samples):
        for w in range(2):
            turned = pltpu.roll(edge[1], (LANES - 1 - 2 * (s * rows + w)) % LANES, 1)
            moved = shifted_lines(lines[s, w], turned, lane)
            for j in range(3):
                zl[s, w, j * channels : (j + 1) * channels, :] = moved[j][0:channels]
            zl[s, w, lat_rows : lat_rows + 4, :] = lat_in[s, 0, lat_rows : lat_rows + 4, :]

    weight = first_weight[...]
    edge_hidden = edge_first(weight, ez[...], edge_mean_in[...], dims)
    stacked = []
    for s in range(samples):
        lat = [zl[s, 0], zl[s, 1], lat_in[s, 0], lat_in[s, 1]]
        for w in range(2):
            stacked.append(stack_taps(lat[w : w + 3], [mean_lines[w + i] for i in range(3)]))
    value = jnp.dot(weight, jnp.concatenate(stacked, axis=1), preferred_element_type=F32)
    value = silu_of_half(value)
    lane_h = lane_index(value.shape[0])
    edge_row = ((lane_h // 2) % rows > 0) | valid[1]
    edge_hidden = jnp.where(edge_row, edge_hidden.astype(F32), 0.0).astype(BF16)
    hidden_lines = []
    for s in range(samples):
        for w in range(2):
            here = value[:, (2 * s + w) * LANES : (2 * s + w + 1) * LANES]
            if w == 0:
                here = jnp.where(valid[1], here, 0.0)
            hidden_lines.append((2 * s + w, 2 * (s * rows + w), here.astype(BF16)))
    store_hidden(hs, hidden_lines, edge_hidden, lane_h)

    def line(s, n, i, j):
        return hs[j, 2 * s + n + i] if n + i < 2 else hs_in[j, 2 * s + n + i - 2]

    net = second(
        own_mid,
        other_mid,
        bias[...],
        out_weight[...],
        [functools.partial(line, s, n) for s in range(samples) for n in range(2)],
    )
    rest_lines = half - 2
    for s in range(samples):
        for n in range(2):
            at = 2 * s + n
            net_out[s * half + n] = net[:, at * LANES : (at + 1) * LANES]
        for n in range(rest_lines):
            net_out[s * half + 2 + n] = net_in[s * rest_lines + n]


def finish_kernel(latent, fresh, own_net, other_net, mean, coef, fine, following):
    samples = latent.shape[0]
    rows = mean.shape[0]
    channels = latent.shape[1] // rows
    half = rows // 2
    upper = lax.axis_index("chan") == 0
    for s in range(samples):
        keep, gain, noise, inverse = (coef[s, n : n + 1, :] for n in range(4))
        for y in range(rows):
            place = s * half + (y if y < half else rows - 1 - y)
            own, other = own_net[place], other_net[place]
            net = jnp.where(upper, own, other) if y < half else jnp.where(upper, other, own)
            denoised = keep * channel_rows(latent, s, y, channels, rows) + gain * net[0:channels]
            at = pl.ds(y, channels, stride=rows)
            line = jnp.where(upper, y, rows - 1 - y)
            fine[s, at, :] = mean[line, 0:channels, :] + denoised
            following[s, at, :] = denoised * inverse + noise * channel_rows(
                fresh, s, y, channels, rows
            )


def on_device(
    dims,
    latent,
    fresh_noise,
    step_index,
    coarse,
    weight_in,
    bias_in,
    weight_noise,
    weight_mid,
    bias_mid,
    weight_out,
):
    samples, channels, rows, cols = latent.shape
    taps, hidden, deep = weight_in.shape
    half = rows // 2
    row_count, col_count = dims["row"], dims["col"]
    messages = dims["messages"]
    vmem = pl.BlockSpec(memory_space=pltpu.VMEM)
    struct = jax.ShapeDtypeStruct
    place = functools.partial(pltpu.with_memory_space_constraint, memory_space=pltpu.VMEM)

    far = functools.partial(pltpu.with_memory_space_constraint, memory_space=pltpu.HBM)
    anywhere = pl.BlockSpec(memory_space=pltpu.HBM)

    flat = latent.reshape(samples, channels * rows, cols)
    swap = [(0, 1), (1, 0)]
    other_mid = lax.ppermute(weight_mid, "chan", swap)
    group = coarse.shape[2] + 2
    depth = CPAD * ((3 * group + CPAD - 1) // CPAD)
    packed = pl.pallas_call(
        functools.partial(pack_kernel, dims),
        out_shape=[
            pltpu.VMEM(flat.shape, F32),
            pltpu.VMEM(coarse.shape, F32),
            pltpu.VMEM((taps, deep, hidden), BF16),
            pltpu.VMEM((1, hidden), F32),
            pltpu.VMEM((1, hidden), F32),
            pltpu.VMEM((8, LANES), F32),
            pltpu.VMEM((depth, 6 * LANES), BF16),
            pltpu.VMEM(weight_mid.shape, BF16),
            pltpu.VMEM((2 * samples, CPAD, cols), BF16),
            pltpu.VMEM((CPAD, hidden // 2), F32),
        ]
        + [pltpu.VMEM((CPAD, LANES), F32)] * messages,
        in_specs=[anywhere] * 9,
        out_specs=[vmem] * (10 + messages),
        scratch_shapes=[
            pltpu.VMEM(weight_out.shape, BF16),
            pltpu.VMEM((1, hidden // 2), F32),
            pltpu.SMEM((samples,), jnp.int32),
            pltpu.SemaphoreType.DMA((9,)),
        ],
        compiler_params=LIMIT,
        name="pack",
    )(
        far(flat),
        far(coarse),
        far(weight_out),
        far(bias_mid.reshape(1, -1)),
        far(jnp.transpose(weight_in, (0, 2, 1))),
        far(bias_in.reshape(1, -1)),
        far(weight_noise.reshape(1, -1)),
        far(step_index),
        far(weight_mid),
    )
    prepared = [place(value) for value in packed[:8]]
    flat_near = prepared[0]
    rows_message, shared, side_messages = packed[8], packed[9], packed[10:]

    down = [(r, 0, r + 1, 0) for r in range(row_count - 1)]
    down += [(r + 1, 1, r, 1) for r in range(row_count - 1)]
    ends = [(row_count - 1, 0, row_count - 1, 1), (0, 1, 0, 0)]
    vertical = [(2 * a + b, 2 * c + d) for a, b, c, d in down + ends]
    sides, corners = [], []
    for n, message in enumerate(side_messages):
        if col_count > 2:
            step = 1 if n == 0 else -1
            columns = [(i, (i + step) % col_count) for i in range(col_count)]
        else:
            columns = [(i, col_count - 1 - i) for i in range(col_count)]
        sides.append(lax.ppermute(message, "col", columns))
        diagonal = [
            (2 * (a * col_count + i) + b, 2 * (c * col_count + k) + d)
            for a, b, c, d in down
            for i, k in columns
        ]
        diagonal += [
            (2 * (a * col_count + i) + b, 2 * (c * col_count + i) + d)
            for a, b, c, d in ends
            for i in range(col_count)
        ]
        corners.append(lax.ppermute(message, ("row", "col", "chan"), diagonal))
    rows_in = lax.ppermute(rows_message, ("row", "chan"), vertical)
    other_shared = lax.ppermute(shared, "chan", swap)

    other_mid = place(other_mid)
    lat_rows = 3 * channels + 4
    inner_lines = samples * (half - 2)
    inner = pl.pallas_call(
        functools.partial(inner_kernel, dims),
        out_shape=[
            pltpu.VMEM((hidden, 6 * lat_rows), BF16),
            pltpu.VMEM((samples, 2, lat_rows, cols), F32),
            pltpu.VMEM((4, lat_rows, cols), F32),
            pltpu.VMEM((lat_rows, cols), F32),
            pltpu.VMEM((lat_rows, cols), F32),
            pltpu.VMEM((3, 2 * samples, hidden, cols), BF16),
            pltpu.VMEM((hidden, 1), F32),
            pltpu.VMEM((CPAD, hidden), BF16),
            pltpu.VMEM((inner_lines, CPAD, cols), F32),
            pltpu.VMEM((rows, CPAD, cols), F32),
            pltpu.VMEM((samples, 8, cols), F32),
        ],
        in_specs=[vmem] * (11 + messages),
        out_specs=[vmem] * 11,
        scratch_shapes=[
            pltpu.VMEM((samples, rows - 2, lat_rows, cols), F32),
            pltpu.VMEM((rows, lat_rows, cols), F32),
            pltpu.VMEM((6 * lat_rows, hidden), F32),
            pltpu.VMEM((coarse.shape[1] * CPAD, LANES), F32),
            pltpu.VMEM((3, samples * half, hidden, cols), BF16),
            pltpu.VMEM((LANES, 2 * LANES), F32),
            pltpu.VMEM((2, lat_rows, cols), F32),
        ],
        compiler_params=LIMIT,
        name="inner",
    )(
        *prepared,
        other_mid,
        place(shared),
        place(other_shared),
        *[place(side) for side in sides],
    )
    inner = [place(value) for value in inner]
    net = pl.pallas_call(
        functools.partial(outer_kernel, dims),
        out_shape=pltpu.VMEM((samples * half, CPAD, cols), F32),
        in_specs=[vmem] * (12 + messages),
        out_specs=vmem,
        scratch_shapes=[
            pltpu.VMEM((samples, 2, lat_rows, cols), F32),
            pltpu.VMEM((3, 2 * samples, hidden, cols), BF16),
            pltpu.VMEM((lat_rows, cols), F32),
        ],
        compiler_params=LIMIT,
        name="outer",
    )(
        place(rows_in),
        prepared[7],
        other_mid,
        *inner[:9],
        *[place(corner) for corner in corners],
    )
    other_net = lax.ppermute(net, "chan", swap)
    results = pl.pallas_call(
        finish_kernel,
        out_shape=[struct(flat.shape, F32)] * 2,
        in_specs=[vmem] * 6,
        out_specs=[vmem] * 2,
        compiler_params=LIMIT,
        name="finish",
    )(
        flat_near,
        place(fresh_noise.reshape(flat.shape)),
        place(net),
        place(other_net),
        inner[9],
        inner[10],
    )
    return tuple(value.reshape(latent.shape) for value in results)


def solution(mesh):
    dims = {axis: mesh.shape[axis] for axis in ("row", "col", "chan")}
    dims["messages"] = 2 if dims["col"] > 2 else 1
    tile = P("ens", None, "row", "col")
    in_specs = (
        tile,
        tile,
        P("ens"),
        P("ens", None, "col"),
        P(),
        P(),
        P(),
        P(None, "chan", None),
        P("chan"),
        P(None, "chan"),
    )

    def body(*args):
        return on_device(dims, *args)

    return jax.shard_map(
        body, mesh=mesh, in_specs=in_specs, out_specs=(tile, tile), check_vma=False
    )
```

```python
import functools

import jax
import jax.numpy as jnp
from jax import lax
from jax.experimental import pallas as pl
from jax.experimental.pallas import tpu as pltpu
from jax.sharding import PartitionSpec as P


STEPS = 18
FACTOR = 8

sigma_data = 0.5
sigma_high = 80.0
sigma_low = 0.002
rho_power = 7.0

F32 = jnp.float32
BF16 = jnp.bfloat16
LANES = 128
CPAD = 16
ORDER = (1, 0, 2)
LIMIT = pltpu.CompilerParams(vmem_limit_bytes=12 * 1024 * 1024)


def lane_index(rows):
    return lax.broadcasted_iota(jnp.int32, (rows, LANES), 1)


def tile_row(w, rows):
    return jnp.where(lax.axis_index("chan") == 0, w - 2, rows + 1 - w)


def tap_row(i):
    return jnp.where(lax.axis_index("chan") == 0, i, 2 - i)


def noise_level(position):
    top_root = sigma_high ** (1.0 / rho_power)
    bottom_root = sigma_low ** (1.0 / rho_power)
    root = top_root + position * (1.0 / (STEPS - 1)) * (bottom_root - top_root)
    square = root * root
    return square * square * square * root


def silu_of_half(half):
    return half + half * jnp.tanh(half)


def three_terms(value):
    high = value.astype(BF16).astype(F32)
    rest = value - high
    mid = rest.astype(BF16).astype(F32)
    return high, mid, (rest - mid).astype(BF16).astype(F32)


def channel_rows(ref, s, y, channels, rows):
    return ref[s, pl.ds(y, channels, stride=rows), :]


def pack_kernel(
    dims,
    latent_far,
    coarse_far,
    weight_out_far,
    bias_mid_far,
    weight_in_far,
    bias_in_far,
    weight_noise_far,
    steps_far,
    weight_mid_far,
    latent,
    coarse,
    weight_in,
    bias_in,
    weight_noise,
    steps_out,
    cols_matrix,
    own_mid,
    rows_out,
    shared_out,
    *rest,
):
    sides = rest[: dims["messages"]]
    weight_out, bias_mid, steps, sem = rest[dims["messages"] :]
    samples = latent.shape[0]
    middle = latent.shape[1] // 2
    pairs = [
        (latent_far.at[s, pl.ds(p * middle, middle)], latent.at[s, pl.ds(p * middle, middle)])
        for s in range(samples)
        for p in range(2)
    ]
    first = len(pairs)
    pairs += [
        (coarse_far, coarse),
        (weight_out_far, weight_out),
        (bias_mid_far, bias_mid),
        (steps_far, steps),
        (weight_in_far, weight_in),
        (bias_in_far, bias_in),
        (weight_noise_far, weight_noise),
        (weight_mid_far, own_mid),
    ]
    copies = [pltpu.make_async_copy(a, b, sem.at[n]) for n, (a, b) in enumerate(pairs)]
    for copy in copies:
        copy.start()
    channels, coarse_rows, local_cols = coarse.shape
    rows = latent.shape[1] // channels
    count = dims["col"]
    col_place = lax.axis_index("col")
    upper = lax.axis_index("chan") == 0

    cols = latent.shape[2]
    width = count * cols
    coarse_cols = count * local_cols
    group = local_cols + 2
    depth = lax.broadcasted_iota(jnp.int32, (cols_matrix.shape[0], LANES), 0)
    spot = depth % group
    index = col_place * local_cols + jnp.where(
        spot < local_cols, spot, jnp.where(spot == local_cols, -1, local_cols)
    )
    index = jnp.where(depth < 3 * group, index, -2).astype(F32)
    wide = lax.broadcasted_iota(jnp.int32, (1, LANES), 1)
    targets = [col_place * cols + wide - 1 + j for j in range(3)]
    targets += [
        col_place * cols + jnp.where(wide % 2 == 0, j - 2, cols - 1 + j) for j in range(3)
    ]
    for n, target in enumerate(targets):
        low, high, fraction = blend(target.astype(F32), coarse_cols)
        outside = (target < 0) | (target >= width)
        low = jnp.where(outside, -3.0, low)
        high = jnp.where(outside, -3.0, high)
        weights = jnp.where(low == index, 1.0 - fraction, 0.0)
        weights += jnp.where(high == index, fraction, 0.0)
        cols_matrix[:, n * LANES : (n + 1) * LANES] = weights.astype(BF16)

    for copy in copies[:first]:
        copy.wait()
    for near in range(2):
        y = jnp.where(upper, rows - 2 + near, 1 - near)
        for s in range(samples):
            got = channel_rows(latent, s, y, channels, rows).astype(BF16)
            rows_out[near * samples + s, 0:channels, :] = got
            rows_out[near * samples + s, channels:CPAD, :] = jnp.zeros(
                (CPAD - channels, LANES), BF16
            )
    lane = lane_index(channels)
    sums = [jnp.zeros((channels, LANES), F32) for _ in sides]
    if count > 2:
        shifts = (2, 0)
    else:
        shifts = (jnp.where(col_place == 0, 2, 0),)
    for s in range(samples):
        for q in range(rows):
            y = jnp.where(upper, q, rows - 1 - q)
            row = channel_rows(latent, s, y, channels, rows)
            place = 2 * (s * rows + q)
            hit = (lane == place) | (lane == place + 1)
            sums = [
                jnp.where(hit, pltpu.roll(row, place + shift, 1), total)
                for shift, total in zip(shifts, sums)
            ]
    for copy in copies[first : first + 4]:
        copy.wait()
    base = 2 * samples * rows
    for h in range(coarse_rows):
        line = coarse[:, h, :]
        right = jnp.broadcast_to(line[:, local_cols - 1 : local_cols], (channels, LANES))
        left = jnp.broadcast_to(line[:, 0:1], (channels, LANES))
        if count > 2:
            values = (right, left)
        else:
            values = (jnp.where(col_place == 0, right, left),)
        sums = [jnp.where(lane == base + h, v, t) for v, t in zip(values, sums)]
    for out, total in zip(sides, sums):
        out[0:channels, :] = total
        out[channels:CPAD, :] = jnp.zeros((CPAD - channels, LANES), F32)
    shared_out[0:channels, :] = weight_out[...].astype(F32)
    shared_out[channels : channels + 1, :] = bias_mid[...]
    shared_out[channels + 1 : CPAD, :] = jnp.zeros((CPAD - channels - 1, LANES), F32)
    for s in range(samples):
        steps_out[s : s + 1, :] = jnp.ones((1, LANES), F32) * steps[s].astype(F32)
    for copy in copies[first + 4 :]:
        copy.wait()


def blend(target, size):
    twice = 2.0 * target + (1.0 - FACTOR)
    lower = jnp.floor(twice * (1.0 / (2 * FACTOR)))
    fraction = (twice - lower * (2.0 * FACTOR)) * (1.0 / (2 * FACTOR))
    fraction = jnp.where(lower < 0.0, 0.0, fraction)
    return jnp.clip(lower, 0.0, size - 1.0), jnp.clip(lower + 1.0, 0.0, size - 1.0), fraction


def edge_parts(from_left, from_right, own, even):
    return (
        jnp.where(even, from_left, own),
        jnp.where(even, pltpu.roll(from_left, LANES - 1, 1), pltpu.roll(from_right, 1, 1)),
        jnp.where(even, own, from_right),
    )


def own_columns(lines, lane, rows):
    own = jnp.zeros(lane.shape, F32)
    for (s, w), line in lines.items():
        at = 2 * (s * rows + w)
        first = line if at == 0 else pltpu.roll(line, at, 1)
        own = jnp.where(lane == at, first, own)
        own = jnp.where(lane == at + 1, pltpu.roll(line, (at + 2) % LANES, 1), own)
    return own


def shifted_lines(line, turned, lane):
    return (
        pltpu.roll(jnp.where(lane == LANES - 1, turned, line), 1, 1),
        line,
        pltpu.roll(jnp.where(lane == 0, turned, line), LANES - 1, 1),
    )


def stack_taps(lat, mean):
    parts = sum([[lat[i], mean[i]] for i in range(3)], [])
    return jnp.concatenate(parts, axis=0).astype(BF16)


def edge_first(weight, lat, mean, dims):
    col_place = lax.axis_index("col")
    stacked = stack_taps(
        [pltpu.roll(lat, LANES - 2 * i, 1) if i else lat for i in range(3)],
        [pltpu.roll(mean, LANES - 2 * i, 1) if i else mean for i in range(3)],
    )
    hidden = silu_of_half(jnp.dot(weight, stacked, preferred_element_type=F32))
    lane = lane_index(hidden.shape[0])
    side = col_place + lane % 2
    return jnp.where((side > 0) & (side < dims["col"]), hidden, 0.0).astype(BF16)


def store_hidden(hs, lines, edge, lane):
    for at, turn, here in lines:
        hs[1, at] = here
    for at, turn, here in lines:
        turned = pltpu.roll(edge, (LANES - 1 - turn) % LANES, 1)
        hs[0, at] = pltpu.roll(jnp.where(lane == LANES - 1, turned, here), 1, 1)
        hs[2, at] = pltpu.roll(jnp.where(lane == 0, turned, here), LANES - 1, 1)


def tap_weight(own_mid, other_mid, tap_rows):
    taps = [(tap_row(i), j) for j in ORDER for i in tap_rows]
    return jnp.concatenate(
        [
            jnp.concatenate([ref[3 * i + j] for i, j in taps], axis=1)
            for ref in (own_mid, other_mid)
        ],
        axis=0,
    )


def section(own_mid, other_mid, tap_rows, lines):
    stacked = jnp.concatenate(
        [
            jnp.concatenate([line(i, j) for line in lines], axis=1)
            for j in ORDER
            for i in tap_rows
        ],
        axis=0,
    )
    weight = tap_weight(own_mid, other_mid, tap_rows)
    return jnp.dot(weight, stacked, preferred_element_type=F32)


def project(value, bias, out_weight):
    middle = silu_of_half(0.5 * value + bias).astype(BF16)
    return jnp.dot(out_weight, middle, preferred_element_type=F32)


def inner_kernel(
    dims,
    latent,
    coarse,
    weight_in,
    bias_in,
    weight_noise,
    steps,
    cols_matrix,
    own_mid,
    other_mid,
    own_shared,
    other_shared,
    *rest,
):
    sides = rest[: dims["messages"]]
    (
        w1_out,
        lat_out,
        mean_lines,
        edge_lat_out,
        edge_mean_out,
        hs_out,
        bias_out,
        weight_out,
        net_out,
        mean_out,
        coef_out,
        zl,
        zm,
        w1t,
        ce,
        hs,
        tr,
        ez,
    ) = rest[dims["messages"] :]
    samples = latent.shape[0]
    channels, coarse_rows, local_cols = coarse.shape
    rows = latent.shape[1] // channels
    _, deep, hidden = weight_in.shape
    half = rows // 2
    lat_rows = 3 * channels
    block = 2 * (lat_rows + 4)
    height = dims["row"] * rows
    row_place = lax.axis_index("row")
    col_place = lax.axis_index("col")
    lane = lane_index(CPAD)
    even = lane % 2 == 0

    tr[...] = jnp.zeros(tr.shape, F32)
    tr[0:CPAD, 0:LANES] = own_shared[...]
    tr[0:CPAD, LANES:] = other_shared[...]
    bias = 0.5 * tr[...].T[:, channels : channels + 1]
    bias_out[...] = bias
    out_weight = tr[0:CPAD, :].astype(BF16)
    weight_out[...] = out_weight

    w1t[...] = jnp.zeros(w1t.shape, F32)
    bias_terms = three_terms(0.5 * bias_in[...])
    noise_terms = three_terms(0.5 * weight_noise[...])
    for i in range(3):
        for j in range(3):
            tap = 0.5 * weight_in[3 * tap_row(i) + j].astype(F32)
            at = i * block + j * channels
            w1t[at : at + channels, :] = tap[0:channels]
            at += lat_rows + 4
            w1t[at : at + channels, :] = tap[channels:deep]
        at = i * block + lat_rows
        w1t[at : at + 1, :] = bias_terms[i]
        for j in range(3 - i):
            w1t[at + 1 + j : at + 2 + j, :] = noise_terms[i]
    first_weight = w1t[...].T.astype(BF16)
    w1_out[...] = first_weight

    lane_w = (lane // 2) % rows
    used = lane < 2 * samples * rows
    inside = used & (lane_w >= 2)

    def halo(side, ok):
        return jnp.where(inside & ok, pltpu.roll(side, 4, 1), 0.0)

    from_left = halo(sides[0][...], col_place > 0)
    from_right = halo(sides[-1][...], col_place < dims["col"] - 1)
    pad = jnp.zeros((CPAD - channels, LANES), F32)
    lines = {}
    for s in range(samples):
        for w in range(2, rows):
            line = channel_rows(latent, s, tile_row(w, rows), channels, rows)
            lines[s, w] = jnp.concatenate([line, pad], axis=0)
    own = own_columns(lines, lane, rows)
    edge = edge_parts(from_left, from_right, own, even)

    ce[...] = jnp.zeros(ce.shape, F32)
    base = 2 * samples * rows
    for h in range(coarse_rows):
        at = h * CPAD
        ce[at : at + channels, 0:local_cols] = coarse[:, h, :]
        ce[at : at + CPAD, local_cols : local_cols + 1] = sides[0][:, base + h : base + h + 1]
        ce[at : at + CPAD, local_cols + 1 : local_cols + 2] = sides[-1][:, base + h : base + h + 1]
    blended = []
    for w in range(rows + 2):
        row = row_place * rows + tile_row(w, rows)
        first, following, fraction = blend(jnp.full((1, LANES), row.astype(F32)), coarse_rows)
        total = None
        for h in range(coarse_rows):
            weight = jnp.where(first == h, 1.0 - fraction, 0.0)
            weight += jnp.where(following == h, fraction, 0.0)
            if w < 2:
                weight = jnp.where((row >= 0) & (row < height), weight, 0.0)
            term = weight * ce[h * CPAD : (h + 1) * CPAD, :]
            total = term if total is None else total + term
        blended.append(total)
    group = local_cols + 2
    high, mid, low = three_terms(jnp.concatenate(blended, axis=0))
    cells = (high + pltpu.roll(mid, group, 1) + pltpu.roll(low, 2 * group, 1)).astype(BF16)
    cells = cells[:, 0 : cols_matrix.shape[0]]
    spread = jnp.dot(cells, cols_matrix[...], preferred_element_type=F32)

    def mean_line(w, j):
        return spread[w * CPAD : (w + 1) * CPAD, j * LANES : (j + 1) * LANES]

    zero_rows = jnp.zeros((4, LANES), F32)
    for w in range(rows + 2):
        if w >= 2:
            mean_out[w - 2] = mean_line(w, 1)
        if w < rows:
            for j in range(3):
                zm[w, j * channels : (j + 1) * channels, :] = mean_line(w, j)[0:channels]
            zm[w, lat_rows : lat_rows + 4, :] = zero_rows
    for j in range(3):
        at = j * channels
        total = jnp.zeros((CPAD, LANES), F32)
        for w in range(rows):
            total = jnp.where(used & (lane_w == w), mean_line(w, 3 + j), total)
        ez[1, at : at + channels, :] = total[0:channels]
        ez[0, at : at + channels, :] = edge[j][0:channels]
    ez[1, lat_rows : lat_rows + 4, :] = zero_rows

    ones = jnp.ones((1, LANES), F32)
    tails = []
    for s in range(samples):
        step = steps[s : s + 1, :]
        now = noise_level(step)
        ahead = noise_level(step + 1.0)
        tails.append(jnp.concatenate([ones, *three_terms(jnp.log(now) * 0.25)], axis=0))
        variance = now * now + sigma_data * sigma_data
        scale = jnp.sqrt(variance)
        inverse = 1.0 / jnp.sqrt(ahead * ahead + sigma_data * sigma_data)
        coef_out[s] = jnp.concatenate(
            [
                sigma_data * sigma_data / variance * scale,
                sigma_data * now / scale,
                ahead * inverse,
                inverse,
                jnp.zeros((4, LANES), F32),
            ],
            axis=0,
        )
    sample_of = lane_index(4) // (2 * rows)
    edge_tail = tails[0]
    for s in range(1, samples):
        edge_tail = jnp.where(sample_of == s, tails[s], edge_tail)
    ez[0, lat_rows : lat_rows + 4, :] = edge_tail

    for s in range(samples):
        for w in range(2, rows):
            turned = pltpu.roll(edge[1], (LANES - 1 - 2 * (s * rows + w)) % LANES, 1)
            moved = shifted_lines(lines[s, w], turned, lane)
            for j in range(3):
                zl[s, w - 2, j * channels : (j + 1) * channels, :] = moved[j][0:channels]
            zl[s, w - 2, lat_rows : lat_rows + 4, :] = tails[s]
    for s in range(samples):
        for w in range(2):
            lat_out[s, w] = zl[s, w]
    for w in range(4):
        mean_lines[w] = zm[w]
    edge_lat, edge_mean = ez[0], ez[1]
    edge_lat_out[...] = edge_lat
    edge_mean_out[...] = edge_mean

    edge_hidden = edge_first(first_weight, edge_lat, edge_mean, dims)
    lane_h = lane_index(hidden)
    hidden_lines = []
    for s in range(samples):
        stacked = jnp.concatenate(
            [
                stack_taps([zl[s, w - 2 + i] for i in range(3)], [zm[w + i] for i in range(3)])
                for w in range(2, half + 2)
            ],
            axis=1,
        )
        value = silu_of_half(jnp.dot(first_weight, stacked, preferred_element_type=F32))
        value = value.astype(BF16)
        for n in range(half):
            here = value[:, n * LANES : (n + 1) * LANES]
            hidden_lines.append((s * half + n, 2 * (s * rows + n + 2), here))
    store_hidden(hs, hidden_lines, edge_hidden, lane_h)
    for s in range(samples):
        for n in range(2):
            for j in range(3):
                hs_out[j, 2 * s + n] = hs[j, s * half + n]

    lines = [
        functools.partial(lambda s, n, i, j: hs[j, s * half + n + i], s, n)
        for s in range(samples)
        for n in range(half - 2)
    ]
    net = project(section(own_mid, other_mid, range(3), lines), bias, out_weight)
    for n in range(samples * (half - 2)):
        net_out[n] = net[:, n * LANES : (n + 1) * LANES]


def outer_kernel(
    dims,
    rows_in,
    own_mid,
    other_mid,
    first_weight,
    lat_in,
    mean_lines,
    edge_lat_in,
    edge_mean_in,
    hs_in,
    bias,
    out_weight,
    net_in,
    *rest,
):
    corners = rest[: dims["messages"]]
    net_out, zl, hs, ez, part = rest[dims["messages"] :]
    samples = rows_in.shape[0] // 2
    rows = 8
    lat_rows = lat_in.shape[2] - 4
    channels = lat_rows // 3
    half = rows // 2
    height = dims["row"] * rows
    row_place = lax.axis_index("row")
    col_place = lax.axis_index("col")
    lane = lane_index(CPAD)
    even = lane % 2 == 0

    def known(n, s, i, j):
        return hs_in[j, 2 * s + n + i - 2]

    lower = [functools.partial(known, n, s) for n in range(2) for s in range(samples)]
    early = section(own_mid, other_mid, (2,), lower)
    wide = samples * LANES
    later = early[:, wide:] + section(own_mid, other_mid, (1,), lower[samples:])
    early = jnp.concatenate([early[:, 0:wide], later], axis=1)
    part[...] = early

    valid = []
    for w in range(2):
        row = row_place * rows + tile_row(w, rows)
        valid.append((row >= 0) & (row < height))
    lines = {}
    for s in range(samples):
        for w in range(2):
            lines[s, w] = jnp.where(valid[w], rows_in[w * samples + s].astype(F32), 0.0)
    lane_w = (lane // 2) % rows
    lane_row = row_place * rows + tile_row(lane_w, rows)
    inside = (lane < 2 * samples * rows) & (lane_w < 2) & (lane_row >= 0) & (lane_row < height)

    def halo(corner, ok):
        return jnp.where(inside & ok, pltpu.roll(corner, LANES - 2 * (rows - 2), 1), 0.0)

    from_left = halo(corners[0][...], col_place > 0)
    from_right = halo(corners[-1][...], col_place < dims["col"] - 1)
    own = own_columns(lines, lane, rows)
    edge = edge_parts(from_left, from_right, own, even)
    for j in range(3):
        at = j * channels
        ez[at : at + channels, :] = edge[j][0:channels] + edge_lat_in[at : at + channels, :]
    ez[lat_rows : lat_rows + 4, :] = edge_lat_in[lat_rows : lat_rows + 4, :]
    for s in range(samples):
        for w in range(2):
            turned = pltpu.roll(edge[1], (LANES - 1 - 2 * (s * rows + w)) % LANES, 1)
            moved = shifted_lines(lines[s, w], turned, lane)
            for j in range(3):
                zl[s, w, j * channels : (j + 1) * channels, :] = moved[j][0:channels]
            zl[s, w, lat_rows : lat_rows + 4, :] = lat_in[s, 0, lat_rows : lat_rows + 4, :]

    weight = first_weight[...]
    edge_hidden = edge_first(weight, ez[...], edge_mean_in[...], dims)
    stacked = []
    for s in range(samples):
        lat = [zl[s, 0], zl[s, 1], lat_in[s, 0], lat_in[s, 1]]
        for w in range(2):
            stacked.append(stack_taps(lat[w : w + 3], [mean_lines[w + i] for i in range(3)]))
    value = jnp.dot(weight, jnp.concatenate(stacked, axis=1), preferred_element_type=F32)
    value = silu_of_half(value)
    lane_h = lane_index(value.shape[0])
    edge_row = ((lane_h // 2) % rows > 0) | valid[1]
    edge_hidden = jnp.where(edge_row, edge_hidden.astype(F32), 0.0).astype(BF16)
    hidden_lines = []
    for s in range(samples):
        for w in range(2):
            here = value[:, (2 * s + w) * LANES : (2 * s + w + 1) * LANES]
            if w == 0:
                here = jnp.where(valid[1], here, 0.0)
            hidden_lines.append((2 * s + w, 2 * (s * rows + w), here.astype(BF16)))
    store_hidden(hs, hidden_lines, edge_hidden, lane_h)

    def line(n, s, i, j):
        return hs[j, 2 * s + n + i]

    every = range(samples)
    upper = [functools.partial(line, n, s) for n in range(2) for s in every]
    value = part[...] + section(own_mid, other_mid, (0,), upper)
    first = value[:, 0:wide] + section(own_mid, other_mid, (1,), upper[0:samples])
    value = jnp.concatenate([first, value[:, wide:]], axis=1)
    net = project(value, bias[...], out_weight[...])
    rest_lines = half - 2
    for s in range(samples):
        for n in range(2):
            at = samples * n + s
            net_out[s * half + n] = net[:, at * LANES : (at + 1) * LANES]
        for n in range(rest_lines):
            net_out[s * half + 2 + n] = net_in[s * rest_lines + n]


def finish_kernel(latent, fresh, own_net, other_net, mean, coef, fine, following):
    samples = latent.shape[0]
    rows = mean.shape[0]
    channels = latent.shape[1] // rows
    half = rows // 2
    upper = lax.axis_index("chan") == 0
    for s in range(samples):
        keep, gain, noise, inverse = (coef[s, n : n + 1, :] for n in range(4))
        for y in range(rows):
            place = s * half + (y if y < half else rows - 1 - y)
            own, other = own_net[place], other_net[place]
            net = jnp.where(upper, own, other) if y < half else jnp.where(upper, other, own)
            denoised = keep * channel_rows(latent, s, y, channels, rows) + gain * net[0:channels]
            at = pl.ds(y, channels, stride=rows)
            line = jnp.where(upper, y, rows - 1 - y)
            fine[s, at, :] = mean[line, 0:channels, :] + denoised
            following[s, at, :] = denoised * inverse + noise * channel_rows(
                fresh, s, y, channels, rows
            )


def on_device(
    dims,
    latent,
    fresh_noise,
    step_index,
    coarse,
    weight_in,
    bias_in,
    weight_noise,
    weight_mid,
    bias_mid,
    weight_out,
):
    samples, channels, rows, cols = latent.shape
    taps, hidden, deep = weight_in.shape
    half = rows // 2
    row_count, col_count = dims["row"], dims["col"]
    messages = dims["messages"]
    vmem = pl.BlockSpec(memory_space=pltpu.VMEM)
    struct = jax.ShapeDtypeStruct
    place = functools.partial(pltpu.with_memory_space_constraint, memory_space=pltpu.VMEM)

    far = functools.partial(pltpu.with_memory_space_constraint, memory_space=pltpu.HBM)
    anywhere = pl.BlockSpec(memory_space=pltpu.HBM)

    flat = latent.reshape(samples, channels * rows, cols)
    swap = [(0, 1), (1, 0)]
    other_mid = lax.ppermute(weight_mid, "chan", swap)
    group = coarse.shape[2] + 2
    depth = CPAD * ((3 * group + CPAD - 1) // CPAD)
    packed = pl.pallas_call(
        functools.partial(pack_kernel, dims),
        out_shape=[
            pltpu.VMEM(flat.shape, F32),
            pltpu.VMEM(coarse.shape, F32),
            pltpu.VMEM((taps, deep, hidden), BF16),
            pltpu.VMEM((1, hidden), F32),
            pltpu.VMEM((1, hidden), F32),
            pltpu.VMEM((8, LANES), F32),
            pltpu.VMEM((depth, 6 * LANES), BF16),
            pltpu.VMEM(weight_mid.shape, BF16),
            pltpu.VMEM((2 * samples, CPAD, cols), BF16),
            pltpu.VMEM((CPAD, hidden // 2), F32),
        ]
        + [pltpu.VMEM((CPAD, LANES), F32)] * messages,
        in_specs=[anywhere] * 9,
        out_specs=[vmem] * (10 + messages),
        scratch_shapes=[
            pltpu.VMEM(weight_out.shape, BF16),
            pltpu.VMEM((1, hidden // 2), F32),
            pltpu.SMEM((samples,), jnp.int32),
            pltpu.SemaphoreType.DMA((8 + 2 * samples,)),
        ],
        compiler_params=LIMIT,
        name="pack",
    )(
        far(flat),
        far(coarse),
        far(weight_out),
        far(bias_mid.reshape(1, -1)),
        far(jnp.transpose(weight_in, (0, 2, 1))),
        far(bias_in.reshape(1, -1)),
        far(weight_noise.reshape(1, -1)),
        far(step_index),
        far(weight_mid),
    )
    prepared = [place(value) for value in packed[:8]]
    flat_near = prepared[0]
    rows_message, shared, side_messages = packed[8], packed[9], packed[10:]

    down = [(r, 0, r + 1, 0) for r in range(row_count - 1)]
    down += [(r + 1, 1, r, 1) for r in range(row_count - 1)]
    ends = [(row_count - 1, 0, row_count - 1, 1), (0, 1, 0, 0)]
    vertical = [(2 * a + b, 2 * c + d) for a, b, c, d in down + ends]
    sides, corners = [], []
    for n, message in enumerate(side_messages):
        if col_count > 2:
            step = 1 if n == 0 else -1
            columns = [(i, (i + step) % col_count) for i in range(col_count)]
        else:
            columns = [(i, col_count - 1 - i) for i in range(col_count)]
        sides.append(lax.ppermute(message, "col", columns))
        diagonal = [
            (2 * (a * col_count + i) + b, 2 * (c * col_count + k) + d)
            for a, b, c, d in down
            for i, k in columns
        ]
        diagonal += [
            (2 * (a * col_count + i) + b, 2 * (c * col_count + i) + d)
            for a, b, c, d in ends
            for i in range(col_count)
        ]
        corners.append(lax.ppermute(message, ("row", "col", "chan"), diagonal))
    rows_in = lax.ppermute(rows_message, ("row", "chan"), vertical)
    other_shared = lax.ppermute(shared, "chan", swap)

    other_mid = place(other_mid)
    lat_rows = 3 * channels + 4
    inner_lines = samples * (half - 2)
    inner = pl.pallas_call(
        functools.partial(inner_kernel, dims),
        out_shape=[
            pltpu.VMEM((hidden, 6 * lat_rows), BF16),
            pltpu.VMEM((samples, 2, lat_rows, cols), F32),
            pltpu.VMEM((4, lat_rows, cols), F32),
            pltpu.VMEM((lat_rows, cols), F32),
            pltpu.VMEM((lat_rows, cols), F32),
            pltpu.VMEM((3, 2 * samples, hidden, cols), BF16),
            pltpu.VMEM((hidden, 1), F32),
            pltpu.VMEM((CPAD, hidden), BF16),
            pltpu.VMEM((inner_lines, CPAD, cols), F32),
            pltpu.VMEM((rows, CPAD, cols), F32),
            pltpu.VMEM((samples, 8, cols), F32),
        ],
        in_specs=[vmem] * (11 + messages),
        out_specs=[vmem] * 11,
        scratch_shapes=[
            pltpu.VMEM((samples, rows - 2, lat_rows, cols), F32),
            pltpu.VMEM((rows, lat_rows, cols), F32),
            pltpu.VMEM((6 * lat_rows, hidden), F32),
            pltpu.VMEM((coarse.shape[1] * CPAD, LANES), F32),
            pltpu.VMEM((3, samples * half, hidden, cols), BF16),
            pltpu.VMEM((LANES, 2 * LANES), F32),
            pltpu.VMEM((2, lat_rows, cols), F32),
        ],
        compiler_params=LIMIT,
        name="inner",
    )(
        *prepared,
        other_mid,
        place(shared),
        place(other_shared),
        *[place(side) for side in sides],
    )
    inner = [place(value) for value in inner]
    net = pl.pallas_call(
        functools.partial(outer_kernel, dims),
        out_shape=pltpu.VMEM((samples * half, CPAD, cols), F32),
        in_specs=[vmem] * (12 + messages),
        out_specs=vmem,
        scratch_shapes=[
            pltpu.VMEM((samples, 2, lat_rows, cols), F32),
            pltpu.VMEM((3, 2 * samples, hidden, cols), BF16),
            pltpu.VMEM((lat_rows, cols), F32),
            pltpu.VMEM((hidden, 2 * samples * cols), F32),
        ],
        compiler_params=LIMIT,
        name="outer",
    )(
        place(rows_in),
        prepared[7],
        other_mid,
        *inner[:9],
        *[place(corner) for corner in corners],
    )
    other_net = lax.ppermute(net, "chan", swap)
    results = pl.pallas_call(
        finish_kernel,
        out_shape=[struct(flat.shape, F32)] * 2,
        in_specs=[vmem] * 6,
        out_specs=[vmem] * 2,
        compiler_params=LIMIT,
        name="finish",
    )(
        flat_near,
        place(fresh_noise.reshape(flat.shape)),
        place(net),
        place(other_net),
        inner[9],
        inner[10],
    )
    return tuple(value.reshape(latent.shape) for value in results)


def solution(mesh):
    dims = {axis: mesh.shape[axis] for axis in ("row", "col", "chan")}
    dims["messages"] = 2 if dims["col"] > 2 else 1
    tile = P("ens", None, "row", "col")
    in_specs = (
        tile,
        tile,
        P("ens"),
        P("ens", None, "col"),
        P(),
        P(),
        P(),
        P(None, "chan", None),
        P("chan"),
        P(None, "chan"),
    )

    def body(*args):
        return on_device(dims, *args)

    return jax.shard_map(
        body, mesh=mesh, in_specs=in_specs, out_specs=(tile, tile), check_vma=False
    )
```

```python
import functools

import jax
import jax.numpy as jnp
from jax import lax
from jax.experimental import pallas as pl
from jax.experimental.pallas import tpu as pltpu
from jax.sharding import PartitionSpec as P


STEPS = 18
FACTOR = 8

sigma_data = 0.5
sigma_high = 80.0
sigma_low = 0.002
rho_power = 7.0

F32 = jnp.float32
BF16 = jnp.bfloat16
LANES = 128
CPAD = 16
ORDER = (1, 0, 2)
LIMIT = pltpu.CompilerParams(vmem_limit_bytes=12 * 1024 * 1024)


def lane_index(rows):
    return lax.broadcasted_iota(jnp.int32, (rows, LANES), 1)


def tile_row(w, rows):
    return jnp.where(lax.axis_index("chan") == 0, w - 2, rows + 1 - w)


def tap_row(i):
    return jnp.where(lax.axis_index("chan") == 0, i, 2 - i)


def noise_level(position):
    top_root = sigma_high ** (1.0 / rho_power)
    bottom_root = sigma_low ** (1.0 / rho_power)
    root = top_root + position * (1.0 / (STEPS - 1)) * (bottom_root - top_root)
    square = root * root
    return square * square * square * root


def silu_of_half(half):
    return half + half * jnp.tanh(half)


def three_terms(value):
    high = value.astype(BF16).astype(F32)
    rest = value - high
    mid = rest.astype(BF16).astype(F32)
    return high, mid, (rest - mid).astype(BF16).astype(F32)


def channel_rows(ref, s, y, channels, rows):
    return ref[s, pl.ds(y, channels, stride=rows), :]


def pack_kernel(
    dims,
    latent_far,
    coarse_far,
    weight_out_far,
    bias_mid_far,
    weight_in_far,
    bias_in_far,
    weight_noise_far,
    steps_far,
    weight_mid_far,
    latent,
    coarse,
    weight_in,
    bias_in,
    weight_noise,
    steps_out,
    cols_matrix,
    own_mid,
    rows_out,
    shared_out,
    *rest,
):
    sides = rest[: dims["messages"]]
    weight_out, bias_mid, steps, sem = rest[dims["messages"] :]
    samples = latent.shape[0]
    middle = latent.shape[1] // 2
    pairs = [
        (latent_far.at[s, pl.ds(p * middle, middle)], latent.at[s, pl.ds(p * middle, middle)])
        for s in range(samples)
        for p in range(2)
    ]
    first = len(pairs)
    pairs += [
        (coarse_far, coarse),
        (weight_out_far, weight_out),
        (bias_mid_far, bias_mid),
        (steps_far, steps),
        (weight_in_far, weight_in),
        (bias_in_far, bias_in),
        (weight_noise_far, weight_noise),
        (weight_mid_far, own_mid),
    ]
    copies = [pltpu.make_async_copy(a, b, sem.at[n]) for n, (a, b) in enumerate(pairs)]
    for copy in copies:
        copy.start()
    channels, coarse_rows, local_cols = coarse.shape
    rows = latent.shape[1] // channels
    count = dims["col"]
    col_place = lax.axis_index("col")
    upper = lax.axis_index("chan") == 0

    cols = latent.shape[2]
    width = count * cols
    coarse_cols = count * local_cols
    group = local_cols + 2
    depth = lax.broadcasted_iota(jnp.int32, (cols_matrix.shape[0], LANES), 0)
    spot = depth % group
    index = col_place * local_cols + jnp.where(
        spot < local_cols, spot, jnp.where(spot == local_cols, -1, local_cols)
    )
    index = jnp.where(depth < 3 * group, index, -2).astype(F32)
    wide = lax.broadcasted_iota(jnp.int32, (1, LANES), 1)
    targets = [col_place * cols + wide - 1 + j for j in range(3)]
    targets += [
        col_place * cols + jnp.where(wide % 2 == 0, j - 2, cols - 1 + j) for j in range(3)
    ]
    for n, target in enumerate(targets):
        low, high, fraction = blend(target.astype(F32), coarse_cols)
        outside = (target < 0) | (target >= width)
        low = jnp.where(outside, -3.0, low)
        high = jnp.where(outside, -3.0, high)
        weights = jnp.where(low == index, 1.0 - fraction, 0.0)
        weights += jnp.where(high == index, fraction, 0.0)
        cols_matrix[:, n * LANES : (n + 1) * LANES] = weights.astype(BF16)

    for copy in copies[:first]:
        copy.wait()
    for near in range(2):
        y = jnp.where(upper, rows - 2 + near, 1 - near)
        for s in range(samples):
            got = channel_rows(latent, s, y, channels, rows).astype(BF16)
            rows_out[near * samples + s, 0:channels, :] = got
            rows_out[near * samples + s, channels:CPAD, :] = jnp.zeros(
                (CPAD - channels, LANES), BF16
            )
    lane = lane_index(channels)
    sums = [jnp.zeros((channels, LANES), F32) for _ in sides]
    if count > 2:
        shifts = (2, 0)
    else:
        shifts = (jnp.where(col_place == 0, 2, 0),)
    for s in range(samples):
        for q in range(rows):
            y = jnp.where(upper, q, rows - 1 - q)
            row = channel_rows(latent, s, y, channels, rows)
            place = 2 * (s * rows + q)
            hit = (lane == place) | (lane == place + 1)
            sums = [
                jnp.where(hit, pltpu.roll(row, place + shift, 1), total)
                for shift, total in zip(shifts, sums)
            ]
    for copy in copies[first : first + 4]:
        copy.wait()
    base = 2 * samples * rows
    for h in range(coarse_rows):
        line = coarse[:, h, :]
        right = jnp.broadcast_to(line[:, local_cols - 1 : local_cols], (channels, LANES))
        left = jnp.broadcast_to(line[:, 0:1], (channels, LANES))
        if count > 2:
            values = (right, left)
        else:
            values = (jnp.where(col_place == 0, right, left),)
        sums = [jnp.where(lane == base + h, v, t) for v, t in zip(values, sums)]
    for out, total in zip(sides, sums):
        out[0:channels, :] = total
        out[channels:CPAD, :] = jnp.zeros((CPAD - channels, LANES), F32)
    shared_out[0:channels, :] = weight_out[...].astype(F32)
    shared_out[channels : channels + 1, :] = bias_mid[...]
    shared_out[channels + 1 : CPAD, :] = jnp.zeros((CPAD - channels - 1, LANES), F32)
    for s in range(samples):
        steps_out[s : s + 1, :] = jnp.ones((1, LANES), F32) * steps[s].astype(F32)
    for copy in copies[first + 4 :]:
        copy.wait()


def blend(target, size):
    twice = 2.0 * target + (1.0 - FACTOR)
    lower = jnp.floor(twice * (1.0 / (2 * FACTOR)))
    fraction = (twice - lower * (2.0 * FACTOR)) * (1.0 / (2 * FACTOR))
    fraction = jnp.where(lower < 0.0, 0.0, fraction)
    return jnp.clip(lower, 0.0, size - 1.0), jnp.clip(lower + 1.0, 0.0, size - 1.0), fraction


def edge_parts(from_left, from_right, own, even):
    return (
        jnp.where(even, from_left, own),
        jnp.where(even, pltpu.roll(from_left, LANES - 1, 1), pltpu.roll(from_right, 1, 1)),
        jnp.where(even, own, from_right),
    )


def own_columns(lines, lane, rows):
    own = jnp.zeros(lane.shape, F32)
    for (s, w), line in lines.items():
        at = 2 * (s * rows + w)
        first = line if at == 0 else pltpu.roll(line, at, 1)
        own = jnp.where(lane == at, first, own)
        own = jnp.where(lane == at + 1, pltpu.roll(line, (at + 2) % LANES, 1), own)
    return own


def shifted_lines(line, turned, lane):
    return (
        pltpu.roll(jnp.where(lane == LANES - 1, turned, line), 1, 1),
        line,
        pltpu.roll(jnp.where(lane == 0, turned, line), LANES - 1, 1),
    )


def stack_taps(lat, mean):
    parts = sum([[lat[i], mean[i]] for i in range(3)], [])
    return jnp.concatenate(parts, axis=0).astype(BF16)


def edge_first(weight, lat, mean, dims):
    col_place = lax.axis_index("col")
    stacked = stack_taps(
        [pltpu.roll(lat, LANES - 2 * i, 1) if i else lat for i in range(3)],
        [pltpu.roll(mean, LANES - 2 * i, 1) if i else mean for i in range(3)],
    )
    hidden = silu_of_half(jnp.dot(weight, stacked, preferred_element_type=F32))
    lane = lane_index(hidden.shape[0])
    side = col_place + lane % 2
    return jnp.where((side > 0) & (side < dims["col"]), hidden, 0.0).astype(BF16)


def store_hidden(hs, lines, edge, lane):
    for at, turn, here in lines:
        hs[1, at] = here
    for at, turn, here in lines:
        turned = pltpu.roll(edge, (LANES - 1 - turn) % LANES, 1)
        hs[0, at] = pltpu.roll(jnp.where(lane == LANES - 1, turned, here), 1, 1)
        hs[2, at] = pltpu.roll(jnp.where(lane == 0, turned, here), LANES - 1, 1)


def tap_weight(own_mid, other_mid, tap_rows):
    taps = [(tap_row(i), j) for j in ORDER for i in tap_rows]
    return jnp.concatenate(
        [
            jnp.concatenate([ref[3 * i + j] for i, j in taps], axis=1)
            for ref in (own_mid, other_mid)
        ],
        axis=0,
    )


def section(own_mid, other_mid, tap_rows, lines):
    stacked = jnp.concatenate(
        [
            jnp.concatenate([line(i, j) for line in lines], axis=1)
            for j in ORDER
            for i in tap_rows
        ],
        axis=0,
    )
    weight = tap_weight(own_mid, other_mid, tap_rows)
    return jnp.dot(weight, stacked, preferred_element_type=F32)


def project(value, bias, out_weight):
    middle = silu_of_half(0.5 * value + bias).astype(BF16)
    return jnp.dot(out_weight, middle, preferred_element_type=F32)


def inner_kernel(
    dims,
    latent,
    coarse,
    weight_in,
    bias_in,
    weight_noise,
    steps,
    cols_matrix,
    own_mid,
    other_mid,
    own_shared,
    other_shared,
    *rest,
):
    sides = rest[: dims["messages"]]
    (
        w1_out,
        lat_out,
        mean_lines,
        edge_lat_out,
        edge_mean_out,
        hs,
        bias_out,
        weight_out,
        net_out,
        mean_out,
        coef_out,
        zl,
        zm,
        w1t,
        ce,
        tr,
        ez,
    ) = rest[dims["messages"] :]
    samples = latent.shape[0]
    channels, coarse_rows, local_cols = coarse.shape
    rows = latent.shape[1] // channels
    _, deep, hidden = weight_in.shape
    half = rows // 2
    lat_rows = 3 * channels
    block = 2 * (lat_rows + 4)
    height = dims["row"] * rows
    row_place = lax.axis_index("row")
    col_place = lax.axis_index("col")
    lane = lane_index(CPAD)
    even = lane % 2 == 0

    tr[...] = jnp.zeros(tr.shape, F32)
    tr[0:CPAD, 0:LANES] = own_shared[...]
    tr[0:CPAD, LANES:] = other_shared[...]
    bias = 0.5 * tr[...].T[:, channels : channels + 1]
    bias_out[...] = bias
    out_weight = tr[0:CPAD, :].astype(BF16)
    weight_out[...] = out_weight

    w1t[...] = jnp.zeros(w1t.shape, F32)
    bias_terms = three_terms(0.5 * bias_in[...])
    noise_terms = three_terms(0.5 * weight_noise[...])
    for i in range(3):
        for j in range(3):
            tap = 0.5 * weight_in[3 * tap_row(i) + j].astype(F32)
            at = i * block + j * channels
            w1t[at : at + channels, :] = tap[0:channels]
            at += lat_rows + 4
            w1t[at : at + channels, :] = tap[channels:deep]
        at = i * block + lat_rows
        w1t[at : at + 1, :] = bias_terms[i]
        for j in range(3 - i):
            w1t[at + 1 + j : at + 2 + j, :] = noise_terms[i]
    first_weight = w1t[...].T.astype(BF16)
    w1_out[...] = first_weight

    lane_w = (lane // 2) % rows
    used = lane < 2 * samples * rows
    inside = used & (lane_w >= 2)

    def halo(side, ok):
        return jnp.where(inside & ok, pltpu.roll(side, 4, 1), 0.0)

    from_left = halo(sides[0][...], col_place > 0)
    from_right = halo(sides[-1][...], col_place < dims["col"] - 1)
    pad = jnp.zeros((CPAD - channels, LANES), F32)
    lines = {}
    for s in range(samples):
        for w in range(2, rows):
            line = channel_rows(latent, s, tile_row(w, rows), channels, rows)
            lines[s, w] = jnp.concatenate([line, pad], axis=0)
    own = own_columns(lines, lane, rows)
    edge = edge_parts(from_left, from_right, own, even)

    ce[...] = jnp.zeros(ce.shape, F32)
    base = 2 * samples * rows
    for h in range(coarse_rows):
        at = h * CPAD
        ce[at : at + channels, 0:local_cols] = coarse[:, h, :]
        ce[at : at + CPAD, local_cols : local_cols + 1] = sides[0][:, base + h : base + h + 1]
        ce[at : at + CPAD, local_cols + 1 : local_cols + 2] = sides[-1][:, base + h : base + h + 1]
    blended = []
    for w in range(rows + 2):
        row = row_place * rows + tile_row(w, rows)
        first, following, fraction = blend(jnp.full((1, LANES), row.astype(F32)), coarse_rows)
        total = None
        for h in range(coarse_rows):
            weight = jnp.where(first == h, 1.0 - fraction, 0.0)
            weight += jnp.where(following == h, fraction, 0.0)
            if w < 2:
                weight = jnp.where((row >= 0) & (row < height), weight, 0.0)
            term = weight * ce[h * CPAD : (h + 1) * CPAD, :]
            total = term if total is None else total + term
        blended.append(total)
    group = local_cols + 2
    high, mid, low = three_terms(jnp.concatenate(blended, axis=0))
    cells = (high + pltpu.roll(mid, group, 1) + pltpu.roll(low, 2 * group, 1)).astype(BF16)
    cells = cells[:, 0 : cols_matrix.shape[0]]
    spread = jnp.dot(cells, cols_matrix[...], preferred_element_type=F32)

    def mean_line(w, j):
        return spread[w * CPAD : (w + 1) * CPAD, j * LANES : (j + 1) * LANES]

    zero_rows = jnp.zeros((4, LANES), F32)
    for w in range(rows + 2):
        if w >= 2:
            mean_out[w - 2] = mean_line(w, 1)
        if w < rows:
            for j in range(3):
                zm[w, j * channels : (j + 1) * channels, :] = mean_line(w, j)[0:channels]
            zm[w, lat_rows : lat_rows + 4, :] = zero_rows
    for j in range(3):
        at = j * channels
        total = jnp.zeros((CPAD, LANES), F32)
        for w in range(rows):
            total = jnp.where(used & (lane_w == w), mean_line(w, 3 + j), total)
        ez[1, at : at + channels, :] = total[0:channels]
        ez[0, at : at + channels, :] = edge[j][0:channels]
    ez[1, lat_rows : lat_rows + 4, :] = zero_rows

    ones = jnp.ones((1, LANES), F32)
    tails = []
    for s in range(samples):
        step = steps[s : s + 1, :]
        now = noise_level(step)
        ahead = noise_level(step + 1.0)
        tails.append(jnp.concatenate([ones, *three_terms(jnp.log(now) * 0.25)], axis=0))
        variance = now * now + sigma_data * sigma_data
        scale = jnp.sqrt(variance)
        inverse = 1.0 / jnp.sqrt(ahead * ahead + sigma_data * sigma_data)
        coef_out[s] = jnp.concatenate(
            [
                sigma_data * sigma_data / variance * scale,
                sigma_data * now / scale,
                ahead * inverse,
                inverse,
                jnp.zeros((4, LANES), F32),
            ],
            axis=0,
        )
    sample_of = lane_index(4) // (2 * rows)
    edge_tail = tails[0]
    for s in range(1, samples):
        edge_tail = jnp.where(sample_of == s, tails[s], edge_tail)
    ez[0, lat_rows : lat_rows + 4, :] = edge_tail

    for s in range(samples):
        for w in range(2, rows):
            turned = pltpu.roll(edge[1], (LANES - 1 - 2 * (s * rows + w)) % LANES, 1)
            moved = shifted_lines(lines[s, w], turned, lane)
            for j in range(3):
                zl[s, w - 2, j * channels : (j + 1) * channels, :] = moved[j][0:channels]
            zl[s, w - 2, lat_rows : lat_rows + 4, :] = tails[s]
    for s in range(samples):
        for w in range(2):
            lat_out[s, w] = zl[s, w]
    for w in range(4):
        mean_lines[w] = zm[w]
    edge_lat, edge_mean = ez[0], ez[1]
    edge_lat_out[...] = edge_lat
    edge_mean_out[...] = edge_mean

    edge_hidden = edge_first(first_weight, edge_lat, edge_mean, dims)
    lane_h = lane_index(hidden)
    hidden_lines = []
    for s in range(samples):
        stacked = jnp.concatenate(
            [
                stack_taps([zl[s, w - 2 + i] for i in range(3)], [zm[w + i] for i in range(3)])
                for w in range(2, half + 2)
            ],
            axis=1,
        )
        value = silu_of_half(jnp.dot(first_weight, stacked, preferred_element_type=F32))
        value = value.astype(BF16)
        for n in range(half):
            here = value[:, n * LANES : (n + 1) * LANES]
            hidden_lines.append((s * half + n, 2 * (s * rows + n + 2), here))
    store_hidden(hs, hidden_lines, edge_hidden, lane_h)

    lines = [
        functools.partial(lambda s, n, i, j: hs[j, s * half + n + i], s, n)
        for s in range(samples)
        for n in range(half - 2)
    ]
    net = project(section(own_mid, other_mid, range(3), lines), bias, out_weight)
    for n in range(samples * (half - 2)):
        net_out[n] = net[:, n * LANES : (n + 1) * LANES]


def outer_kernel(
    dims,
    rows_in,
    own_mid,
    other_mid,
    first_weight,
    lat_in,
    mean_lines,
    edge_lat_in,
    edge_mean_in,
    hs_in,
    bias,
    out_weight,
    net_in,
    *rest,
):
    corners = rest[: dims["messages"]]
    net_out, zl, hs, ez, part = rest[dims["messages"] :]
    samples = rows_in.shape[0] // 2
    rows = 8
    lat_rows = lat_in.shape[2] - 4
    channels = lat_rows // 3
    half = rows // 2
    height = dims["row"] * rows
    row_place = lax.axis_index("row")
    col_place = lax.axis_index("col")
    lane = lane_index(CPAD)
    even = lane % 2 == 0

    def known(n, s, i, j):
        return hs_in[j, s * half + n + i - 2]

    lower = [functools.partial(known, n, s) for n in range(2) for s in range(samples)]
    early = section(own_mid, other_mid, (2,), lower)
    wide = samples * LANES
    later = early[:, wide:] + section(own_mid, other_mid, (1,), lower[samples:])
    early = jnp.concatenate([early[:, 0:wide], later], axis=1)
    part[...] = early

    valid = []
    for w in range(2):
        row = row_place * rows + tile_row(w, rows)
        valid.append((row >= 0) & (row < height))
    lines = {}
    for s in range(samples):
        for w in range(2):
            lines[s, w] = jnp.where(valid[w], rows_in[w * samples + s].astype(F32), 0.0)
    lane_w = (lane // 2) % rows
    lane_row = row_place * rows + tile_row(lane_w, rows)
    inside = (lane < 2 * samples * rows) & (lane_w < 2) & (lane_row >= 0) & (lane_row < height)

    def halo(corner, ok):
        return jnp.where(inside & ok, pltpu.roll(corner, LANES - 2 * (rows - 2), 1), 0.0)

    from_left = halo(corners[0][...], col_place > 0)
    from_right = halo(corners[-1][...], col_place < dims["col"] - 1)
    own = own_columns(lines, lane, rows)
    edge = edge_parts(from_left, from_right, own, even)
    for j in range(3):
        at = j * channels
        ez[at : at + channels, :] = edge[j][0:channels] + edge_lat_in[at : at + channels, :]
    ez[lat_rows : lat_rows + 4, :] = edge_lat_in[lat_rows : lat_rows + 4, :]
    for s in range(samples):
        for w in range(2):
            turned = pltpu.roll(edge[1], (LANES - 1 - 2 * (s * rows + w)) % LANES, 1)
            moved = shifted_lines(lines[s, w], turned, lane)
            for j in range(3):
                zl[s, w, j * channels : (j + 1) * channels, :] = moved[j][0:channels]
            zl[s, w, lat_rows : lat_rows + 4, :] = lat_in[s, 0, lat_rows : lat_rows + 4, :]

    weight = first_weight[...]
    edge_hidden = edge_first(weight, ez[...], edge_mean_in[...], dims)
    stacked = []
    for s in range(samples):
        lat = [zl[s, 0], zl[s, 1], lat_in[s, 0], lat_in[s, 1]]
        for w in range(2):
            stacked.append(stack_taps(lat[w : w + 3], [mean_lines[w + i] for i in range(3)]))
    value = jnp.dot(weight, jnp.concatenate(stacked, axis=1), preferred_element_type=F32)
    value = silu_of_half(value)
    lane_h = lane_index(value.shape[0])
    edge_row = ((lane_h // 2) % rows > 0) | valid[1]
    edge_hidden = jnp.where(edge_row, edge_hidden.astype(F32), 0.0).astype(BF16)
    hidden_lines = []
    for s in range(samples):
        for w in range(2):
            here = value[:, (2 * s + w) * LANES : (2 * s + w + 1) * LANES]
            if w == 0:
                here = jnp.where(valid[1], here, 0.0)
            hidden_lines.append((2 * s + w, 2 * (s * rows + w), here.astype(BF16)))
    store_hidden(hs, hidden_lines, edge_hidden, lane_h)

    def line(n, s, i, j):
        return hs[j, 2 * s + n + i]

    every = range(samples)
    upper = [functools.partial(line, n, s) for n in range(2) for s in every]
    value = part[...] + section(own_mid, other_mid, (0,), upper)
    first = value[:, 0:wide] + section(own_mid, other_mid, (1,), upper[0:samples])
    value = jnp.concatenate([first, value[:, wide:]], axis=1)
    net = project(value, bias[...], out_weight[...])
    rest_lines = half - 2
    for s in range(samples):
        for n in range(2):
            at = samples * n + s
            net_out[s * half + n] = net[:, at * LANES : (at + 1) * LANES]
        for n in range(rest_lines):
            net_out[s * half + 2 + n] = net_in[s * rest_lines + n]


def finish_kernel(latent, fresh, own_net, other_net, mean, coef, fine, following):
    samples = latent.shape[0]
    rows = mean.shape[0]
    channels = latent.shape[1] // rows
    half = rows // 2
    upper = lax.axis_index("chan") == 0
    for s in range(samples):
        keep, gain, noise, inverse = (coef[s, n : n + 1, :] for n in range(4))
        for y in range(rows):
            place = s * half + (y if y < half else rows - 1 - y)
            own, other = own_net[place], other_net[place]
            net = jnp.where(upper, own, other) if y < half else jnp.where(upper, other, own)
            denoised = keep * channel_rows(latent, s, y, channels, rows) + gain * net[0:channels]
            at = pl.ds(y, channels, stride=rows)
            line = jnp.where(upper, y, rows - 1 - y)
            fine[s, at, :] = mean[line, 0:channels, :] + denoised
            following[s, at, :] = denoised * inverse + noise * channel_rows(
                fresh, s, y, channels, rows
            )


def on_device(
    dims,
    latent,
    fresh_noise,
    step_index,
    coarse,
    weight_in,
    bias_in,
    weight_noise,
    weight_mid,
    bias_mid,
    weight_out,
):
    samples, channels, rows, cols = latent.shape
    taps, hidden, deep = weight_in.shape
    half = rows // 2
    row_count, col_count = dims["row"], dims["col"]
    messages = dims["messages"]
    vmem = pl.BlockSpec(memory_space=pltpu.VMEM)
    struct = jax.ShapeDtypeStruct
    place = functools.partial(pltpu.with_memory_space_constraint, memory_space=pltpu.VMEM)

    far = functools.partial(pltpu.with_memory_space_constraint, memory_space=pltpu.HBM)
    anywhere = pl.BlockSpec(memory_space=pltpu.HBM)

    flat = latent.reshape(samples, channels * rows, cols)
    swap = [(0, 1), (1, 0)]
    other_mid = lax.ppermute(weight_mid, "chan", swap)
    group = coarse.shape[2] + 2
    depth = CPAD * ((3 * group + CPAD - 1) // CPAD)
    packed = pl.pallas_call(
        functools.partial(pack_kernel, dims),
        out_shape=[
            pltpu.VMEM(flat.shape, F32),
            pltpu.VMEM(coarse.shape, F32),
            pltpu.VMEM((taps, deep, hidden), BF16),
            pltpu.VMEM((1, hidden), F32),
            pltpu.VMEM((1, hidden), F32),
            pltpu.VMEM((8, LANES), F32),
            pltpu.VMEM((depth, 6 * LANES), BF16),
            pltpu.VMEM(weight_mid.shape, BF16),
            pltpu.VMEM((2 * samples, CPAD, cols), BF16),
            pltpu.VMEM((CPAD, hidden // 2), F32),
        ]
        + [pltpu.VMEM((CPAD, LANES), F32)] * messages,
        in_specs=[anywhere] * 9,
        out_specs=[vmem] * (10 + messages),
        scratch_shapes=[
            pltpu.VMEM(weight_out.shape, BF16),
            pltpu.VMEM((1, hidden // 2), F32),
            pltpu.SMEM((samples,), jnp.int32),
            pltpu.SemaphoreType.DMA((8 + 2 * samples,)),
        ],
        compiler_params=LIMIT,
        name="pack",
    )(
        far(flat),
        far(coarse),
        far(weight_out),
        far(bias_mid.reshape(1, -1)),
        far(jnp.transpose(weight_in, (0, 2, 1))),
        far(bias_in.reshape(1, -1)),
        far(weight_noise.reshape(1, -1)),
        far(step_index),
        far(weight_mid),
    )
    prepared = [place(value) for value in packed[:8]]
    flat_near = prepared[0]
    rows_message, shared, side_messages = packed[8], packed[9], packed[10:]

    down = [(r, 0, r + 1, 0) for r in range(row_count - 1)]
    down += [(r + 1, 1, r, 1) for r in range(row_count - 1)]
    ends = [(row_count - 1, 0, row_count - 1, 1), (0, 1, 0, 0)]
    vertical = [(2 * a + b, 2 * c + d) for a, b, c, d in down + ends]
    sides, corners = [], []
    for n, message in enumerate(side_messages):
        if col_count > 2:
            step = 1 if n == 0 else -1
            columns = [(i, (i + step) % col_count) for i in range(col_count)]
        else:
            columns = [(i, col_count - 1 - i) for i in range(col_count)]
        sides.append(lax.ppermute(message, "col", columns))
        diagonal = [
            (2 * (a * col_count + i) + b, 2 * (c * col_count + k) + d)
            for a, b, c, d in down
            for i, k in columns
        ]
        diagonal += [
            (2 * (a * col_count + i) + b, 2 * (c * col_count + i) + d)
            for a, b, c, d in ends
            for i in range(col_count)
        ]
        corners.append(lax.ppermute(message, ("row", "col", "chan"), diagonal))
    rows_in = lax.ppermute(rows_message, ("row", "chan"), vertical)
    other_shared = lax.ppermute(shared, "chan", swap)

    other_mid = place(other_mid)
    lat_rows = 3 * channels + 4
    inner_lines = samples * (half - 2)
    inner = pl.pallas_call(
        functools.partial(inner_kernel, dims),
        out_shape=[
            pltpu.VMEM((hidden, 6 * lat_rows), BF16),
            pltpu.VMEM((samples, 2, lat_rows, cols), F32),
            pltpu.VMEM((4, lat_rows, cols), F32),
            pltpu.VMEM((lat_rows, cols), F32),
            pltpu.VMEM((lat_rows, cols), F32),
            pltpu.VMEM((3, samples * half, hidden, cols), BF16),
            pltpu.VMEM((hidden, 1), F32),
            pltpu.VMEM((CPAD, hidden), BF16),
            pltpu.VMEM((inner_lines, CPAD, cols), F32),
            pltpu.VMEM((rows, CPAD, cols), F32),
            pltpu.VMEM((samples, 8, cols), F32),
        ],
        in_specs=[vmem] * (11 + messages),
        out_specs=[vmem] * 11,
        scratch_shapes=[
            pltpu.VMEM((samples, rows - 2, lat_rows, cols), F32),
            pltpu.VMEM((rows, lat_rows, cols), F32),
            pltpu.VMEM((6 * lat_rows, hidden), F32),
            pltpu.VMEM((coarse.shape[1] * CPAD, LANES), F32),
            pltpu.VMEM((LANES, 2 * LANES), F32),
            pltpu.VMEM((2, lat_rows, cols), F32),
        ],
        compiler_params=LIMIT,
        name="inner",
    )(
        *prepared,
        other_mid,
        place(shared),
        place(other_shared),
        *[place(side) for side in sides],
    )
    inner = [place(value) for value in inner]
    net = pl.pallas_call(
        functools.partial(outer_kernel, dims),
        out_shape=pltpu.VMEM((samples * half, CPAD, cols), F32),
        in_specs=[vmem] * (12 + messages),
        out_specs=vmem,
        scratch_shapes=[
            pltpu.VMEM((samples, 2, lat_rows, cols), F32),
            pltpu.VMEM((3, 2 * samples, hidden, cols), BF16),
            pltpu.VMEM((lat_rows, cols), F32),
            pltpu.VMEM((hidden, 2 * samples * cols), F32),
        ],
        compiler_params=LIMIT,
        name="outer",
    )(
        place(rows_in),
        prepared[7],
        other_mid,
        *inner[:9],
        *[place(corner) for corner in corners],
    )
    other_net = lax.ppermute(net, "chan", swap)
    results = pl.pallas_call(
        finish_kernel,
        out_shape=[struct(flat.shape, F32)] * 2,
        in_specs=[vmem] * 6,
        out_specs=[vmem] * 2,
        compiler_params=LIMIT,
        name="finish",
    )(
        flat_near,
        place(fresh_noise.reshape(flat.shape)),
        place(net),
        place(other_net),
        inner[9],
        inner[10],
    )
    return tuple(value.reshape(latent.shape) for value in results)


def solution(mesh):
    dims = {axis: mesh.shape[axis] for axis in ("row", "col", "chan")}
    dims["messages"] = 2 if dims["col"] > 2 else 1
    tile = P("ens", None, "row", "col")
    in_specs = (
        tile,
        tile,
        P("ens"),
        P("ens", None, "col"),
        P(),
        P(),
        P(),
        P(None, "chan", None),
        P("chan"),
        P(None, "chan"),
    )

    def body(*args):
        return on_device(dims, *args)

    return jax.shard_map(
        body, mesh=mesh, in_specs=in_specs, out_specs=(tile, tile), check_vma=False
    )
```

```python
import functools

import jax
import jax.numpy as jnp
from jax import lax
from jax.experimental import pallas as pl
from jax.experimental.pallas import tpu as pltpu
from jax.sharding import PartitionSpec as P


STEPS = 18
FACTOR = 8

sigma_data = 0.5
sigma_high = 80.0
sigma_low = 0.002
rho_power = 7.0

F32 = jnp.float32
BF16 = jnp.bfloat16
LANES = 128
CPAD = 16
ORDER = (1, 0, 2)
LIMIT = pltpu.CompilerParams(vmem_limit_bytes=12 * 1024 * 1024)


def lane_index(rows):
    return lax.broadcasted_iota(jnp.int32, (rows, LANES), 1)


def tile_row(w, rows):
    return jnp.where(lax.axis_index("chan") == 0, w - 2, rows + 1 - w)


def tap_row(i):
    return jnp.where(lax.axis_index("chan") == 0, i, 2 - i)


def noise_level(position):
    top_root = sigma_high ** (1.0 / rho_power)
    bottom_root = sigma_low ** (1.0 / rho_power)
    root = top_root + position * (1.0 / (STEPS - 1)) * (bottom_root - top_root)
    square = root * root
    return square * square * square * root


def silu_of_half(half):
    return half + half * jnp.tanh(half)


def three_terms(value):
    high = value.astype(BF16).astype(F32)
    rest = value - high
    mid = rest.astype(BF16).astype(F32)
    return high, mid, (rest - mid).astype(BF16).astype(F32)


def channel_rows(ref, s, y, channels, rows):
    return ref[s, pl.ds(y, channels, stride=rows), :]


def pack_kernel(
    dims,
    latent_far,
    coarse_far,
    weight_out_far,
    bias_mid_far,
    weight_in_far,
    bias_in_far,
    weight_noise_far,
    steps_far,
    weight_mid_far,
    latent,
    coarse,
    weight_in,
    bias_in,
    weight_noise,
    steps_out,
    cols_matrix,
    own_mid,
    rows_out,
    shared_out,
    *rest,
):
    sides = rest[: dims["messages"]]
    weight_out, bias_mid, steps, sem = rest[dims["messages"] :]
    samples = latent.shape[0]
    middle = latent.shape[1] // 2
    pairs = [
        (latent_far.at[s, pl.ds(p * middle, middle)], latent.at[s, pl.ds(p * middle, middle)])
        for s in range(samples)
        for p in range(2)
    ]
    first = len(pairs)
    pairs += [
        (coarse_far, coarse),
        (weight_out_far, weight_out),
        (bias_mid_far, bias_mid),
        (steps_far, steps),
        (weight_in_far, weight_in),
        (bias_in_far, bias_in),
        (weight_noise_far, weight_noise),
    ]
    copies = [pltpu.make_async_copy(a, b, sem.at[n]) for n, (a, b) in enumerate(pairs)]
    big = pltpu.make_async_copy(weight_mid_far, own_mid, sem.at[len(pairs)])
    for copy in copies[:first] + [big] + copies[first:]:
        copy.start()
    copies.append(big)
    channels, coarse_rows, local_cols = coarse.shape
    rows = latent.shape[1] // channels
    count = dims["col"]
    col_place = lax.axis_index("col")
    upper = lax.axis_index("chan") == 0

    cols = latent.shape[2]
    width = count * cols
    coarse_cols = count * local_cols
    group = local_cols + 2
    depth = lax.broadcasted_iota(jnp.int32, (cols_matrix.shape[0], LANES), 0)
    spot = depth % group
    index = col_place * local_cols + jnp.where(
        spot < local_cols, spot, jnp.where(spot == local_cols, -1, local_cols)
    )
    index = jnp.where(depth < 3 * group, index, -2).astype(F32)
    wide = lax.broadcasted_iota(jnp.int32, (1, LANES), 1)
    targets = [col_place * cols + wide - 1 + j for j in range(3)]
    targets += [
        col_place * cols + jnp.where(wide % 2 == 0, j - 2, cols - 1 + j) for j in range(3)
    ]
    for n, target in enumerate(targets):
        low, high, fraction = blend(target.astype(F32), coarse_cols)
        outside = (target < 0) | (target >= width)
        low = jnp.where(outside, -3.0, low)
        high = jnp.where(outside, -3.0, high)
        weights = jnp.where(low == index, 1.0 - fraction, 0.0)
        weights += jnp.where(high == index, fraction, 0.0)
        cols_matrix[:, n * LANES : (n + 1) * LANES] = weights.astype(BF16)

    for copy in copies[:first]:
        copy.wait()
    for near in range(2):
        y = jnp.where(upper, rows - 2 + near, 1 - near)
        for s in range(samples):
            got = channel_rows(latent, s, y, channels, rows).astype(BF16)
            rows_out[near * samples + s, 0:channels, :] = got
            rows_out[near * samples + s, channels:CPAD, :] = jnp.zeros(
                (CPAD - channels, LANES), BF16
            )
    lane = lane_index(channels)
    sums = [jnp.zeros((channels, LANES), F32) for _ in sides]
    if count > 2:
        shifts = (2, 0)
    else:
        shifts = (jnp.where(col_place == 0, 2, 0),)
    for s in range(samples):
        for q in range(rows):
            y = jnp.where(upper, q, rows - 1 - q)
            row = channel_rows(latent, s, y, channels, rows)
            place = 2 * (s * rows + q)
            hit = (lane == place) | (lane == place + 1)
            sums = [
                jnp.where(hit, pltpu.roll(row, place + shift, 1), total)
                for shift, total in zip(shifts, sums)
            ]
    for copy in copies[first : first + 4]:
        copy.wait()
    base = 2 * samples * rows
    for h in range(coarse_rows):
        line = coarse[:, h, :]
        right = jnp.broadcast_to(line[:, local_cols - 1 : local_cols], (channels, LANES))
        left = jnp.broadcast_to(line[:, 0:1], (channels, LANES))
        if count > 2:
            values = (right, left)
        else:
            values = (jnp.where(col_place == 0, right, left),)
        sums = [jnp.where(lane == base + h, v, t) for v, t in zip(values, sums)]
    for out, total in zip(sides, sums):
        out[0:channels, :] = total
        out[channels:CPAD, :] = jnp.zeros((CPAD - channels, LANES), F32)
    shared_out[0:channels, :] = weight_out[...].astype(F32)
    shared_out[channels : channels + 1, :] = bias_mid[...]
    shared_out[channels + 1 : CPAD, :] = jnp.zeros((CPAD - channels - 1, LANES), F32)
    for s in range(samples):
        steps_out[s : s + 1, :] = jnp.ones((1, LANES), F32) * steps[s].astype(F32)
    for copy in copies[first + 4 :]:
        copy.wait()


def blend(target, size):
    twice = 2.0 * target + (1.0 - FACTOR)
    lower = jnp.floor(twice * (1.0 / (2 * FACTOR)))
    fraction = (twice - lower * (2.0 * FACTOR)) * (1.0 / (2 * FACTOR))
    fraction = jnp.where(lower < 0.0, 0.0, fraction)
    return jnp.clip(lower, 0.0, size - 1.0), jnp.clip(lower + 1.0, 0.0, size - 1.0), fraction


def edge_parts(from_left, from_right, own, even):
    return (
        jnp.where(even, from_left, own),
        jnp.where(even, pltpu.roll(from_left, LANES - 1, 1), pltpu.roll(from_right, 1, 1)),
        jnp.where(even, own, from_right),
    )


def own_columns(lines, lane, rows):
    own = jnp.zeros(lane.shape, F32)
    for (s, w), line in lines.items():
        at = 2 * (s * rows + w)
        first = line if at == 0 else pltpu.roll(line, at, 1)
        own = jnp.where(lane == at, first, own)
        own = jnp.where(lane == at + 1, pltpu.roll(line, (at + 2) % LANES, 1), own)
    return own


def shifted_lines(line, turned, lane):
    return (
        pltpu.roll(jnp.where(lane == LANES - 1, turned, line), 1, 1),
        line,
        pltpu.roll(jnp.where(lane == 0, turned, line), LANES - 1, 1),
    )


def stack_taps(lat, mean):
    parts = sum([[lat[i], mean[i]] for i in range(3)], [])
    return jnp.concatenate(parts, axis=0).astype(BF16)


def edge_first(weight, lat, mean, dims):
    col_place = lax.axis_index("col")
    stacked = stack_taps(
        [pltpu.roll(lat, LANES - 2 * i, 1) if i else lat for i in range(3)],
        [pltpu.roll(mean, LANES - 2 * i, 1) if i else mean for i in range(3)],
    )
    hidden = silu_of_half(jnp.dot(weight, stacked, preferred_element_type=F32))
    lane = lane_index(hidden.shape[0])
    side = col_place + lane % 2
    return jnp.where((side > 0) & (side < dims["col"]), hidden, 0.0).astype(BF16)


def store_hidden(hs, lines, edge, lane):
    for at, turn, here in lines:
        hs[1, at] = here
    for at, turn, here in lines:
        turned = pltpu.roll(edge, (LANES - 1 - turn) % LANES, 1)
        hs[0, at] = pltpu.roll(jnp.where(lane == LANES - 1, turned, here), 1, 1)
        hs[2, at] = pltpu.roll(jnp.where(lane == 0, turned, here), LANES - 1, 1)


def tap_weight(own_mid, other_mid, tap_rows):
    taps = [(tap_row(i), j) for j in ORDER for i in tap_rows]
    return jnp.concatenate(
        [
            jnp.concatenate([ref[3 * i + j] for i, j in taps], axis=1)
            for ref in (own_mid, other_mid)
        ],
        axis=0,
    )


def section(own_mid, other_mid, tap_rows, lines):
    stacked = jnp.concatenate(
        [
            jnp.concatenate([line(i, j) for line in lines], axis=1)
            for j in ORDER
            for i in tap_rows
        ],
        axis=0,
    )
    weight = tap_weight(own_mid, other_mid, tap_rows)
    return jnp.dot(weight, stacked, preferred_element_type=F32)


def project(value, bias, out_weight):
    middle = silu_of_half(0.5 * value + bias).astype(BF16)
    return jnp.dot(out_weight, middle, preferred_element_type=F32)


def inner_kernel(
    dims,
    latent,
    coarse,
    weight_in,
    bias_in,
    weight_noise,
    steps,
    cols_matrix,
    own_mid,
    other_mid,
    own_shared,
    other_shared,
    *rest,
):
    sides = rest[: dims["messages"]]
    (
        w1_out,
        lat_out,
        mean_lines,
        edge_lat_out,
        edge_mean_out,
        hs,
        bias_out,
        weight_out,
        net_out,
        mean_out,
        coef_out,
        zl,
        zm,
        w1t,
        ce,
        tr,
        ez,
    ) = rest[dims["messages"] :]
    samples = latent.shape[0]
    channels, coarse_rows, local_cols = coarse.shape
    rows = latent.shape[1] // channels
    _, deep, hidden = weight_in.shape
    half = rows // 2
    lat_rows = 3 * channels
    block = 2 * (lat_rows + 4)
    height = dims["row"] * rows
    row_place = lax.axis_index("row")
    col_place = lax.axis_index("col")
    lane = lane_index(CPAD)
    even = lane % 2 == 0

    tr[...] = jnp.zeros(tr.shape, F32)
    tr[0:CPAD, 0:LANES] = own_shared[...]
    tr[0:CPAD, LANES:] = other_shared[...]
    bias = 0.5 * tr[...].T[:, channels : channels + 1]
    bias_out[...] = bias
    out_weight = tr[0:CPAD, :].astype(BF16)
    weight_out[...] = out_weight

    w1t[...] = jnp.zeros(w1t.shape, F32)
    bias_terms = three_terms(0.5 * bias_in[...])
    noise_terms = three_terms(0.5 * weight_noise[...])
    for i in range(3):
        for j in range(3):
            tap = 0.5 * weight_in[3 * tap_row(i) + j].astype(F32)
            at = i * block + j * channels
            w1t[at : at + channels, :] = tap[0:channels]
            at += lat_rows + 4
            w1t[at : at + channels, :] = tap[channels:deep]
        at = i * block + lat_rows
        w1t[at : at + 1, :] = bias_terms[i]
        for j in range(3 - i):
            w1t[at + 1 + j : at + 2 + j, :] = noise_terms[i]
    first_weight = w1t[...].T.astype(BF16)
    w1_out[...] = first_weight

    lane_w = (lane // 2) % rows
    used = lane < 2 * samples * rows
    inside = used & (lane_w >= 2)

    def halo(side, ok):
        return jnp.where(inside & ok, pltpu.roll(side, 4, 1), 0.0)

    from_left = halo(sides[0][...], col_place > 0)
    from_right = halo(sides[-1][...], col_place < dims["col"] - 1)
    pad = jnp.zeros((CPAD - channels, LANES), F32)
    lines = {}
    for s in range(samples):
        for w in range(2, rows):
            line = channel_rows(latent, s, tile_row(w, rows), channels, rows)
            lines[s, w] = jnp.concatenate([line, pad], axis=0)
    own = own_columns(lines, lane, rows)
    edge = edge_parts(from_left, from_right, own, even)

    ce[...] = jnp.zeros(ce.shape, F32)
    base = 2 * samples * rows
    for h in range(coarse_rows):
        at = h * CPAD
        ce[at : at + channels, 0:local_cols] = coarse[:, h, :]
        ce[at : at + CPAD, local_cols : local_cols + 1] = sides[0][:, base + h : base + h + 1]
        ce[at : at + CPAD, local_cols + 1 : local_cols + 2] = sides[-1][:, base + h : base + h + 1]
    blended = []
    for w in range(rows + 2):
        row = row_place * rows + tile_row(w, rows)
        first, following, fraction = blend(jnp.full((1, LANES), row.astype(F32)), coarse_rows)
        total = None
        for h in range(coarse_rows):
            weight = jnp.where(first == h, 1.0 - fraction, 0.0)
            weight += jnp.where(following == h, fraction, 0.0)
            if w < 2:
                weight = jnp.where((row >= 0) & (row < height), weight, 0.0)
            term = weight * ce[h * CPAD : (h + 1) * CPAD, :]
            total = term if total is None else total + term
        blended.append(total)
    group = local_cols + 2
    high, mid, low = three_terms(jnp.concatenate(blended, axis=0))
    cells = (high + pltpu.roll(mid, group, 1) + pltpu.roll(low, 2 * group, 1)).astype(BF16)
    cells = cells[:, 0 : cols_matrix.shape[0]]
    spread = jnp.dot(cells, cols_matrix[...], preferred_element_type=F32)

    def mean_line(w, j):
        return spread[w * CPAD : (w + 1) * CPAD, j * LANES : (j + 1) * LANES]

    zero_rows = jnp.zeros((4, LANES), F32)
    for w in range(rows + 2):
        if w >= 2:
            mean_out[w - 2] = mean_line(w, 1)
        if w < rows:
            for j in range(3):
                zm[w, j * channels : (j + 1) * channels, :] = mean_line(w, j)[0:channels]
            zm[w, lat_rows : lat_rows + 4, :] = zero_rows
    for j in range(3):
        at = j * channels
        total = jnp.zeros((CPAD, LANES), F32)
        for w in range(rows):
            total = jnp.where(used & (lane_w == w), mean_line(w, 3 + j), total)
        ez[1, at : at + channels, :] = total[0:channels]
        ez[0, at : at + channels, :] = edge[j][0:channels]
    ez[1, lat_rows : lat_rows + 4, :] = zero_rows

    ones = jnp.ones((1, LANES), F32)
    tails = []
    for s in range(samples):
        step = steps[s : s + 1, :]
        now = noise_level(step)
        ahead = noise_level(step + 1.0)
        tails.append(jnp.concatenate([ones, *three_terms(jnp.log(now) * 0.25)], axis=0))
        variance = now * now + sigma_data * sigma_data
        scale = jnp.sqrt(variance)
        inverse = 1.0 / jnp.sqrt(ahead * ahead + sigma_data * sigma_data)
        coef_out[s] = jnp.concatenate(
            [
                sigma_data * sigma_data / variance * scale,
                sigma_data * now / scale,
                ahead * inverse,
                inverse,
                jnp.zeros((4, LANES), F32),
            ],
            axis=0,
        )
    sample_of = lane_index(4) // (2 * rows)
    edge_tail = tails[0]
    for s in range(1, samples):
        edge_tail = jnp.where(sample_of == s, tails[s], edge_tail)
    ez[0, lat_rows : lat_rows + 4, :] = edge_tail

    for s in range(samples):
        for w in range(2, rows):
            turned = pltpu.roll(edge[1], (LANES - 1 - 2 * (s * rows + w)) % LANES, 1)
            moved = shifted_lines(lines[s, w], turned, lane)
            for j in range(3):
                zl[s, w - 2, j * channels : (j + 1) * channels, :] = moved[j][0:channels]
            zl[s, w - 2, lat_rows : lat_rows + 4, :] = tails[s]
    for s in range(samples):
        for w in range(2):
            lat_out[s, w] = zl[s, w]
    for w in range(4):
        mean_lines[w] = zm[w]
    edge_lat, edge_mean = ez[0], ez[1]
    edge_lat_out[...] = edge_lat
    edge_mean_out[...] = edge_mean

    edge_hidden = edge_first(first_weight, edge_lat, edge_mean, dims)
    lane_h = lane_index(hidden)
    hidden_lines = []
    for s in range(samples):
        stacked = jnp.concatenate(
            [
                stack_taps([zl[s, w - 2 + i] for i in range(3)], [zm[w + i] for i in range(3)])
                for w in range(2, half + 2)
            ],
            axis=1,
        )
        value = silu_of_half(jnp.dot(first_weight, stacked, preferred_element_type=F32))
        value = value.astype(BF16)
        for n in range(half):
            here = value[:, n * LANES : (n + 1) * LANES]
            hidden_lines.append((s * half + n, 2 * (s * rows + n + 2), here))
    store_hidden(hs, hidden_lines, edge_hidden, lane_h)

    lines = [
        functools.partial(lambda s, n, i, j: hs[j, s * half + n + i], s, n)
        for s in range(samples)
        for n in range(half - 2)
    ]
    net = project(section(own_mid, other_mid, range(3), lines), bias, out_weight)
    for n in range(samples * (half - 2)):
        net_out[n] = net[:, n * LANES : (n + 1) * LANES]


def outer_kernel(
    dims,
    rows_in,
    own_mid,
    other_mid,
    first_weight,
    lat_in,
    mean_lines,
    edge_lat_in,
    edge_mean_in,
    hs_in,
    bias,
    out_weight,
    net_in,
    *rest,
):
    corners = rest[: dims["messages"]]
    net_out, zl, hs, ez, part = rest[dims["messages"] :]
    samples = rows_in.shape[0] // 2
    rows = 8
    lat_rows = lat_in.shape[2] - 4
    channels = lat_rows // 3
    half = rows // 2
    height = dims["row"] * rows
    row_place = lax.axis_index("row")
    col_place = lax.axis_index("col")
    lane = lane_index(CPAD)
    even = lane % 2 == 0

    def known(n, s, i, j):
        return hs_in[j, s * half + n + i - 2]

    lower = [functools.partial(known, n, s) for n in range(2) for s in range(samples)]
    early = section(own_mid, other_mid, (2,), lower)
    wide = samples * LANES
    later = early[:, wide:] + section(own_mid, other_mid, (1,), lower[samples:])
    early = jnp.concatenate([early[:, 0:wide], later], axis=1)
    part[...] = early

    valid = []
    for w in range(2):
        row = row_place * rows + tile_row(w, rows)
        valid.append((row >= 0) & (row < height))
    lines = {}
    for s in range(samples):
        for w in range(2):
            lines[s, w] = jnp.where(valid[w], rows_in[w * samples + s].astype(F32), 0.0)
    lane_w = (lane // 2) % rows
    lane_row = row_place * rows + tile_row(lane_w, rows)
    inside = (lane < 2 * samples * rows) & (lane_w < 2) & (lane_row >= 0) & (lane_row < height)

    def halo(corner, ok):
        return jnp.where(inside & ok, pltpu.roll(corner, LANES - 2 * (rows - 2), 1), 0.0)

    from_left = halo(corners[0][...], col_place > 0)
    from_right = halo(corners[-1][...], col_place < dims["col"] - 1)
    own = own_columns(lines, lane, rows)
    edge = edge_parts(from_left, from_right, own, even)
    for j in range(3):
        at = j * channels
        ez[at : at + channels, :] = edge[j][0:channels] + edge_lat_in[at : at + channels, :]
    ez[lat_rows : lat_rows + 4, :] = edge_lat_in[lat_rows : lat_rows + 4, :]
    for s in range(samples):
        for w in range(2):
            turned = pltpu.roll(edge[1], (LANES - 1 - 2 * (s * rows + w)) % LANES, 1)
            moved = shifted_lines(lines[s, w], turned, lane)
            for j in range(3):
                zl[s, w, j * channels : (j + 1) * channels, :] = moved[j][0:channels]
            zl[s, w, lat_rows : lat_rows + 4, :] = lat_in[s, 0, lat_rows : lat_rows + 4, :]

    weight = first_weight[...]
    edge_hidden = edge_first(weight, ez[...], edge_mean_in[...], dims)
    stacked = []
    for s in range(samples):
        lat = [zl[s, 0], zl[s, 1], lat_in[s, 0], lat_in[s, 1]]
        for w in range(2):
            stacked.append(stack_taps(lat[w : w + 3], [mean_lines[w + i] for i in range(3)]))
    value = jnp.dot(weight, jnp.concatenate(stacked, axis=1), preferred_element_type=F32)
    value = silu_of_half(value)
    lane_h = lane_index(value.shape[0])
    edge_row = ((lane_h // 2) % rows > 0) | valid[1]
    edge_hidden = jnp.where(edge_row, edge_hidden.astype(F32), 0.0).astype(BF16)
    hidden_lines = []
    for s in range(samples):
        for w in range(2):
            here = value[:, (2 * s + w) * LANES : (2 * s + w + 1) * LANES]
            if w == 0:
                here = jnp.where(valid[1], here, 0.0)
            hidden_lines.append((2 * s + w, 2 * (s * rows + w), here.astype(BF16)))
    store_hidden(hs, hidden_lines, edge_hidden, lane_h)

    def line(n, s, i, j):
        return hs[j, 2 * s + n + i]

    every = range(samples)
    upper = [functools.partial(line, n, s) for n in range(2) for s in every]
    value = part[...] + section(own_mid, other_mid, (0,), upper)
    first = value[:, 0:wide] + section(own_mid, other_mid, (1,), upper[0:samples])
    value = jnp.concatenate([first, value[:, wide:]], axis=1)
    net = project(value, bias[...], out_weight[...])
    rest_lines = half - 2
    for s in range(samples):
        for n in range(2):
            at = samples * n + s
            net_out[s * half + n] = net[:, at * LANES : (at + 1) * LANES]
        for n in range(rest_lines):
            net_out[s * half + 2 + n] = net_in[s * rest_lines + n]


def finish_kernel(latent, fresh, own_net, other_net, mean, coef, fine, following):
    samples = latent.shape[0]
    rows = mean.shape[0]
    channels = latent.shape[1] // rows
    half = rows // 2
    upper = lax.axis_index("chan") == 0
    for s in range(samples):
        keep, gain, noise, inverse = (coef[s, n : n + 1, :] for n in range(4))
        for y in range(rows):
            place = s * half + (y if y < half else rows - 1 - y)
            own, other = own_net[place], other_net[place]
            net = jnp.where(upper, own, other) if y < half else jnp.where(upper, other, own)
            denoised = keep * channel_rows(latent, s, y, channels, rows) + gain * net[0:channels]
            at = pl.ds(y, channels, stride=rows)
            line = jnp.where(upper, y, rows - 1 - y)
            fine[s, at, :] = mean[line, 0:channels, :] + denoised
            following[s, at, :] = denoised * inverse + noise * channel_rows(
                fresh, s, y, channels, rows
            )


def on_device(
    dims,
    latent,
    fresh_noise,
    step_index,
    coarse,
    weight_in,
    bias_in,
    weight_noise,
    weight_mid,
    bias_mid,
    weight_out,
):
    samples, channels, rows, cols = latent.shape
    taps, hidden, deep = weight_in.shape
    half = rows // 2
    row_count, col_count = dims["row"], dims["col"]
    messages = dims["messages"]
    vmem = pl.BlockSpec(memory_space=pltpu.VMEM)
    struct = jax.ShapeDtypeStruct
    place = functools.partial(pltpu.with_memory_space_constraint, memory_space=pltpu.VMEM)

    far = functools.partial(pltpu.with_memory_space_constraint, memory_space=pltpu.HBM)
    anywhere = pl.BlockSpec(memory_space=pltpu.HBM)

    flat = latent.reshape(samples, channels * rows, cols)
    swap = [(0, 1), (1, 0)]
    other_mid = lax.ppermute(weight_mid, "chan", swap)
    group = coarse.shape[2] + 2
    depth = CPAD * ((3 * group + CPAD - 1) // CPAD)
    packed = pl.pallas_call(
        functools.partial(pack_kernel, dims),
        out_shape=[
            pltpu.VMEM(flat.shape, F32),
            pltpu.VMEM(coarse.shape, F32),
            pltpu.VMEM((taps, deep, hidden), BF16),
            pltpu.VMEM((1, hidden), F32),
            pltpu.VMEM((1, hidden), F32),
            pltpu.VMEM((8, LANES), F32),
            pltpu.VMEM((depth, 6 * LANES), BF16),
            pltpu.VMEM(weight_mid.shape, BF16),
            pltpu.VMEM((2 * samples, CPAD, cols), BF16),
            pltpu.VMEM((CPAD, hidden // 2), F32),
        ]
        + [pltpu.VMEM((CPAD, LANES), F32)] * messages,
        in_specs=[anywhere] * 9,
        out_specs=[vmem] * (10 + messages),
        scratch_shapes=[
            pltpu.VMEM(weight_out.shape, BF16),
            pltpu.VMEM((1, hidden // 2), F32),
            pltpu.SMEM((samples,), jnp.int32),
            pltpu.SemaphoreType.DMA((8 + 2 * samples,)),
        ],
        compiler_params=LIMIT,
        name="pack",
    )(
        far(flat),
        far(coarse),
        far(weight_out),
        far(bias_mid.reshape(1, -1)),
        far(jnp.transpose(weight_in, (0, 2, 1))),
        far(bias_in.reshape(1, -1)),
        far(weight_noise.reshape(1, -1)),
        far(step_index),
        far(weight_mid),
    )
    prepared = [place(value) for value in packed[:8]]
    flat_near = prepared[0]
    rows_message, shared, side_messages = packed[8], packed[9], packed[10:]

    down = [(r, 0, r + 1, 0) for r in range(row_count - 1)]
    down += [(r + 1, 1, r, 1) for r in range(row_count - 1)]
    ends = [(row_count - 1, 0, row_count - 1, 1), (0, 1, 0, 0)]
    vertical = [(2 * a + b, 2 * c + d) for a, b, c, d in down + ends]
    sides, corners = [], []
    for n, message in enumerate(side_messages):
        if col_count > 2:
            step = 1 if n == 0 else -1
            columns = [(i, (i + step) % col_count) for i in range(col_count)]
        else:
            columns = [(i, col_count - 1 - i) for i in range(col_count)]
        sides.append(lax.ppermute(message, "col", columns))
        diagonal = [
            (2 * (a * col_count + i) + b, 2 * (c * col_count + k) + d)
            for a, b, c, d in down
            for i, k in columns
        ]
        diagonal += [
            (2 * (a * col_count + i) + b, 2 * (c * col_count + i) + d)
            for a, b, c, d in ends
            for i in range(col_count)
        ]
        corners.append(lax.ppermute(message, ("row", "col", "chan"), diagonal))
    rows_in = lax.ppermute(rows_message, ("row", "chan"), vertical)
    other_shared = lax.ppermute(shared, "chan", swap)

    other_mid = place(other_mid)
    lat_rows = 3 * channels + 4
    inner_lines = samples * (half - 2)
    inner = pl.pallas_call(
        functools.partial(inner_kernel, dims),
        out_shape=[
            pltpu.VMEM((hidden, 6 * lat_rows), BF16),
            pltpu.VMEM((samples, 2, lat_rows, cols), F32),
            pltpu.VMEM((4, lat_rows, cols), F32),
            pltpu.VMEM((lat_rows, cols), F32),
            pltpu.VMEM((lat_rows, cols), F32),
            pltpu.VMEM((3, samples * half, hidden, cols), BF16),
            pltpu.VMEM((hidden, 1), F32),
            pltpu.VMEM((CPAD, hidden), BF16),
            pltpu.VMEM((inner_lines, CPAD, cols), F32),
            pltpu.VMEM((rows, CPAD, cols), F32),
            pltpu.VMEM((samples, 8, cols), F32),
        ],
        in_specs=[vmem] * (11 + messages),
        out_specs=[vmem] * 11,
        scratch_shapes=[
            pltpu.VMEM((samples, rows - 2, lat_rows, cols), F32),
            pltpu.VMEM((rows, lat_rows, cols), F32),
            pltpu.VMEM((6 * lat_rows, hidden), F32),
            pltpu.VMEM((coarse.shape[1] * CPAD, LANES), F32),
            pltpu.VMEM((LANES, 2 * LANES), F32),
            pltpu.VMEM((2, lat_rows, cols), F32),
        ],
        compiler_params=LIMIT,
        name="inner",
    )(
        *prepared,
        other_mid,
        place(shared),
        place(other_shared),
        *[place(side) for side in sides],
    )
    inner = [place(value) for value in inner]
    net = pl.pallas_call(
        functools.partial(outer_kernel, dims),
        out_shape=pltpu.VMEM((samples * half, CPAD, cols), F32),
        in_specs=[vmem] * (12 + messages),
        out_specs=vmem,
        scratch_shapes=[
            pltpu.VMEM((samples, 2, lat_rows, cols), F32),
            pltpu.VMEM((3, 2 * samples, hidden, cols), BF16),
            pltpu.VMEM((lat_rows, cols), F32),
            pltpu.VMEM((hidden, 2 * samples * cols), F32),
        ],
        compiler_params=LIMIT,
        name="outer",
    )(
        place(rows_in),
        prepared[7],
        other_mid,
        *inner[:9],
        *[place(corner) for corner in corners],
    )
    other_net = lax.ppermute(net, "chan", swap)
    results = pl.pallas_call(
        finish_kernel,
        out_shape=[struct(flat.shape, F32)] * 2,
        in_specs=[vmem] * 6,
        out_specs=[vmem] * 2,
        compiler_params=LIMIT,
        name="finish",
    )(
        flat_near,
        place(fresh_noise.reshape(flat.shape)),
        place(net),
        place(other_net),
        inner[9],
        inner[10],
    )
    return tuple(value.reshape(latent.shape) for value in results)


def solution(mesh):
    dims = {axis: mesh.shape[axis] for axis in ("row", "col", "chan")}
    dims["messages"] = 2 if dims["col"] > 2 else 1
    tile = P("ens", None, "row", "col")
    in_specs = (
        tile,
        tile,
        P("ens"),
        P("ens", None, "col"),
        P(),
        P(),
        P(),
        P(None, "chan", None),
        P("chan"),
        P(None, "chan"),
    )

    def body(*args):
        return on_device(dims, *args)

    return jax.shard_map(
        body, mesh=mesh, in_specs=in_specs, out_specs=(tile, tile), check_vma=False
    )
```
